32 devices in a mesh: groups: 2 (over y), hist: 4 (over z), head: 2 (over x), rep: 2 (over core).
Axes of the slice: x: 2, y: 2, z: 4, core: 2. Of those that a mesh axis runs over, the one named last changes fastest.
Arguments:
- item_feats: bfloat16 [4096, 4096], P(('groups', 'hist', 'rep')), parts along dimension 0, may hold values from -6 to 6
- adapter: bfloat16 [4096, 512], P('hist', 'head'), may hold values from -0.09375 to 0.09375
- hist_emb: bfloat16 [8192, 512], P(('groups', 'hist')), parts along dimension 0, may hold values from -6 to 6
- key_weight: bfloat16 [512, 512], P(None, 'head'), may hold values from -0.25 to 0.25
- value_weight: bfloat16 [512, 512], P(None, 'head'), may hold values from -0.25 to 0.25
- routes: int32 [4096, 1], P(('groups', 'hist', 'rep')), parts along dimension 0, may hold values from 0 to 3; in each aligned block of 256 rows (0 to 255, 256 to 511, ...) at most 128 rows name the same one
- cand_index: int32 [1024], P(('groups', 'hist', 'rep')), parts along dimension 0, may hold values from 0 to 255
- item_user: int32 [4096], P(('groups', 'hist', 'rep')), parts along dimension 0, may hold values from 0 to 255
- hist_user: int32 [8192], P(('groups', 'hist')), parts along dimension 0, may hold values from 0 to 255
Outputs:
- scored: bfloat16 [1024, 512], P(('groups', 'hist', 'rep'), 'head'), parts along dimension 0
The draws below stay inside these ranges and needn't reach their ends.
There are 2 independent parts, one for each index of `groups`. The reference program is written for one: setup_inputs(seed, part) draws one part's arguments, and reference() takes and returns one part's arrays. A program takes and returns all parts, laid end to end along the dimension named above; an argument that names none is the same for every part. Nothing has to cross between parts.
Inputs may be any that keep to these rules, and one draw needn't show every extreme that they name: `routes`: in the rows of one device no owner is named more than 128 times; some owner is named exactly 128 times.
All inputs are finite; a program needn't handle non-finite values.
Results may differ from the reference program's by a relative error of at most 0.0081.
Values may be sent and summed in bfloat16 or wider, within the bound.
No kernel may reach another device: no remote copies, remote signals or barrier semaphores. Data moves between devices by JAX's collectives and lax.ppermute only.
A program may use at most 64 MiB of HBM per device.

```python
import math
import jax
import jax.numpy as jnp
import numpy as np
from jax import lax

DIN = 4096
D = 512
HEADS = 8
HS = 64
USERS = 256
ITEM_DEV = 256
HIST_DEV = 1024
CAND_DEV = 64
CAP = 128
ITEMS = 2048
HIST = 4096
CANDS = 512
N_HIST = 4
N_REP = 2


def touch_ends(drawn, key, smallest, largest):
    dims = drawn.shape
    place = [jax.random.randint(jax.random.fold_in(key, axis), (), 0, dims[axis]) for axis in range(len(dims))]
    drawn = drawn.at[tuple(place)].set(smallest)
    longest = dims.index(max(dims))
    place[longest] = (place[longest] + 1) % dims[longest]
    return drawn.at[tuple(place)].set(largest)


def block_scale(stream_key, shape, split, least, largest):
    def one(axis_at, blocks):
        steps = jax.random.uniform(jax.random.fold_in(jax.random.fold_in(stream_key, 6), axis_at), (blocks,), jnp.float32, least / len(split), largest / len(split))
        return jnp.repeat(jnp.exp(steps), shape[axis_at] // blocks).reshape((-1,) + (1,) * (len(shape) - axis_at - 1))

    factor_of = one(*split[0])
    for cut in split[1:]:
        factor_of = factor_of * one(*cut)
    return factor_of


def deal_out(stream_key, own, number, rows, amount, top, bound, lean):
    ranking = jax.random.permutation(stream_key, amount)
    crowded, usual = shares(amount, rows * top, bound, lean, True), shares(amount, rows * top, bound, lean, False)
    places = jnp.arange(amount)

    def named(lengths, rotation):
        used = int((lengths > 0).sum())
        fixed = max(1, used // 4)
        shifted = fixed + (places - fixed + rotation * (used - fixed)) % max(1, amount - fixed)
        return jnp.zeros((amount,), jnp.int32).at[ranking[jnp.where(places < fixed, places, shifted)]].set(jnp.asarray(lengths, jnp.int32))

    lengths = jnp.where(number % 4 == 0, named(crowded, number // 4), named(usual, number - number // 4 - 1))
    mixed = jax.random.permutation(jax.random.fold_in(own, 3), amount)
    giver, receiver = mixed[0:amount // 2 * 2:2], mixed[1:amount // 2 * 2:2]
    margin = jnp.minimum(lengths[giver] - 1, bound - lengths[receiver]) // 2
    margin = jnp.where((giver == ranking[0]) | (receiver == ranking[0]) | (lengths[receiver] == 0), 0, jnp.maximum(margin, 0))
    shifted = jax.random.randint(jax.random.fold_in(own, 4), (amount // 2,), 0, 1 << 20) % (margin + 1)
    lengths = lengths.at[giver].add(-shifted).at[receiver].add(shifted)
    items = jnp.searchsorted(jnp.cumsum(lengths), jnp.arange(rows * top), side="right").astype(jnp.int32)
    grid = items.reshape(top, rows).T
    grid = grid[jax.random.permutation(jax.random.fold_in(own, 1), rows)]
    rotation = jax.random.randint(jax.random.fold_in(own, 2), (rows, 1), 0, top)
    return jnp.take_along_axis(grid, (jnp.arange(top)[None, :] + rotation) % top, axis=1)


def shares(amount, total, limit, lean, full):
    portions = [(1 << 20) // math.isqrt(grade ** lean) + 1 for grade in range(1, amount + 1)]
    largest = limit if full else min(limit, max(-(-total // amount), total * portions[0] // sum(portions)))
    least = 1 if total - largest >= amount - 1 else 0
    counts, surplus = [largest] + [least] * (amount - 1), total - largest - least * (amount - 1)
    while surplus > 0:
        candidates = [i for i in range(1, amount) if counts[i] < largest] or [i for i in range(1, amount) if counts[i] < limit]
        whole, budget = sum([portions[i] for i in candidates]), surplus
        for i in candidates:
            more = min(limit - counts[i], max(1, budget * portions[i] // whole), surplus)
            counts[i] = counts[i] + more
            surplus = surplus - more
    return np.array(counts)


def centred(key, dims, scale, bound, pieces=(), kind=jnp.bfloat16):
    values = scale * jax.random.normal(key, dims, jnp.float32)
    if pieces:
        values = values * block_scale(key, dims, pieces, -0.22, 0.18)
    return jnp.clip(values, -bound, bound).astype(kind)


def setup_inputs(seed: int = 0, part: int = 0) -> dict:
    key_list = jax.random.split(jax.random.key(seed), 10)
    part_splits = jax.random.split(jax.random.fold_in(key_list[9], part), 10)
    item_feats = centred(part_splits[0], (ITEMS, DIN), 1.0, 6.0, ((0, 8),))
    adapter = centred(key_list[1], (DIN, D), DIN ** -0.5, 0.09375, ((0, 4), (1, 2)))
    hist_emb = centred(part_splits[2], (HIST, D), 1.0, 6.0, ((0, 4),))
    key_weight = centred(key_list[3], (D, D), D ** -0.5, 0.25, ((1, 2),))
    value_weight = centred(key_list[4], (D, D), D ** -0.5, 0.25, ((1, 2),))
    routes_keys = jax.random.split(jax.random.fold_in(part_splits[5], 1), ITEMS // ITEM_DEV)
    routes_turns = jax.random.permutation(jax.random.fold_in(part_splits[5], 3), ITEMS // ITEM_DEV)
    routes = jax.vmap(lambda own, number: deal_out(jax.random.fold_in(part_splits[5], 2), own, number, ITEM_DEV, N_HIST, 1, CAP, 2))(routes_keys, routes_turns).reshape((ITEMS, 1))
    cand_index = touch_ends(jax.random.randint(part_splits[6], (CANDS,), 0, ITEM_DEV), jax.random.fold_in(part_splits[6], 1), 0, ITEM_DEV - 1).astype(jnp.int32)
    item_user = touch_ends(jax.random.randint(part_splits[7], (ITEMS,), 0, USERS), jax.random.fold_in(part_splits[7], 1), 0, USERS - 1).astype(jnp.int32)
    hist_user = touch_ends(jax.random.randint(part_splits[8], (HIST,), 0, USERS), jax.random.fold_in(part_splits[8], 1), 0, USERS - 1).astype(jnp.int32)
    return {"item_feats": item_feats, "adapter": adapter, "hist_emb": hist_emb, "key_weight": key_weight, "value_weight": value_weight, "routes": routes, "cand_index": cand_index, "item_user": item_user, "hist_user": hist_user}


def reference(item_feats, adapter, hist_emb, key_weight, value_weight, routes, cand_index, item_user, hist_user):
    embedded = jnp.dot(item_feats, adapter, preferred_element_type=jnp.float32).astype(jnp.bfloat16)
    cand_rows = ((jnp.arange(CANDS, dtype=jnp.int32) // CAND_DEV) * ITEM_DEV + cand_index.astype(jnp.int32)).astype(jnp.int32)
    queries = embedded[cand_rows]
    cand_user = item_user.astype(jnp.int32)[cand_rows]
    key_rows = jnp.dot(hist_emb, key_weight, preferred_element_type=jnp.float32).astype(jnp.bfloat16)
    value_rows = jnp.dot(hist_emb, value_weight, preferred_element_type=jnp.float32).astype(jnp.bfloat16)
    owner_of = routes[:, 0].astype(jnp.int32)
    owner_hot = (owner_of.reshape(ITEMS // ITEM_DEV, ITEM_DEV)[:, :, None] == jnp.arange(N_HIST, dtype=jnp.int32)[None, None, :]).astype(jnp.int32)
    earlier = jnp.cumsum(owner_hot, axis=1) - owner_hot
    slot_of = jnp.sum(earlier * owner_hot, axis=2).reshape(ITEMS).astype(jnp.int32)
    source = jnp.arange(ITEMS, dtype=jnp.int32) // ITEM_DEV
    position = (source * CAP + slot_of).astype(jnp.int32)
    slot_total = N_HIST * N_REP * CAP
    routed = jnp.zeros((N_HIST, slot_total, D), jnp.bfloat16).at[owner_of, position].set(embedded)
    routed_user = jnp.full((N_HIST, slot_total), -1, jnp.int32).at[owner_of, position].set(item_user.astype(jnp.int32))
    set_keys = jnp.concatenate([key_rows.reshape(N_HIST, HIST_DEV, D), routed], axis=1)
    set_values = jnp.concatenate([value_rows.reshape(N_HIST, HIST_DEV, D), routed], axis=1)
    set_users = jnp.concatenate([hist_user.astype(jnp.int32).reshape(N_HIST, HIST_DEV), routed_user], axis=1)
    att_scale = float(HS) ** -0.5
    highest = lax.Precision.HIGHEST
    cand_block = math.gcd(CANDS, 512)

    def per_block(operands):
        query_block, user_block = operands
        matching = user_block[:, None, None] == set_users[None]
        counted = jnp.sum(matching.astype(jnp.float32), axis=2)
        inverse = 1.0 / jnp.maximum(counted, 1.0)

        def per_head(head_index):
            offset = (head_index * HS).astype(jnp.int32)
            query_head = lax.dynamic_slice_in_dim(query_block, offset, HS, 1).astype(jnp.float32)
            key_head = lax.dynamic_slice_in_dim(set_keys, offset, HS, 2).astype(jnp.float32)
            value_head = lax.dynamic_slice_in_dim(set_values, offset, HS, 2).astype(jnp.float32)
            scores = jnp.einsum('cd,okd->cok', query_head, key_head, precision=highest) * att_scale
            weights = lax.optimization_barrier(jax.nn.silu(scores).astype(jnp.bfloat16)).astype(jnp.float32)
            weights = jnp.where(matching, weights, 0.0)
            summed = jnp.einsum('cok,okd->cod', weights, value_head, precision=highest)
            return jnp.sum(summed * inverse[:, :, None], axis=1)

        per_heads = lax.map(per_head, jnp.arange(HEADS, dtype=jnp.int32))
        return jnp.transpose(per_heads, (1, 0, 2)).reshape(-1, D)

    blocks = lax.map(per_block, (queries.reshape(-1, cand_block, D), cand_user.reshape(-1, cand_block)))
    attended = blocks.reshape(CANDS, D)
    gating = jax.nn.silu(queries.astype(jnp.float32))
    return (gating * attended).astype(jnp.bfloat16)
```

```python
import functools
import math

import jax
import jax.numpy as jnp
from jax import lax
from jax.experimental import pallas as pl
from jax.experimental.pallas import tpu as pltpu
from jax.sharding import PartitionSpec as P

HS = 64
USERS = 256
VM = pl.BlockSpec(memory_space=pltpu.VMEM)
HBM = pl.BlockSpec(memory_space=pl.ANY)
F32 = jnp.float32
BF16 = jnp.bfloat16


def attend(query_block, user_block, key_rows, value_rows, key_users):
    row_count = query_block.shape[0]
    col_count = query_block.shape[1]
    heads_here = col_count // HS
    att_scale = float(HS) ** (-0.5)
    query_three = query_block.reshape(row_count, heads_here, HS)
    key_three = key_rows.reshape(-1, heads_here, HS)
    value_three = value_rows.reshape(-1, heads_here, HS)
    scores = (
        jnp.einsum("rhd,khd->hrk", query_three, key_three, preferred_element_type=jnp.float32)
        * att_scale
    )
    matching = user_block[:, None] == key_users[None, :]
    weights = jnp.where(matching[None], jax.nn.silu(scores), 0.0).astype(jnp.bfloat16)
    mixture = jnp.einsum("hrk,khd->rhd", weights, value_three, preferred_element_type=jnp.float32)
    counted = jnp.sum(matching.astype(jnp.float32), axis=1)
    inverse = 1.0 / jnp.maximum(counted, 1.0)
    return mixture.reshape(row_count, col_count) * inverse[:, None]


def dense_partial(queries, users, key_rows, value_rows, key_users):
    total_rows = queries.shape[0]
    col_count = queries.shape[1]
    block_size = math.gcd(total_rows, 512)
    blocked_queries = queries.reshape(total_rows // block_size, block_size, col_count)
    blocked_users = users.reshape(total_rows // block_size, block_size)

    def one_block(operands):
        return attend(operands[0], operands[1], key_rows, value_rows, key_users)

    return lax.map(one_block, (blocked_queries, blocked_users)).reshape(total_rows, col_count)


def generic_body(
    item_feats,
    adapter,
    hist_emb,
    key_weight,
    value_weight,
    routes,
    cand_index,
    item_user,
    hist_user,
):
    owners = lax.axis_size("hist")
    item_count = item_feats.shape[0]
    col_count = adapter.shape[1]
    embedded = jnp.dot(
        item_feats,
        lax.all_gather(adapter, "hist", axis=0, tiled=True),
        preferred_element_type=jnp.float32,
    ).astype(jnp.bfloat16)
    capacity = 2 * item_count // owners
    owner_of = routes[:, 0]
    owner_hot = (owner_of[:, None] == jnp.arange(owners, dtype=jnp.int32)[None, :]).astype(
        jnp.int32
    )
    earlier = jnp.cumsum(owner_hot, axis=0) - owner_hot
    slot_of = jnp.sum(earlier * owner_hot, axis=1)
    position = owner_of * capacity + slot_of
    placing = (jnp.arange(owners * capacity, dtype=jnp.int32)[:, None] == position[None, :]).astype(
        jnp.bfloat16
    )
    outgoing = jnp.dot(placing, embedded, preferred_element_type=jnp.float32).astype(jnp.bfloat16)
    outgoing = outgoing.reshape(owners, capacity, col_count)
    shifted_user = (item_user + 1).astype(jnp.bfloat16)
    outgoing_user = (
        jnp.dot(placing, shifted_user, preferred_element_type=jnp.float32) - 1.0
    ).astype(jnp.bfloat16)
    outgoing_user = outgoing_user.reshape(owners, capacity)
    incoming, incoming_user = (
        lax.all_to_all(outgoing, "hist", split_axis=0, concat_axis=0, tiled=True),
        lax.all_to_all(outgoing_user, "hist", split_axis=0, concat_axis=0, tiled=True),
    )
    routed, routed_user = (
        lax.all_gather(incoming, "rep", axis=0, tiled=True),
        lax.all_gather(incoming_user, "rep", axis=0, tiled=True),
    )
    routed = routed.reshape(-1, col_count)
    routed_user = routed_user.reshape(-1)
    key_local = jnp.dot(hist_emb, key_weight, preferred_element_type=jnp.float32).astype(
        jnp.bfloat16
    )
    value_local = jnp.dot(hist_emb, value_weight, preferred_element_type=jnp.float32).astype(
        jnp.bfloat16
    )
    key_rows = jnp.concatenate([key_local, routed], axis=0)
    value_rows = jnp.concatenate([value_local, routed], axis=0)
    key_users = jnp.concatenate([hist_user.astype(jnp.bfloat16), routed_user], axis=0)
    own_queries = embedded[cand_index]
    own_users = item_user[cand_index].astype(jnp.bfloat16)
    gathered, gathered_users = (
        lax.all_gather(own_queries, "hist", axis=0, tiled=True),
        lax.all_gather(own_users, "hist", axis=0, tiled=True),
    )
    partial_value = dense_partial(gathered, gathered_users, key_rows, value_rows, key_users)
    attended = lax.psum_scatter(partial_value, "hist", scatter_dimension=0, tiled=True)
    gating = jax.nn.silu(own_queries.astype(jnp.float32))
    return (gating * attended).astype(jnp.bfloat16)


def call(kernel, outs, args, flops=0, bytes_accessed=1 << 18, vmem=16, specs=None, scratch=(), name=None):
    return pl.pallas_call(
        kernel,
        out_shape=outs,
        in_specs=specs or [VM] * len(args),
        out_specs=jax.tree.map(lambda _: VM, outs),
        scratch_shapes=scratch,
        compiler_params=pltpu.CompilerParams(vmem_limit_bytes=vmem << 20),
        cost_estimate=pl.CostEstimate(flops=flops, bytes_accessed=bytes_accessed, transcendentals=0),
        name=name,
    )(*args)


def shape(dims, dtype):
    return jax.ShapeDtypeStruct(dims, dtype)


def iota(dims, axis):
    return lax.broadcasted_iota(jnp.int32, dims, axis)


def dot(a, b, contract=((1,), (0,))):
    return lax.dot_general(a, b, (contract, ((), ())), preferred_element_type=F32)


def col_start(width):
    return pl.multiple_of(lax.axis_index("rep") * width, width)


def share_kernel(adapter, out, sem):
    rows, cols = out.shape
    row = pl.multiple_of(lax.axis_index("groups") * rows, rows)
    copy = pltpu.make_async_copy(adapter.at[pl.ds(row, rows), pl.ds(col_start(cols), cols)], out, sem)
    copy.start()
    copy.wait()


def users_kernel(mine, other, hist_user, pay, hot, pick):
    items = (mine.shape[1] - pick.shape[0]) // 2
    owners = pay.shape[0] - 8
    both_user = jnp.concatenate([mine[:, :items], other[:, :items]], axis=1)
    both_owner = jnp.concatenate([mine[:, items : 2 * items], other[:, items : 2 * items]], axis=1)
    lanes = pick.shape[0]
    half = lanes // 2
    lane = iota((1, lanes), 1)
    cand = jnp.where(
        lane < half,
        mine[:, 2 * items :],
        pltpu.roll(jnp.broadcast_to(other[:, 2 * items :], (8, lanes)), half, 1)[:1] + items,
    )
    events = hist_user.shape[1]
    here = lax.axis_index("hist")
    item_hot = (iota((USERS, 2 * items), 0) == both_user).astype(F32).astype(BF16)
    event_hot = (iota((USERS, events), 0) == hist_user[...]).astype(F32).astype(BF16)
    hot[:, :events] = event_hot
    hot[:, events:] = item_hot
    rows = pay.shape[0]
    owns_item = (iota((rows, 2 * items), 0) == both_owner).astype(F32).astype(BF16)
    owns_event = (iota((rows, events), 0) == here).astype(F32).astype(BF16)
    counts = dot(owns_item, item_hot, ((1,), (1,))) + dot(owns_event, event_hot, ((1,), (1,)))
    chosen = (iota((2 * items, lanes), 0) == cand).astype(F32)
    users = dot(jnp.broadcast_to(both_user, (8, 2 * items)).astype(F32).astype(BF16), chosen.astype(BF16))
    padded = jnp.concatenate([users, jnp.zeros((8, USERS - lanes), F32)], axis=1)
    pay[...] = counts
    pay[owners:, :] = padded
    pick[...] = jnp.transpose(chosen).astype(BF16)


def scale_kernel(n, mine, other, hist_user, hot, *refs):
    pays, out = refs[:n], refs[n]
    rows = pays[0].shape[0]
    owners = rows - 8
    lanes = out.shape[1]
    items = (mine.shape[1] - lanes) // 2
    events = hist_user.shape[1]
    total = pays[0][...]
    for pay in pays[1:]:
        total = total + pay[...]
    high = jnp.floor(total * (1.0 / 256.0))
    low = total - 256.0 * high
    counts = 256.0 * dot(high.astype(BF16), hot[...]) + dot(low.astype(BF16), hot[...])
    both_owner = jnp.concatenate([mine[:, items : 2 * items], other[:, items : 2 * items]], axis=1)
    here = jnp.zeros((1, events), jnp.int32) + lax.axis_index("hist")
    owner = jnp.concatenate([here, both_owner], axis=1)
    count = jnp.sum(jnp.where(iota(counts.shape, 0) == owner, counts, 0.0), axis=0, keepdims=True)
    inverse = 1.0 / jnp.maximum(count, 1.0)
    user = jnp.concatenate([hist_user[...], mine[:, :items], other[:, :items]], axis=1).astype(F32)
    diagonal = iota((lanes, lanes), 0) == iota((lanes, lanes), 1)
    for k in range(n):
        row = pays[k][owners : owners + 1, :lanes]
        column = jnp.sum(jnp.where(diagonal, row, 0.0), axis=1, keepdims=True)
        out[k] = jnp.where(column == user, inverse, 0.0)


def project_kernel(hist_emb, key_weight, value_weight, key_t, value):
    width = value.shape[1]
    columns = pl.ds(col_start(width), width)
    keys = dot(hist_emb[...], key_weight[:, columns])
    value[...] = dot(hist_emb[...], value_weight[:, columns]).astype(BF16)
    key_t[...] = jnp.transpose(keys.astype(BF16))


def embed_own_kernel(mine, other, adapter, total):
    items = mine.shape[0]
    depth = adapter.shape[0]
    width = total.shape[1]
    at = pl.ds(pl.multiple_of(lax.axis_index("hist") * depth, depth), depth)
    block = adapter[:, pl.ds(col_start(width), width)]
    total[:items] = dot(mine[:, at], block)
    total[items:] = dot(other[:, at], block)


def add_blocks(n, k, mine, other, base, blocks):
    depth = blocks[0].shape[0]
    groups = len(blocks)
    source = lax.rem(lax.axis_index("hist") + n - k, n)
    top, bottom = base
    for step, block in enumerate(blocks):
        group = lax.rem(lax.axis_index("groups") + groups - step, groups)
        at = pl.ds(pl.multiple_of((source * groups + group) * depth, depth), depth)
        top = top + dot(mine[:, at], block[...])
        bottom = bottom + dot(other[:, at], block[...])
    return top, bottom


def embed_add_kernel(n, k, groups, mine, other, total, *refs):
    items = mine.shape[0]
    top, bottom = add_blocks(n, k, mine, other, (total[:items], total[items:]), refs[:groups])
    refs[groups][:items] = top
    refs[groups][items:] = bottom


def embed_last_kernel(n, k, groups, mine, other, pick, total, *refs):
    items = mine.shape[0]
    top, bottom = add_blocks(n, k, mine, other, (total[:items], total[items:]), refs[:groups])
    rows, rows_t, query = refs[groups:]
    rows[:items] = top.astype(BF16)
    rows[items:] = bottom.astype(BF16)
    query[...] = dot(pick[...], rows[...]).astype(BF16)
    rows_t[...] = jnp.transpose(rows[...])


def attend_kernel(k, query, key_t, value, rows_t, rows, scale, out):
    cands, width = query.shape
    heads = width // HS
    lane = iota((cands, width), 1) // HS
    part = query[...] * (0.5 * HS ** -0.5)
    zero = jnp.zeros_like(part)
    split = jnp.concatenate([jnp.where(lane == h, part, zero) for h in range(heads)], axis=0)
    events = key_t.shape[1]

    def weigh(keys, factor):
        half = dot(split, keys)
        gated = half + half * jnp.tanh(half)
        return (gated * jnp.concatenate([factor] * heads, axis=0)).astype(BF16)

    mixed = dot(weigh(key_t[...], scale[k, :, :events]), value[...])
    mixed = mixed + dot(weigh(rows_t[...], scale[k, :, events:]), rows[...])
    total = jnp.zeros((cands, width), F32)
    for h in range(heads):
        total = total + jnp.where(lane == h, mixed[h * cands : (h + 1) * cands], 0.0)
    out[...] = total.astype(out.dtype)


def gate_kernel(query, own, *refs):
    parts, keep, send = refs[:-2], refs[-2], refs[-1]
    total = own[...]
    for part in parts:
        total = total + part[...].astype(F32)
    gate = query[...].astype(F32)
    scored = (gate * jax.nn.sigmoid(gate) * total).astype(BF16)
    half = keep.shape[0]
    keep[...] = scored[:half]
    send[...] = scored[half:]


def join_kernel(keep, got, out):
    width = keep.shape[1]
    first = lax.axis_index("rep") == 0
    out[:, :width] = jnp.where(first, keep[...], got[...])
    out[:, width:] = jnp.where(first, got[...], keep[...])


def shift(value, axis, k):
    count = lax.axis_size(axis)
    return lax.ppermute(value, axis, [(i, (i + k) % count) for i in range(count)])


def fast_body(
    item_feats, adapter, hist_emb, key_weight, value_weight, routes, cand_index, item_user, hist_user
):
    n, groups = lax.axis_size("hist"), lax.axis_size("groups")
    items, din = item_feats.shape
    depth, cols = adapter.shape
    width = cols // 2
    cands = 2 * cand_index.shape[0]
    events, dim = hist_emb.shape
    order = list(range(1, n))

    own_share = call(
        share_kernel,
        shape((depth // groups, width), BF16),
        (adapter,),
        specs=[HBM],
        scratch=[pltpu.SemaphoreType.DMA],
        name="share",
    )
    along = {k: shift(own_share, "hist", k) for k in order}
    feats_other = shift(item_feats, "rep", 1)
    mine = jnp.concatenate([item_user, routes[:, 0], cand_index, cand_index]).reshape(1, -1)
    other = shift(mine, "rep", 1)
    hist_row = hist_user.reshape(1, -1)
    keys = events + 2 * items
    pay, hot, pick = call(
        users_kernel,
        (
            shape((8 + 8 * ((n + 7) // 8), USERS), F32),
            shape((USERS, keys), BF16),
            shape((cands, 2 * items), BF16),
        ),
        (mine, other, hist_row),
        name="users",
    )
    pays = [pay] + [shift(pay, "hist", k) for k in order]
    key_t, value = call(
        project_kernel,
        (shape((width, events), BF16), shape((events, width), BF16)),
        (hist_emb, key_weight, value_weight),
        flops=4 * events * dim * width,
        bytes_accessed=4 << 20,
        name="project",
    )
    total = call(
        embed_own_kernel,
        shape((2 * items, width), F32),
        (item_feats, feats_other, adapter),
        flops=4 * items * depth * width,
        bytes_accessed=4 << 20,
        name="embed_own",
    )
    scale = call(
        functools.partial(scale_kernel, n),
        shape((n, cands, keys), F32),
        (mine, other, hist_row, hot, *pays),
        bytes_accessed=4 << 20,
        name="scale",
    )
    across = {k: [along[k]] + [shift(along[k], "groups", g) for g in range(1, groups)] for k in order}
    for k in order[:-1]:
        total = call(
            functools.partial(embed_add_kernel, n, k, groups),
            shape((2 * items, width), F32),
            (item_feats, feats_other, total, *across[k]),
            flops=4 * items * depth * width,
            bytes_accessed=2 << 20,
            name="embed_add",
        )
    k = order[-1]
    rows, rows_t, query = call(
        functools.partial(embed_last_kernel, n, k, groups),
        (shape((2 * items, width), BF16), shape((width, 2 * items), BF16), shape((cands, width), BF16)),
        (item_feats, feats_other, pick, total, *across[k]),
        flops=4 * items * depth * width,
        bytes_accessed=2 << 20,
        name="embed_last",
    )
    queries = {k: shift(query, "hist", k) for k in order}

    def attend(k, block, dtype):
        return call(
            functools.partial(attend_kernel, k),
            shape((cands, width), dtype),
            (block, key_t, value, rows_t, rows, scale),
            flops=8 * cands * keys * width,
            bytes_accessed=1 << 20,
            name="attend",
        )

    own = attend(0, query, F32)
    parts = [shift(attend(k, queries[k], BF16), "hist", n - k) for k in order]
    keep, send = call(
        gate_kernel,
        (shape((cands // 2, width), BF16), shape((cands // 2, width), BF16)),
        (query, own, *parts),
        name="gate",
    )
    got = shift(send, "rep", 1)
    return call(join_kernel, shape((cands // 2, cols), BF16), (keep, got), name="join")


def body(*args):
    item_feats, adapter, cand_index = args[0], args[1], args[6]
    fits = (
        lax.axis_size("rep") == 2
        and lax.axis_size("hist") > 1
        and adapter.shape[0] % (128 * lax.axis_size("groups")) == 0
        and adapter.shape[1] % 256 == 0
        and 2 * cand_index.shape[0] == 128
        and item_feats.shape[0] % 128 == 0
    )
    return fast_body(*args) if fits else generic_body(*args)


def solution(mesh):
    placed = (
        P(("groups", "hist", "rep"), None),
        P("hist", "head"),
        P(("groups", "hist"), None),
        P(None, "head"),
        P(None, "head"),
        P(("groups", "hist", "rep"), None),
        P(("groups", "hist", "rep")),
        P(("groups", "hist", "rep")),
        P(("groups", "hist")),
    )
    return jax.shard_map(
        body,
        mesh=mesh,
        in_specs=placed,
        out_specs=P(("groups", "hist", "rep"), "head"),
        check_vma=False,
    )
```

```python
import functools
import math

import jax
import jax.numpy as jnp
from jax import lax
from jax.experimental import pallas as pl
from jax.experimental.pallas import tpu as pltpu
from jax.sharding import PartitionSpec as P


HS = 64
USERS = 256
VM = pl.BlockSpec(memory_space=pltpu.VMEM)
HBM = pl.BlockSpec(memory_space=pltpu.HBM)
F32 = jnp.float32
BF16 = jnp.bfloat16


def attend(query_block, user_block, key_rows, value_rows, key_users):
    row_count = query_block.shape[0]
    col_count = query_block.shape[1]
    heads_here = col_count // HS
    att_scale = float(HS) ** (-0.5)
    query_three = query_block.reshape(row_count, heads_here, HS)
    key_three = key_rows.reshape(-1, heads_here, HS)
    value_three = value_rows.reshape(-1, heads_here, HS)
    scores = (
        jnp.einsum("rhd,khd->hrk", query_three, key_three, preferred_element_type=jnp.float32)
        * att_scale
    )
    matching = user_block[:, None] == key_users[None, :]
    weights = jnp.where(matching[None], jax.nn.silu(scores), 0.0).astype(jnp.bfloat16)
    mixture = jnp.einsum("hrk,khd->rhd", weights, value_three, preferred_element_type=jnp.float32)
    counted = jnp.sum(matching.astype(jnp.float32), axis=1)
    inverse = 1.0 / jnp.maximum(counted, 1.0)
    return mixture.reshape(row_count, col_count) * inverse[:, None]


def dense_partial(queries, users, key_rows, value_rows, key_users):
    total_rows = queries.shape[0]
    col_count = queries.shape[1]
    block_size = math.gcd(total_rows, 512)
    blocked_queries = queries.reshape(total_rows // block_size, block_size, col_count)
    blocked_users = users.reshape(total_rows // block_size, block_size)

    def one_block(operands):
        return attend(operands[0], operands[1], key_rows, value_rows, key_users)

    return lax.map(one_block, (blocked_queries, blocked_users)).reshape(total_rows, col_count)


def generic_body(
    item_feats,
    adapter,
    hist_emb,
    key_weight,
    value_weight,
    routes,
    cand_index,
    item_user,
    hist_user,
):
    owners = lax.axis_size("hist")
    item_count = item_feats.shape[0]
    col_count = adapter.shape[1]
    embedded = jnp.dot(
        item_feats,
        lax.all_gather(adapter, "hist", axis=0, tiled=True),
        preferred_element_type=jnp.float32,
    ).astype(jnp.bfloat16)
    capacity = 2 * item_count // owners
    owner_of = routes[:, 0]
    owner_hot = (owner_of[:, None] == jnp.arange(owners, dtype=jnp.int32)[None, :]).astype(
        jnp.int32
    )
    earlier = jnp.cumsum(owner_hot, axis=0) - owner_hot
    slot_of = jnp.sum(earlier * owner_hot, axis=1)
    position = owner_of * capacity + slot_of
    placing = (jnp.arange(owners * capacity, dtype=jnp.int32)[:, None] == position[None, :]).astype(
        jnp.bfloat16
    )
    outgoing = jnp.dot(placing, embedded, preferred_element_type=jnp.float32).astype(jnp.bfloat16)
    outgoing = outgoing.reshape(owners, capacity, col_count)
    shifted_user = (item_user + 1).astype(jnp.bfloat16)
    outgoing_user = (
        jnp.dot(placing, shifted_user, preferred_element_type=jnp.float32) - 1.0
    ).astype(jnp.bfloat16)
    outgoing_user = outgoing_user.reshape(owners, capacity)
    incoming, incoming_user = (
        lax.all_to_all(outgoing, "hist", split_axis=0, concat_axis=0, tiled=True),
        lax.all_to_all(outgoing_user, "hist", split_axis=0, concat_axis=0, tiled=True),
    )
    routed, routed_user = (
        lax.all_gather(incoming, "rep", axis=0, tiled=True),
        lax.all_gather(incoming_user, "rep", axis=0, tiled=True),
    )
    routed = routed.reshape(-1, col_count)
    routed_user = routed_user.reshape(-1)
    key_local = jnp.dot(hist_emb, key_weight, preferred_element_type=jnp.float32).astype(
        jnp.bfloat16
    )
    value_local = jnp.dot(hist_emb, value_weight, preferred_element_type=jnp.float32).astype(
        jnp.bfloat16
    )
    key_rows = jnp.concatenate([key_local, routed], axis=0)
    value_rows = jnp.concatenate([value_local, routed], axis=0)
    key_users = jnp.concatenate([hist_user.astype(jnp.bfloat16), routed_user], axis=0)
    own_queries = embedded[cand_index]
    own_users = item_user[cand_index].astype(jnp.bfloat16)
    gathered, gathered_users = (
        lax.all_gather(own_queries, "hist", axis=0, tiled=True),
        lax.all_gather(own_users, "hist", axis=0, tiled=True),
    )
    partial_value = dense_partial(gathered, gathered_users, key_rows, value_rows, key_users)
    attended = lax.psum_scatter(partial_value, "hist", scatter_dimension=0, tiled=True)
    gating = jax.nn.silu(own_queries.astype(jnp.float32))
    return (gating * attended).astype(jnp.bfloat16)


def call(kernel, outs, args, flops=0, bytes_accessed=1 << 18, vmem=16, specs=None, scratch=()):
    return pl.pallas_call(
        kernel,
        out_shape=outs,
        in_specs=specs or [VM] * len(args),
        out_specs=jax.tree.map(lambda _: VM, outs),
        scratch_shapes=scratch,
        compiler_params=pltpu.CompilerParams(vmem_limit_bytes=vmem << 20),
        cost_estimate=pl.CostEstimate(flops=flops, bytes_accessed=bytes_accessed, transcendentals=0),
    )(*args)


def shape(dims, dtype):
    return jax.ShapeDtypeStruct(dims, dtype)


def iota(dims, axis):
    return lax.broadcasted_iota(jnp.int32, dims, axis)


def dot(a, b, contract=((1,), (0,))):
    return lax.dot_general(a, b, (contract, ((), ())), preferred_element_type=F32)


def col_start(width):
    return pl.multiple_of(lax.axis_index("rep") * width, width)


def share_kernel(adapter, block, out, sems):
    rows, cols = out.shape
    row = pl.multiple_of(lax.axis_index("groups") * rows, rows)
    columns = pl.ds(col_start(cols), cols)
    copies = [
        pltpu.make_async_copy(adapter.at[pl.ds(row, rows), columns], out, sems.at[0]),
        pltpu.make_async_copy(adapter.at[:, columns], block, sems.at[1]),
    ]
    for copy in copies:
        copy.start()
    for copy in copies:
        copy.wait()


def users_kernel(mine, other, pay, hot, pick):
    items = pick.shape[1] // 2
    owners = pay.shape[0] - 8
    both_user = jnp.concatenate([mine[:, :items], other[:, :items]], axis=1)
    both_owner = jnp.concatenate([mine[:, items : 2 * items], other[:, items : 2 * items]], axis=1)
    lanes = pick.shape[0]
    half = lanes // 2
    lane = iota((1, lanes), 1)
    cand = jnp.where(
        lane < half,
        mine[:, 2 * items : 2 * items + lanes],
        pltpu.roll(jnp.broadcast_to(other[:, 2 * items : 2 * items + lanes], (8, lanes)), half, 1)[:1] + items,
    )
    hist_user = mine[:, 2 * items + lanes :]
    events = hist_user.shape[1]
    here = lax.axis_index("hist")
    item_hot = (iota((USERS, 2 * items), 0) == both_user).astype(F32).astype(BF16)
    event_hot = (iota((USERS, events), 0) == hist_user).astype(F32).astype(BF16)
    hot[:, :events] = event_hot
    hot[:, events:] = item_hot
    rows = pay.shape[0]
    owns_item = (iota((rows, 2 * items), 0) == both_owner).astype(F32).astype(BF16)
    owns_event = (iota((rows, events), 0) == here).astype(F32).astype(BF16)
    counts = dot(owns_item, item_hot, ((1,), (1,))) + dot(owns_event, event_hot, ((1,), (1,)))
    chosen = (iota((2 * items, lanes), 0) == cand).astype(F32)
    users = dot(jnp.broadcast_to(both_user, (8, 2 * items)).astype(F32).astype(BF16), chosen.astype(BF16))
    padded = jnp.concatenate([users, jnp.zeros((8, USERS - lanes), F32)], axis=1)
    pay[...] = counts
    pay[owners:, :] = padded
    pick[...] = jnp.transpose(chosen).astype(BF16)


def scale_kernel(n, items, mine, other, hot, *refs):
    pays, out = refs[:n], refs[n]
    rows = pays[0].shape[0]
    owners = rows - 8
    lanes = out.shape[1]
    hist_user = mine[:, 2 * items + lanes :]
    events = hist_user.shape[1]
    total = pays[0][...]
    for pay in pays[1:]:
        total = total + pay[...]
    high = jnp.floor(total * (1.0 / 256.0))
    low = total - 256.0 * high
    counts = 256.0 * dot(high.astype(BF16), hot[...]) + dot(low.astype(BF16), hot[...])
    both_owner = jnp.concatenate([mine[:, items : 2 * items], other[:, items : 2 * items]], axis=1)
    here = jnp.zeros((1, events), jnp.int32) + lax.axis_index("hist")
    owner = jnp.concatenate([here, both_owner], axis=1)
    count = jnp.sum(jnp.where(iota(counts.shape, 0) == owner, counts, 0.0), axis=0, keepdims=True)
    inverse = 1.0 / jnp.maximum(count, 1.0)
    user = jnp.concatenate([hist_user, mine[:, :items], other[:, :items]], axis=1).astype(F32)
    diagonal = iota((lanes, lanes), 0) == iota((lanes, lanes), 1)
    for k in range(n):
        row = pays[k][owners : owners + 1, :lanes]
        column = jnp.sum(jnp.where(diagonal, row, 0.0), axis=1, keepdims=True)
        out[k] = jnp.where(column == user, inverse, 0.0)


def project_kernel(hist_emb, key_weight, value_weight, key_t, value, emb, keys, values, sems):
    width = value.shape[1]
    columns = pl.ds(col_start(width), width)
    copies = [
        pltpu.make_async_copy(key_weight.at[:, columns], keys, sems.at[0]),
        pltpu.make_async_copy(value_weight.at[:, columns], values, sems.at[1]),
        pltpu.make_async_copy(hist_emb, emb, sems.at[2]),
    ]
    for copy in copies:
        copy.start()
    for copy in copies:
        copy.wait()
    value[...] = dot(emb[...], values[...]).astype(BF16)
    key_t[...] = jnp.transpose(dot(emb[...], keys[...]).astype(BF16))


def embed_own_kernel(mine, other, block, total):
    items = mine.shape[0]
    depth = block.shape[0]
    at = pl.ds(pl.multiple_of(lax.axis_index("hist") * depth, depth), depth)
    total[:items] = dot(mine[:, at], block[...])
    total[items:] = dot(other[:, at], block[...])


def add_blocks(n, k, mine, other, base, blocks):
    depth = blocks[0].shape[0]
    groups = len(blocks)
    source = lax.rem(lax.axis_index("hist") + n - k, n)
    top, bottom = base
    for step, block in enumerate(blocks):
        group = lax.rem(lax.axis_index("groups") + groups - step, groups)
        at = pl.ds(pl.multiple_of((source * groups + group) * depth, depth), depth)
        top = top + dot(mine[:, at], block[...])
        bottom = bottom + dot(other[:, at], block[...])
    return top, bottom


def embed_add_kernel(n, k, groups, mine, other, total, *refs):
    items = mine.shape[0]
    top, bottom = add_blocks(n, k, mine, other, (total[:items], total[items:]), refs[:groups])
    refs[groups][:items] = top
    refs[groups][items:] = bottom


def embed_last_kernel(n, k, groups, mine, other, pick, total, *refs):
    items = mine.shape[0]
    top, bottom = add_blocks(n, k, mine, other, (total[:items], total[items:]), refs[:groups])
    rows, rows_t, query = refs[groups:]
    rows[:items] = top.astype(BF16)
    rows[items:] = bottom.astype(BF16)
    query[...] = dot(pick[...], rows[...]).astype(BF16)
    rows_t[...] = jnp.transpose(rows[...])


def attend_kernel(k, query, key_t, value, rows_t, rows, scale, out):
    cands, width = query.shape
    heads = width // HS
    lane = iota((cands, width), 1) // HS
    part = query[...] * (0.5 * HS ** -0.5)
    zero = jnp.zeros_like(part)
    split = jnp.concatenate([jnp.where(lane == h, part, zero) for h in range(heads)], axis=0)
    events = key_t.shape[1]

    def weigh(keys, factor):
        half = dot(split, keys)
        gated = half + half * jnp.tanh(half)
        return (gated * jnp.concatenate([factor] * heads, axis=0)).astype(BF16)

    mixed = dot(weigh(key_t[...], scale[k, :, :events]), value[...])
    mixed = mixed + dot(weigh(rows_t[...], scale[k, :, events:]), rows[...])
    total = jnp.zeros((cands, width), F32)
    for h in range(heads):
        total = total + jnp.where(lane == h, mixed[h * cands : (h + 1) * cands], 0.0)
    out[...] = total.astype(out.dtype)


def gate_kernel(query, own, *refs):
    parts, keep, send = refs[:-2], refs[-2], refs[-1]
    total = own[...]
    for part in parts:
        total = total + part[...].astype(F32)
    gate = query[...].astype(F32)
    scored = (gate * jax.nn.sigmoid(gate) * total).astype(BF16)
    half = keep.shape[0]
    keep[...] = scored[:half]
    send[...] = scored[half:]


def join_kernel(keep, got, out):
    width = keep.shape[1]
    first = lax.axis_index("rep") == 0
    out[:, :width] = jnp.where(first, keep[...], got[...])
    out[:, width:] = jnp.where(first, got[...], keep[...])


def shift(value, axis, k):
    count = lax.axis_size(axis)
    return lax.ppermute(value, axis, [(i, (i + k) % count) for i in range(count)])


def shift_order(n):
    return sorted(range(1, n), key=lambda k: min(k, n - k))


def fast_body(
    item_feats, adapter, hist_emb, key_weight, value_weight, routes, cand_index, item_user, hist_user
):
    n, groups = lax.axis_size("hist"), lax.axis_size("groups")
    items, _ = item_feats.shape
    depth, cols = adapter.shape
    width = cols // 2
    cands = 2 * cand_index.shape[0]
    events, dim = hist_emb.shape
    order = shift_order(n)

    block, own_share = call(
        share_kernel,
        (shape((depth, width), BF16), shape((depth // groups, width), BF16)),
        (adapter,),
        specs=[HBM],
        scratch=[pltpu.SemaphoreType.DMA((2,))],
    )
    along = {k: shift(own_share, "hist", k) for k in order}
    feats_other = shift(item_feats, "rep", 1)
    mine = jnp.concatenate([item_user, routes[:, 0], cand_index, cand_index, hist_user]).reshape(1, -1)
    other = shift(mine, "rep", 1)
    keys = events + 2 * items
    pay, hot, pick = call(
        users_kernel,
        (
            shape((8 + 8 * ((n + 7) // 8), USERS), F32),
            shape((USERS, keys), BF16),
            shape((cands, 2 * items), BF16),
        ),
        (mine, other),
    )
    pays = [pay] + [shift(pay, "hist", k) for k in range(1, n)]
    key_t, value = call(
        project_kernel,
        (shape((width, events), BF16), shape((events, width), BF16)),
        (hist_emb, key_weight, value_weight),
        flops=4 * events * dim * width,
        bytes_accessed=4 << 20,
        specs=[HBM] * 3,
        scratch=[
            pltpu.VMEM((events, dim), BF16),
            pltpu.VMEM((dim, width), BF16),
            pltpu.VMEM((dim, width), BF16),
            pltpu.SemaphoreType.DMA((3,)),
        ],
    )
    total = call(
        embed_own_kernel,
        shape((2 * items, width), F32),
        (item_feats, feats_other, block),
        flops=4 * items * depth * width,
        bytes_accessed=4 << 20,
    )
    scale = call(
        functools.partial(scale_kernel, n, items),
        shape((n, cands, keys), F32),
        (mine, other, hot, *pays),
        bytes_accessed=4 << 20,
    )
    across = {k: [along[k]] + [shift(along[k], "groups", g) for g in range(1, groups)] for k in order}
    for k in order[:-1]:
        total = call(
            functools.partial(embed_add_kernel, n, k, groups),
            shape((2 * items, width), F32),
            (item_feats, feats_other, total, *across[k]),
            flops=4 * items * depth * width,
            bytes_accessed=2 << 20,
        )
    k = order[-1]
    rows, rows_t, query = call(
        functools.partial(embed_last_kernel, n, k, groups),
        (shape((2 * items, width), BF16), shape((width, 2 * items), BF16), shape((cands, width), BF16)),
        (item_feats, feats_other, pick, total, *across[k]),
        flops=4 * items * depth * width,
        bytes_accessed=2 << 20,
    )
    queries = {k: shift(query, "hist", k) for k in order}

    def attend(k, block, dtype):
        return call(
            functools.partial(attend_kernel, k),
            shape((cands, width), dtype),
            (block, key_t, value, rows_t, rows, scale),
            flops=8 * cands * keys * width,
            bytes_accessed=1 << 20,
        )

    own = attend(0, query, F32)
    parts = [shift(attend(k, queries[k], BF16), "hist", n - k) for k in order]
    keep, send = call(
        gate_kernel,
        (shape((cands // 2, width), BF16), shape((cands // 2, width), BF16)),
        (query, own, *parts),
    )
    got = shift(send, "rep", 1)
    return call(join_kernel, shape((cands // 2, cols), BF16), (keep, got))


def body(*args):
    item_feats, adapter, cand_index = args[0], args[1], args[6]
    fits = (
        lax.axis_size("rep") == 2
        and lax.axis_size("hist") > 1
        and adapter.shape[0] % (128 * lax.axis_size("groups")) == 0
        and adapter.shape[1] % 256 == 0
        and 2 * cand_index.shape[0] == 128
        and item_feats.shape[0] % 128 == 0
    )
    return fast_body(*args) if fits else generic_body(*args)


def solution(mesh):
    placed = (
        P(("groups", "hist", "rep"), None),
        P("hist", "head"),
        P(("groups", "hist"), None),
        P(None, "head"),
        P(None, "head"),
        P(("groups", "hist", "rep"), None),
        P(("groups", "hist", "rep")),
        P(("groups", "hist", "rep")),
        P(("groups", "hist")),
    )
    return jax.shard_map(
        body,
        mesh=mesh,
        in_specs=placed,
        out_specs=P(("groups", "hist", "rep"), "head"),
        check_vma=False,
    )
```

```python
import functools
import math

import jax
import jax.numpy as jnp
from jax import lax
from jax.experimental import pallas as pl
from jax.experimental.pallas import tpu as pltpu
from jax.sharding import PartitionSpec as P


HS = 64
USERS = 256
LISTED = 32
VM = pl.BlockSpec(memory_space=pltpu.VMEM)
HBM = pl.BlockSpec(memory_space=pltpu.HBM)
F32 = jnp.float32
BF16 = jnp.bfloat16


def attend(query_block, user_block, key_rows, value_rows, key_users):
    row_count = query_block.shape[0]
    col_count = query_block.shape[1]
    heads_here = col_count // HS
    att_scale = float(HS) ** (-0.5)
    query_three = query_block.reshape(row_count, heads_here, HS)
    key_three = key_rows.reshape(-1, heads_here, HS)
    value_three = value_rows.reshape(-1, heads_here, HS)
    scores = (
        jnp.einsum("rhd,khd->hrk", query_three, key_three, preferred_element_type=jnp.float32)
        * att_scale
    )
    matching = user_block[:, None] == key_users[None, :]
    weights = jnp.where(matching[None], jax.nn.silu(scores), 0.0).astype(jnp.bfloat16)
    mixture = jnp.einsum("hrk,khd->rhd", weights, value_three, preferred_element_type=jnp.float32)
    counted = jnp.sum(matching.astype(jnp.float32), axis=1)
    inverse = 1.0 / jnp.maximum(counted, 1.0)
    return mixture.reshape(row_count, col_count) * inverse[:, None]


def dense_partial(queries, users, key_rows, value_rows, key_users):
    total_rows = queries.shape[0]
    col_count = queries.shape[1]
    block_size = math.gcd(total_rows, 512)
    blocked_queries = queries.reshape(total_rows // block_size, block_size, col_count)
    blocked_users = users.reshape(total_rows // block_size, block_size)

    def one_block(operands):
        return attend(operands[0], operands[1], key_rows, value_rows, key_users)

    return lax.map(one_block, (blocked_queries, blocked_users)).reshape(total_rows, col_count)


def generic_body(
    item_feats,
    adapter,
    hist_emb,
    key_weight,
    value_weight,
    routes,
    cand_index,
    item_user,
    hist_user,
):
    owners = lax.axis_size("hist")
    item_count = item_feats.shape[0]
    col_count = adapter.shape[1]
    embedded = jnp.dot(
        item_feats,
        lax.all_gather(adapter, "hist", axis=0, tiled=True),
        preferred_element_type=jnp.float32,
    ).astype(jnp.bfloat16)
    capacity = 2 * item_count // owners
    owner_of = routes[:, 0]
    owner_hot = (owner_of[:, None] == jnp.arange(owners, dtype=jnp.int32)[None, :]).astype(
        jnp.int32
    )
    earlier = jnp.cumsum(owner_hot, axis=0) - owner_hot
    slot_of = jnp.sum(earlier * owner_hot, axis=1)
    position = owner_of * capacity + slot_of
    placing = (jnp.arange(owners * capacity, dtype=jnp.int32)[:, None] == position[None, :]).astype(
        jnp.bfloat16
    )
    outgoing = jnp.dot(placing, embedded, preferred_element_type=jnp.float32).astype(jnp.bfloat16)
    outgoing = outgoing.reshape(owners, capacity, col_count)
    shifted_user = (item_user + 1).astype(jnp.bfloat16)
    outgoing_user = (
        jnp.dot(placing, shifted_user, preferred_element_type=jnp.float32) - 1.0
    ).astype(jnp.bfloat16)
    outgoing_user = outgoing_user.reshape(owners, capacity)
    incoming, incoming_user = (
        lax.all_to_all(outgoing, "hist", split_axis=0, concat_axis=0, tiled=True),
        lax.all_to_all(outgoing_user, "hist", split_axis=0, concat_axis=0, tiled=True),
    )
    routed, routed_user = (
        lax.all_gather(incoming, "rep", axis=0, tiled=True),
        lax.all_gather(incoming_user, "rep", axis=0, tiled=True),
    )
    routed = routed.reshape(-1, col_count)
    routed_user = routed_user.reshape(-1)
    key_local = jnp.dot(hist_emb, key_weight, preferred_element_type=jnp.float32).astype(
        jnp.bfloat16
    )
    value_local = jnp.dot(hist_emb, value_weight, preferred_element_type=jnp.float32).astype(
        jnp.bfloat16
    )
    key_rows = jnp.concatenate([key_local, routed], axis=0)
    value_rows = jnp.concatenate([value_local, routed], axis=0)
    key_users = jnp.concatenate([hist_user.astype(jnp.bfloat16), routed_user], axis=0)
    own_queries = embedded[cand_index]
    own_users = item_user[cand_index].astype(jnp.bfloat16)
    gathered, gathered_users = (
        lax.all_gather(own_queries, "hist", axis=0, tiled=True),
        lax.all_gather(own_users, "hist", axis=0, tiled=True),
    )
    partial_value = dense_partial(gathered, gathered_users, key_rows, value_rows, key_users)
    attended = lax.psum_scatter(partial_value, "hist", scatter_dimension=0, tiled=True)
    gating = jax.nn.silu(own_queries.astype(jnp.float32))
    return (gating * attended).astype(jnp.bfloat16)


def call(kernel, outs, args, flops=0, bytes_accessed=1 << 18, vmem=16, specs=None, scratch=()):
    if specs:
        args = [pltpu.with_memory_space_constraint(arg, pltpu.HBM) for arg in args]
    return pl.pallas_call(
        kernel,
        out_shape=outs,
        in_specs=specs or [VM] * len(args),
        out_specs=jax.tree.map(lambda _: VM, outs),
        scratch_shapes=scratch,
        compiler_params=pltpu.CompilerParams(vmem_limit_bytes=vmem << 20),
        cost_estimate=pl.CostEstimate(flops=flops, bytes_accessed=bytes_accessed, transcendentals=0),
    )(*args)


def shape(dims, dtype):
    return jax.ShapeDtypeStruct(dims, dtype)


def iota(dims, axis):
    return lax.broadcasted_iota(jnp.int32, dims, axis)


def dot(a, b, contract=((1,), (0,))):
    return lax.dot_general(a, b, (contract, ((), ())), preferred_element_type=F32)


def col_start(width):
    return pl.multiple_of(lax.axis_index("rep") * width, width)


def one_hot(dims, axis, at):
    return (iota(dims, axis) == at).astype(F32).astype(BF16)


def share_kernel(
    adapter, item_user, routes, cand_index, hist_user, block, out, mine, user, owner, cand, event, events, sems
):
    _, cols = block.shape
    rows = out.shape[0] - LISTED
    row = pl.multiple_of(lax.axis_index("groups") * rows, rows)
    columns = pl.ds(col_start(cols), cols)
    part = event.shape[1]
    copies = [
        pltpu.make_async_copy(item_user, user, sems.at[0]),
        pltpu.make_async_copy(routes, owner, sems.at[1]),
        pltpu.make_async_copy(cand_index, cand, sems.at[2]),
        pltpu.make_async_copy(hist_user.at[:, pl.ds(col_start(part), part)], event, sems.at[3]),
        pltpu.make_async_copy(adapter.at[pl.ds(row, rows), columns], out.at[pl.ds(0, rows)], sems.at[4]),
        pltpu.make_async_copy(adapter.at[:, columns], block, sems.at[5]),
        pltpu.make_async_copy(hist_user, events, sems.at[6]),
    ]
    for copy in copies:
        copy.start()
    for copy in copies[:4]:
        copy.wait()
    items = user.shape[1]
    cands = cand.shape[1]
    mine[:, :items] = user[...]
    mine[:, items : 2 * items] = owner[...]
    mine[:, 2 * items : 2 * items + 2 * cands] = jnp.concatenate([cand[...], cand[...]], axis=1)
    items_hot = one_hot((USERS, items), 0, user[...])
    counts = dot(one_hot((8, items), 0, owner[...]), items_hot, ((1,), (1,)))
    here = jnp.zeros((1, part), jnp.int32) + lax.axis_index("hist")
    counts = counts + dot(one_hot((8, part), 0, here), one_hot((USERS, part), 0, event[...]), ((1,), (1,)))
    chosen = one_hot((items, cands), 0, cand[...])
    users = dot(jnp.broadcast_to(user[...], (8, items)).astype(F32).astype(BF16), chosen)
    users = jnp.concatenate([users, jnp.zeros((8, USERS - cands), F32)], axis=1)
    high = jnp.floor(counts * (1.0 / 256.0))
    low = jnp.where(iota(counts.shape, 0) == 7, users, counts - 256.0 * high)
    half = USERS // 2
    listed = jnp.concatenate([low[:, :half], low[:, half:], high[:, :half], high[:, half:]], axis=0)
    out[rows:] = listed.astype(BF16)
    for copy in copies[4:]:
        copy.wait()
    mine[:, 2 * items + 2 * cands :] = events[...]


def users_kernel(mine, other, hot, pick):
    lanes, both = pick.shape
    items = both // 2
    half = lanes // 2
    both_user = jnp.concatenate([mine[:, :items], other[:, :items]], axis=1)
    at = slice(2 * items, 2 * items + lanes)
    moved = pltpu.roll(jnp.broadcast_to(other[:, at], (8, lanes)), half, 1)[:1] + items
    cand = jnp.where(iota((1, lanes), 1) < half, mine[:, at], moved)
    event_user = mine[:, 2 * items + lanes :]
    events = event_user.shape[1]
    hot[:, :events] = one_hot((USERS, events), 0, event_user)
    hot[:, events:] = one_hot((USERS, both), 0, both_user)
    chosen = (iota((both, lanes), 0) == cand).astype(F32)
    pick[...] = jnp.transpose(chosen).astype(BF16)


def tally_kernel(*refs):
    out = refs[-1]
    total = jnp.zeros((8, USERS), F32)
    for k, ref in enumerate(refs[:-1]):
        listed = ref[ref.shape[0] - LISTED :].astype(F32)
        low = jnp.concatenate([listed[:8], listed[8:16]], axis=1)
        high = jnp.concatenate([listed[16:24], listed[24:]], axis=1)
        total = total + low + 256.0 * high
        out[8 + k : 9 + k] = low[7:8]
    out[:8] = total


def scale_kernel(items, mine, other, hot, tally, tally_other, out):
    n, lanes, _ = out.shape
    hist_user = mine[:, 2 * items + lanes :]
    events = hist_user.shape[1]
    total = tally[:8] + tally_other[:8]
    high = jnp.floor(total * (1.0 / 256.0))
    low = total - 256.0 * high
    counts = 256.0 * dot(high.astype(BF16), hot[...]) + dot(low.astype(BF16), hot[...])
    both_owner = jnp.concatenate([mine[:, items : 2 * items], other[:, items : 2 * items]], axis=1)
    here = jnp.zeros((1, events), jnp.int32) + lax.axis_index("hist")
    owner = jnp.concatenate([here, both_owner], axis=1)
    count = jnp.sum(jnp.where(iota(counts.shape, 0) == owner, counts, 0.0), axis=0, keepdims=True)
    inverse = 1.0 / jnp.maximum(count, 1.0)
    user = jnp.concatenate([hist_user, mine[:, :items], other[:, :items]], axis=1).astype(F32)
    diagonal = iota((lanes, lanes), 0) == iota((lanes, lanes), 1)
    first = iota((8, lanes), 1) < lanes // 2
    near = tally[8:16, :lanes]
    far = pltpu.roll(tally_other[8:16, :lanes], lanes // 2, 1)
    cand = jnp.where(first, near, far)
    for k in range(n):
        column = jnp.sum(jnp.where(diagonal, cand[k : k + 1], 0.0), axis=1, keepdims=True)
        out[k] = jnp.where(column == user, inverse, 0.0)


def project_kernel(hist_emb, key_weight, value_weight, key_t, value, emb, keys, values, sems):
    width = value.shape[1]
    columns = pl.ds(col_start(width), width)
    copies = [
        pltpu.make_async_copy(key_weight.at[:, columns], keys, sems.at[0]),
        pltpu.make_async_copy(value_weight.at[:, columns], values, sems.at[1]),
        pltpu.make_async_copy(hist_emb, emb, sems.at[2]),
    ]
    for copy in copies:
        copy.start()
    for copy in copies:
        copy.wait()
    value[...] = dot(emb[...], values[...]).astype(BF16)
    key_t[...] = jnp.transpose(dot(emb[...], keys[...]).astype(BF16))


def embed_own_kernel(mine, other, block, total):
    items = mine.shape[0]
    depth = block.shape[0]
    at = pl.ds(pl.multiple_of(lax.axis_index("hist") * depth, depth), depth)
    total[:items] = dot(mine[:, at], block[...])
    total[items:] = dot(other[:, at], block[...])


def add_blocks(n, k, mine, other, base, blocks):
    depth = blocks[0].shape[0] - LISTED
    groups = len(blocks)
    source = lax.rem(lax.axis_index("hist") + n - k, n)
    top, bottom = base
    for step, block in enumerate(blocks):
        group = lax.rem(lax.axis_index("groups") + groups - step, groups)
        at = pl.ds(pl.multiple_of((source * groups + group) * depth, depth), depth)
        top = top + dot(mine[:, at], block[:depth])
        bottom = bottom + dot(other[:, at], block[:depth])
    return top, bottom


def embed_add_kernel(n, k, groups, mine, other, total, *refs):
    items = mine.shape[0]
    top, bottom = add_blocks(n, k, mine, other, (total[:items], total[items:]), refs[:groups])
    refs[groups][:items] = top
    refs[groups][items:] = bottom


def embed_last_kernel(n, k, groups, mine, other, pick, total, *refs):
    items = mine.shape[0]
    top, bottom = add_blocks(n, k, mine, other, (total[:items], total[items:]), refs[:groups])
    rows, rows_t, query = refs[groups:]
    rows[:items] = top.astype(BF16)
    rows[items:] = bottom.astype(BF16)
    query[...] = dot(pick[...], rows[...]).astype(BF16)
    rows_t[...] = jnp.transpose(rows[...])


def attend_kernel(k, query, key_t, value, rows_t, rows, scale, out):
    cands, width = query.shape
    heads = width // HS
    lane = iota((cands, width), 1) // HS
    part = query[...] * (0.5 * HS ** -0.5)
    zero = jnp.zeros_like(part)
    split = jnp.concatenate([jnp.where(lane == h, part, zero) for h in range(heads)], axis=0)
    events = key_t.shape[1]

    def weigh(keys, factor):
        half = dot(split, keys)
        gated = half + half * jnp.tanh(half)
        return (gated * jnp.concatenate([factor] * heads, axis=0)).astype(BF16)

    mixed = dot(weigh(key_t[...], scale[k, :, :events]), value[...])
    mixed = mixed + dot(weigh(rows_t[...], scale[k, :, events:]), rows[...])
    total = jnp.zeros((cands, width), F32)
    for h in range(heads):
        total = total + jnp.where(lane == h, mixed[h * cands : (h + 1) * cands], 0.0)
    out[...] = total.astype(out.dtype)


def gate_kernel(query, own, *refs):
    parts, keep, send = refs[:-2], refs[-2], refs[-1]
    total = own[...]
    for part in parts:
        total = total + part[...].astype(F32)
    gate = query[...].astype(F32)
    scored = (gate * jax.nn.sigmoid(gate) * total).astype(BF16)
    half = keep.shape[0]
    keep[...] = scored[:half]
    send[...] = scored[half:]


def join_kernel(keep, got, out):
    width = keep.shape[1]
    first = lax.axis_index("rep") == 0
    out[:, :width] = jnp.where(first, keep[...], got[...])
    out[:, width:] = jnp.where(first, got[...], keep[...])


def shift(value, axis, k):
    count = lax.axis_size(axis)
    return lax.ppermute(value, axis, [(i, (i + k) % count) for i in range(count)])


def shift_order(n):
    return sorted(range(1, n), key=lambda k: min(k, n - k))


def fast_body(
    item_feats, adapter, hist_emb, key_weight, value_weight, routes, cand_index, item_user, hist_user
):
    n, groups = lax.axis_size("hist"), lax.axis_size("groups")
    items, _ = item_feats.shape
    depth, cols = adapter.shape
    width = cols // 2
    cands = 2 * cand_index.shape[0]
    events, dim = hist_emb.shape
    order = shift_order(n)

    block, own_share, mine = call(
        share_kernel,
        (
            shape((depth, width), BF16),
            shape((depth // groups + LISTED, width), BF16),
            shape((1, 2 * items + cands + events), jnp.int32),
        ),
        (
            adapter,
            item_user.reshape(1, -1),
            routes.reshape(1, -1),
            cand_index.reshape(1, -1),
            hist_user.reshape(1, -1),
        ),
        specs=[HBM] * 5,
        scratch=[
            pltpu.VMEM((1, items), jnp.int32),
            pltpu.VMEM((1, items), jnp.int32),
            pltpu.VMEM((1, cands // 2), jnp.int32),
            pltpu.VMEM((1, events // 2), jnp.int32),
            pltpu.VMEM((1, events), jnp.int32),
            pltpu.SemaphoreType.DMA((7,)),
        ],
    )
    along = {k: shift(own_share, "hist", k) for k in order}
    feats_other = shift(item_feats, "rep", 1)
    other = shift(mine, "rep", 1)
    keys = events + 2 * items
    hot, pick = call(
        users_kernel, (shape((USERS, keys), BF16), shape((cands, 2 * items), BF16)), (mine, other)
    )
    key_t, value = call(
        project_kernel,
        (shape((width, events), BF16), shape((events, width), BF16)),
        (hist_emb, key_weight, value_weight),
        flops=4 * events * dim * width,
        bytes_accessed=4 << 20,
        specs=[HBM] * 3,
        scratch=[
            pltpu.VMEM((events, dim), BF16),
            pltpu.VMEM((dim, width), BF16),
            pltpu.VMEM((dim, width), BF16),
            pltpu.SemaphoreType.DMA((3,)),
        ],
    )
    total = call(
        embed_own_kernel,
        shape((2 * items, width), F32),
        (item_feats, feats_other, block),
        flops=4 * items * depth * width,
        bytes_accessed=4 << 20,
    )
    tally = call(
        tally_kernel, shape((16, USERS), F32), (own_share, *[along[k] for k in range(1, n)])
    )
    scale = call(
        functools.partial(scale_kernel, items),
        shape((n, cands, keys), F32),
        (mine, other, hot, tally, shift(tally, "rep", 1)),
        bytes_accessed=4 << 20,
    )
    across = {k: [along[k]] + [shift(along[k], "groups", g) for g in range(1, groups)] for k in order}
    for k in order[:-1]:
        total = call(
            functools.partial(embed_add_kernel, n, k, groups),
            shape((2 * items, width), F32),
            (item_feats, feats_other, total, *across[k]),
            flops=4 * items * depth * width,
            bytes_accessed=2 << 20,
        )
    k = order[-1]
    rows, rows_t, query = call(
        functools.partial(embed_last_kernel, n, k, groups),
        (shape((2 * items, width), BF16), shape((width, 2 * items), BF16), shape((cands, width), BF16)),
        (item_feats, feats_other, pick, total, *across[k]),
        flops=4 * items * depth * width,
        bytes_accessed=2 << 20,
    )
    queries = {k: shift(query, "hist", k) for k in order}

    def attend(k, block, dtype):
        return call(
            functools.partial(attend_kernel, k),
            shape((cands, width), dtype),
            (block, key_t, value, rows_t, rows, scale),
            flops=8 * cands * keys * width,
            bytes_accessed=1 << 20,
        )

    own = attend(0, query, F32)
    parts = [shift(attend(k, queries[k], BF16), "hist", n - k) for k in order]
    keep, send = call(
        gate_kernel,
        (shape((cands // 2, width), BF16), shape((cands // 2, width), BF16)),
        (query, own, *parts),
    )
    got = shift(send, "rep", 1)
    return call(join_kernel, shape((cands // 2, cols), BF16), (keep, got))


def body(*args):
    item_feats, adapter, cand_index, hist_user = args[0], args[1], args[6], args[8]
    fits = (
        lax.axis_size("rep") == 2
        and 1 < lax.axis_size("hist") < 8
        and hist_user.shape[0] % 256 == 0
        and adapter.shape[0] % (128 * lax.axis_size("groups")) == 0
        and adapter.shape[1] % 256 == 0
        and 2 * cand_index.shape[0] == 128
        and item_feats.shape[0] % 128 == 0
    )
    return fast_body(*args) if fits else generic_body(*args)


def solution(mesh):
    placed = (
        P(("groups", "hist", "rep"), None),
        P("hist", "head"),
        P(("groups", "hist"), None),
        P(None, "head"),
        P(None, "head"),
        P(("groups", "hist", "rep"), None),
        P(("groups", "hist", "rep")),
        P(("groups", "hist", "rep")),
        P(("groups", "hist")),
    )
    return jax.shard_map(
        body,
        mesh=mesh,
        in_specs=placed,
        out_specs=P(("groups", "hist", "rep"), "head"),
        check_vma=False,
    )
```

```python
import functools
import math

import jax
import jax.numpy as jnp
from jax import lax
from jax.experimental import pallas as pl
from jax.experimental.pallas import tpu as pltpu
from jax.sharding import PartitionSpec as P


HS = 64
USERS = 256
LISTED = 32
VM = pl.BlockSpec(memory_space=pltpu.VMEM)
HBM = pl.BlockSpec(memory_space=pltpu.HBM)
F32 = jnp.float32
BF16 = jnp.bfloat16


def attend(query_block, user_block, key_rows, value_rows, key_users):
    row_count = query_block.shape[0]
    col_count = query_block.shape[1]
    heads_here = col_count // HS
    att_scale = float(HS) ** (-0.5)
    query_three = query_block.reshape(row_count, heads_here, HS)
    key_three = key_rows.reshape(-1, heads_here, HS)
    value_three = value_rows.reshape(-1, heads_here, HS)
    scores = (
        jnp.einsum("rhd,khd->hrk", query_three, key_three, preferred_element_type=jnp.float32)
        * att_scale
    )
    matching = user_block[:, None] == key_users[None, :]
    weights = jnp.where(matching[None], jax.nn.silu(scores), 0.0).astype(jnp.bfloat16)
    mixture = jnp.einsum("hrk,khd->rhd", weights, value_three, preferred_element_type=jnp.float32)
    counted = jnp.sum(matching.astype(jnp.float32), axis=1)
    inverse = 1.0 / jnp.maximum(counted, 1.0)
    return mixture.reshape(row_count, col_count) * inverse[:, None]


def dense_partial(queries, users, key_rows, value_rows, key_users):
    total_rows = queries.shape[0]
    col_count = queries.shape[1]
    block_size = math.gcd(total_rows, 512)
    blocked_queries = queries.reshape(total_rows // block_size, block_size, col_count)
    blocked_users = users.reshape(total_rows // block_size, block_size)

    def one_block(operands):
        return attend(operands[0], operands[1], key_rows, value_rows, key_users)

    return lax.map(one_block, (blocked_queries, blocked_users)).reshape(total_rows, col_count)


def generic_body(
    item_feats,
    adapter,
    hist_emb,
    key_weight,
    value_weight,
    routes,
    cand_index,
    item_user,
    hist_user,
):
    owners = lax.axis_size("hist")
    item_count = item_feats.shape[0]
    col_count = adapter.shape[1]
    embedded = jnp.dot(
        item_feats,
        lax.all_gather(adapter, "hist", axis=0, tiled=True),
        preferred_element_type=jnp.float32,
    ).astype(jnp.bfloat16)
    capacity = 2 * item_count // owners
    owner_of = routes[:, 0]
    owner_hot = (owner_of[:, None] == jnp.arange(owners, dtype=jnp.int32)[None, :]).astype(
        jnp.int32
    )
    earlier = jnp.cumsum(owner_hot, axis=0) - owner_hot
    slot_of = jnp.sum(earlier * owner_hot, axis=1)
    position = owner_of * capacity + slot_of
    placing = (jnp.arange(owners * capacity, dtype=jnp.int32)[:, None] == position[None, :]).astype(
        jnp.bfloat16
    )
    outgoing = jnp.dot(placing, embedded, preferred_element_type=jnp.float32).astype(jnp.bfloat16)
    outgoing = outgoing.reshape(owners, capacity, col_count)
    shifted_user = (item_user + 1).astype(jnp.bfloat16)
    outgoing_user = (
        jnp.dot(placing, shifted_user, preferred_element_type=jnp.float32) - 1.0
    ).astype(jnp.bfloat16)
    outgoing_user = outgoing_user.reshape(owners, capacity)
    incoming, incoming_user = (
        lax.all_to_all(outgoing, "hist", split_axis=0, concat_axis=0, tiled=True),
        lax.all_to_all(outgoing_user, "hist", split_axis=0, concat_axis=0, tiled=True),
    )
    routed, routed_user = (
        lax.all_gather(incoming, "rep", axis=0, tiled=True),
        lax.all_gather(incoming_user, "rep", axis=0, tiled=True),
    )
    routed = routed.reshape(-1, col_count)
    routed_user = routed_user.reshape(-1)
    key_local = jnp.dot(hist_emb, key_weight, preferred_element_type=jnp.float32).astype(
        jnp.bfloat16
    )
    value_local = jnp.dot(hist_emb, value_weight, preferred_element_type=jnp.float32).astype(
        jnp.bfloat16
    )
    key_rows = jnp.concatenate([key_local, routed], axis=0)
    value_rows = jnp.concatenate([value_local, routed], axis=0)
    key_users = jnp.concatenate([hist_user.astype(jnp.bfloat16), routed_user], axis=0)
    own_queries = embedded[cand_index]
    own_users = item_user[cand_index].astype(jnp.bfloat16)
    gathered, gathered_users = (
        lax.all_gather(own_queries, "hist", axis=0, tiled=True),
        lax.all_gather(own_users, "hist", axis=0, tiled=True),
    )
    partial_value = dense_partial(gathered, gathered_users, key_rows, value_rows, key_users)
    attended = lax.psum_scatter(partial_value, "hist", scatter_dimension=0, tiled=True)
    gating = jax.nn.silu(own_queries.astype(jnp.float32))
    return (gating * attended).astype(jnp.bfloat16)


def call(kernel, outs, args, flops=0, bytes_accessed=1 << 18, vmem=16, specs=None, scratch=()):
    if specs:
        args = [pltpu.with_memory_space_constraint(arg, pltpu.HBM) for arg in args]
    return pl.pallas_call(
        kernel,
        out_shape=outs,
        in_specs=specs or [VM] * len(args),
        out_specs=jax.tree.map(lambda _: VM, outs),
        scratch_shapes=scratch,
        compiler_params=pltpu.CompilerParams(vmem_limit_bytes=vmem << 20),
        cost_estimate=pl.CostEstimate(flops=flops, bytes_accessed=bytes_accessed, transcendentals=0),
    )(*args)


def shape(dims, dtype):
    return jax.ShapeDtypeStruct(dims, dtype)


def iota(dims, axis):
    return lax.broadcasted_iota(jnp.int32, dims, axis)


def dot(a, b, contract=((1,), (0,))):
    return lax.dot_general(a, b, (contract, ((), ())), preferred_element_type=F32)


def col_start(width):
    return pl.multiple_of(lax.axis_index("rep") * width, width)


def one_hot(dims, axis, at):
    return (iota(dims, axis) == at).astype(F32).astype(BF16)


def share_kernel(
    adapter, item_user, routes, cand_index, hist_user, block, out, mine, user, owner, cand, event, events, sems
):
    _, cols = block.shape
    rows = out.shape[0] - LISTED
    row = pl.multiple_of(lax.axis_index("groups") * rows, rows)
    columns = pl.ds(col_start(cols), cols)
    part = event.shape[1]
    copies = [
        pltpu.make_async_copy(item_user, user, sems.at[0]),
        pltpu.make_async_copy(routes, owner, sems.at[1]),
        pltpu.make_async_copy(cand_index, cand, sems.at[2]),
        pltpu.make_async_copy(hist_user.at[:, pl.ds(col_start(part), part)], event, sems.at[3]),
        pltpu.make_async_copy(adapter.at[pl.ds(row, rows), columns], out.at[pl.ds(0, rows)], sems.at[4]),
        pltpu.make_async_copy(adapter.at[:, columns], block, sems.at[5]),
        pltpu.make_async_copy(hist_user, events, sems.at[6]),
    ]
    for copy in copies:
        copy.start()
    for copy in copies[:4]:
        copy.wait()
    items = user.shape[1]
    cands = cand.shape[1]
    mine[:, :items] = user[...]
    mine[:, items : 2 * items] = owner[...]
    mine[:, 2 * items : 2 * items + 2 * cands] = jnp.concatenate([cand[...], cand[...]], axis=1)
    items_hot = one_hot((USERS, items), 0, user[...])
    counts = dot(one_hot((8, items), 0, owner[...]), items_hot, ((1,), (1,)))
    here = jnp.zeros((1, part), jnp.int32) + lax.axis_index("hist")
    counts = counts + dot(one_hot((8, part), 0, here), one_hot((USERS, part), 0, event[...]), ((1,), (1,)))
    chosen = one_hot((items, cands), 0, cand[...])
    users = dot(jnp.broadcast_to(user[...], (8, items)).astype(F32).astype(BF16), chosen)
    users = jnp.concatenate([users, jnp.zeros((8, USERS - cands), F32)], axis=1)
    high = jnp.floor(counts * (1.0 / 256.0))
    low = jnp.where(iota(counts.shape, 0) == 7, users, counts - 256.0 * high)
    half = USERS // 2
    listed = jnp.concatenate([low[:, :half], low[:, half:], high[:, :half], high[:, half:]], axis=0)
    out[rows:] = listed.astype(BF16)
    for copy in copies[4:]:
        copy.wait()
    mine[:, 2 * items + 2 * cands :] = events[...]


def users_kernel(mine, other, hot, pick):
    lanes, both = pick.shape
    items = both // 2
    half = lanes // 2
    both_user = jnp.concatenate([mine[:, :items], other[:, :items]], axis=1)
    at = slice(2 * items, 2 * items + lanes)
    moved = pltpu.roll(jnp.broadcast_to(other[:, at], (8, lanes)), half, 1)[:1] + items
    cand = jnp.where(iota((1, lanes), 1) < half, mine[:, at], moved)
    event_user = mine[:, 2 * items + lanes :]
    events = event_user.shape[1]
    hot[:, :events] = one_hot((USERS, events), 0, event_user)
    hot[:, events:] = one_hot((USERS, both), 0, both_user)
    chosen = (iota((both, lanes), 0) == cand).astype(F32)
    pick[...] = jnp.transpose(chosen).astype(BF16)


def tally_kernel(*refs):
    out = refs[-1]
    total = jnp.zeros((8, USERS), F32)
    for k, ref in enumerate(refs[:-1]):
        listed = ref[ref.shape[0] - LISTED :].astype(F32)
        low = jnp.concatenate([listed[:8], listed[8:16]], axis=1)
        high = jnp.concatenate([listed[16:24], listed[24:]], axis=1)
        total = total + low + 256.0 * high
        out[8 + k : 9 + k] = low[7:8]
    out[:8] = total


def scale_kernel(items, mine, other, hot, tally, tally_other, out):
    n, lanes, _ = out.shape
    hist_user = mine[:, 2 * items + lanes :]
    events = hist_user.shape[1]
    total = tally[:8] + tally_other[:8]
    high = jnp.floor(total * (1.0 / 256.0))
    low = total - 256.0 * high
    counts = 256.0 * dot(high.astype(BF16), hot[...]) + dot(low.astype(BF16), hot[...])
    both_owner = jnp.concatenate([mine[:, items : 2 * items], other[:, items : 2 * items]], axis=1)
    here = jnp.zeros((1, events), jnp.int32) + lax.axis_index("hist")
    owner = jnp.concatenate([here, both_owner], axis=1)
    count = jnp.sum(jnp.where(iota(counts.shape, 0) == owner, counts, 0.0), axis=0, keepdims=True)
    inverse = 1.0 / jnp.maximum(count, 1.0)
    user = jnp.concatenate([hist_user, mine[:, :items], other[:, :items]], axis=1).astype(F32)
    diagonal = iota((lanes, lanes), 0) == iota((lanes, lanes), 1)
    first = iota((8, lanes), 1) < lanes // 2
    near = tally[8:16, :lanes]
    far = pltpu.roll(tally_other[8:16, :lanes], lanes // 2, 1)
    cand = jnp.where(first, near, far)
    for k in range(n):
        column = jnp.sum(jnp.where(diagonal, cand[k : k + 1], 0.0), axis=1, keepdims=True)
        out[k] = jnp.where(column == user, inverse, 0.0)


def project_kernel(hist_emb, key_weight, value_weight, key_t, value, emb, keys, values, sems):
    width = value.shape[1]
    columns = pl.ds(col_start(width), width)
    copies = [
        pltpu.make_async_copy(key_weight.at[:, columns], keys, sems.at[0]),
        pltpu.make_async_copy(value_weight.at[:, columns], values, sems.at[1]),
        pltpu.make_async_copy(hist_emb, emb, sems.at[2]),
    ]
    for copy in copies:
        copy.start()
    for copy in copies:
        copy.wait()
    value[...] = dot(emb[...], values[...]).astype(BF16)
    key_t[...] = jnp.transpose(dot(emb[...], keys[...]).astype(BF16))


def embed_own_kernel(mine, other, block, total):
    items = mine.shape[0]
    depth = block.shape[0]
    at = pl.ds(pl.multiple_of(lax.axis_index("hist") * depth, depth), depth)
    total[:items] = dot(mine[:, at], block[...])
    total[items:] = dot(other[:, at], block[...])


def add_block(n, groups, k, step, mine, other, top, bottom, block):
    depth = block.shape[0] - LISTED
    source = lax.rem(lax.axis_index("hist") + n - k, n)
    group = lax.rem(lax.axis_index("groups") + groups - step, groups)
    at = pl.ds(pl.multiple_of((source * groups + group) * depth, depth), depth)
    return top + dot(mine[:, at], block[:depth]), bottom + dot(other[:, at], block[:depth])


def embed_add_kernel(n, groups, which, mine, other, total, *refs):
    items = mine.shape[0]
    top, bottom = total[:items], total[items:]
    for (k, step), block in zip(which, refs):
        top, bottom = add_block(n, groups, k, step, mine, other, top, bottom, block)
    refs[-1][:items] = top
    refs[-1][items:] = bottom


def embed_last_kernel(n, groups, which, mine, other, pick, total, *refs):
    items = mine.shape[0]
    top, bottom = total[:items], total[items:]
    for (k, step), block in zip(which, refs):
        top, bottom = add_block(n, groups, k, step, mine, other, top, bottom, block)
    rows, rows_t, query = refs[len(which) :]
    rows[:items] = top.astype(BF16)
    rows[items:] = bottom.astype(BF16)
    query[...] = dot(pick[...], rows[...]).astype(BF16)
    rows_t[...] = jnp.transpose(rows[...])


def attend_kernel(k, query, key_t, value, rows_t, rows, scale, out):
    cands, width = query.shape
    heads = width // HS
    lane = iota((cands, width), 1) // HS
    part = query[...] * (0.5 * HS ** -0.5)
    zero = jnp.zeros_like(part)
    split = jnp.concatenate([jnp.where(lane == h, part, zero) for h in range(heads)], axis=0)
    events = key_t.shape[1]

    def weigh(keys, factor):
        half = dot(split, keys)
        gated = half + half * jnp.tanh(half)
        return (gated * jnp.concatenate([factor] * heads, axis=0)).astype(BF16)

    mixed = dot(weigh(key_t[...], scale[k, :, :events]), value[...])
    mixed = mixed + dot(weigh(rows_t[...], scale[k, :, events:]), rows[...])
    total = jnp.zeros((cands, width), F32)
    for h in range(heads):
        total = total + jnp.where(lane == h, mixed[h * cands : (h + 1) * cands], 0.0)
    out[...] = total.astype(out.dtype)


def gate_kernel(query, own, *refs):
    parts, keep, send = refs[:-2], refs[-2], refs[-1]
    total = own[...]
    for part in parts:
        total = total + part[...].astype(F32)
    gate = query[...].astype(F32)
    scored = (gate * jax.nn.sigmoid(gate) * total).astype(BF16)
    half = keep.shape[0]
    keep[...] = scored[:half]
    send[...] = scored[half:]


def join_kernel(keep, got, out):
    width = keep.shape[1]
    first = lax.axis_index("rep") == 0
    out[:, :width] = jnp.where(first, keep[...], got[...])
    out[:, width:] = jnp.where(first, got[...], keep[...])


def shift(value, axis, k):
    count = lax.axis_size(axis)
    return lax.ppermute(value, axis, [(i, (i + k) % count) for i in range(count)])


def shift_order(n):
    return sorted(range(1, n), key=lambda k: min(k, n - k))


def fast_body(
    item_feats, adapter, hist_emb, key_weight, value_weight, routes, cand_index, item_user, hist_user
):
    n, groups = lax.axis_size("hist"), lax.axis_size("groups")
    items, _ = item_feats.shape
    depth, cols = adapter.shape
    width = cols // 2
    cands = 2 * cand_index.shape[0]
    events, dim = hist_emb.shape
    order = shift_order(n)

    block, own_share, mine = call(
        share_kernel,
        (
            shape((depth, width), BF16),
            shape((depth // groups + LISTED, width), BF16),
            shape((1, 2 * items + cands + events), jnp.int32),
        ),
        (
            adapter,
            item_user.reshape(1, -1),
            routes.reshape(1, -1),
            cand_index.reshape(1, -1),
            hist_user.reshape(1, -1),
        ),
        specs=[HBM] * 5,
        scratch=[
            pltpu.VMEM((1, items), jnp.int32),
            pltpu.VMEM((1, items), jnp.int32),
            pltpu.VMEM((1, cands // 2), jnp.int32),
            pltpu.VMEM((1, events // 2), jnp.int32),
            pltpu.VMEM((1, events), jnp.int32),
            pltpu.SemaphoreType.DMA((7,)),
        ],
    )
    along = {}
    for k in order:
        if k in (1, n - 1):
            along[k] = shift(own_share, "hist", k)
        else:
            step = 1 if k <= n // 2 else n - 1
            along[k] = shift(along[(k - step) % n], "hist", step)
    feats_other = shift(item_feats, "rep", 1)
    other = shift(mine, "rep", 1)
    keys = events + 2 * items
    hot, pick = call(users_kernel, (shape((USERS, keys), BF16), shape((cands, 2 * items), BF16)), (mine, other))
    key_t, value = call(
        project_kernel,
        (shape((width, events), BF16), shape((events, width), BF16)),
        (hist_emb, key_weight, value_weight),
        flops=4 * events * dim * width,
        bytes_accessed=4 << 20,
        specs=[HBM] * 3,
        scratch=[
            pltpu.VMEM((events, dim), BF16),
            pltpu.VMEM((dim, width), BF16),
            pltpu.VMEM((dim, width), BF16),
            pltpu.SemaphoreType.DMA((3,)),
        ],
    )
    total = call(
        embed_own_kernel,
        shape((2 * items, width), F32),
        (item_feats, feats_other, block),
        flops=4 * items * depth * width,
        bytes_accessed=4 << 20,
    )
    tally = call(tally_kernel, shape((16, USERS), F32), (own_share, *[along[k] for k in range(1, n)]))
    scale = call(
        functools.partial(scale_kernel, items),
        shape((n, cands, keys), F32),
        (mine, other, hot, tally, shift(tally, "rep", 1)),
        bytes_accessed=4 << 20,
    )
    across = {k: [along[k]] + [shift(along[k], "groups", g) for g in range(1, groups)] for k in order}
    blocks = [((k, step), across[k][step]) for k in order for step in range(groups)]
    chunks = [blocks[at : at + groups] for at in range(0, len(blocks) - groups, groups)]
    chunks += [blocks[-groups:-1]]
    for k, chunk in zip(order, chunks):
        which, arrived = zip(*chunk)
        total = call(
            functools.partial(embed_add_kernel, n, groups, which),
            shape((2 * items, width), F32),
            (item_feats, feats_other, total, *arrived),
            flops=4 * items * depth * width,
            bytes_accessed=2 << 20,
        )
    which, arrived = zip(*blocks[-1:])
    rows, rows_t, query = call(
        functools.partial(embed_last_kernel, n, groups, which),
        (shape((2 * items, width), BF16), shape((width, 2 * items), BF16), shape((cands, width), BF16)),
        (item_feats, feats_other, pick, total, *arrived),
        flops=4 * items * depth * width,
        bytes_accessed=2 << 20,
    )
    queries = {k: shift(query, "hist", k) for k in order}

    def attend(k, block, dtype):
        return call(
            functools.partial(attend_kernel, k),
            shape((cands, width), dtype),
            (block, key_t, value, rows_t, rows, scale),
            flops=8 * cands * keys * width,
            bytes_accessed=1 << 20,
        )

    own = attend(0, query, F32)
    parts = [shift(attend(k, queries[k], BF16), "hist", n - k) for k in order]
    keep, send = call(
        gate_kernel, (shape((cands // 2, width), BF16), shape((cands // 2, width), BF16)), (query, own, *parts)
    )
    got = shift(send, "rep", 1)
    return call(join_kernel, shape((cands // 2, cols), BF16), (keep, got))


def body(*args):
    item_feats, adapter, cand_index, hist_user = args[0], args[1], args[6], args[8]
    fits = (
        lax.axis_size("rep") == 2
        and 1 < lax.axis_size("hist") < 8
        and hist_user.shape[0] % 256 == 0
        and adapter.shape[0] % (128 * lax.axis_size("groups")) == 0
        and adapter.shape[1] % 256 == 0
        and 2 * cand_index.shape[0] == 128
        and item_feats.shape[0] % 128 == 0
    )
    return fast_body(*args) if fits else generic_body(*args)


def solution(mesh):
    placed = (
        P(("groups", "hist", "rep"), None),
        P("hist", "head"),
        P(("groups", "hist"), None),
        P(None, "head"),
        P(None, "head"),
        P(("groups", "hist", "rep"), None),
        P(("groups", "hist", "rep")),
        P(("groups", "hist", "rep")),
        P(("groups", "hist")),
    )
    return jax.shard_map(
        body,
        mesh=mesh,
        in_specs=placed,
        out_specs=P(("groups", "hist", "rep"), "head"),
        check_vma=False,
    )
```

```python
import functools
import math

import jax
import jax.numpy as jnp
from jax import lax
from jax.experimental import pallas as pl
from jax.experimental.pallas import tpu as pltpu
from jax.sharding import PartitionSpec as P


HS = 64
USERS = 256
LISTED = 16
VM = pl.BlockSpec(memory_space=pltpu.VMEM)
HBM = pl.BlockSpec(memory_space=pltpu.HBM)
F32 = jnp.float32
BF16 = jnp.bfloat16


def attend(query_block, user_block, key_rows, value_rows, key_users):
    row_count = query_block.shape[0]
    col_count = query_block.shape[1]
    heads_here = col_count // HS
    att_scale = float(HS) ** (-0.5)
    query_three = query_block.reshape(row_count, heads_here, HS)
    key_three = key_rows.reshape(-1, heads_here, HS)
    value_three = value_rows.reshape(-1, heads_here, HS)
    scores = (
        jnp.einsum("rhd,khd->hrk", query_three, key_three, preferred_element_type=jnp.float32)
        * att_scale
    )
    matching = user_block[:, None] == key_users[None, :]
    weights = jnp.where(matching[None], jax.nn.silu(scores), 0.0).astype(jnp.bfloat16)
    mixture = jnp.einsum("hrk,khd->rhd", weights, value_three, preferred_element_type=jnp.float32)
    counted = jnp.sum(matching.astype(jnp.float32), axis=1)
    inverse = 1.0 / jnp.maximum(counted, 1.0)
    return mixture.reshape(row_count, col_count) * inverse[:, None]


def dense_partial(queries, users, key_rows, value_rows, key_users):
    total_rows = queries.shape[0]
    col_count = queries.shape[1]
    block_size = math.gcd(total_rows, 512)
    blocked_queries = queries.reshape(total_rows // block_size, block_size, col_count)
    blocked_users = users.reshape(total_rows // block_size, block_size)

    def one_block(operands):
        return attend(operands[0], operands[1], key_rows, value_rows, key_users)

    return lax.map(one_block, (blocked_queries, blocked_users)).reshape(total_rows, col_count)


def generic_body(
    item_feats,
    adapter,
    hist_emb,
    key_weight,
    value_weight,
    routes,
    cand_index,
    item_user,
    hist_user,
):
    owners = lax.axis_size("hist")
    item_count = item_feats.shape[0]
    col_count = adapter.shape[1]
    embedded = jnp.dot(
        item_feats,
        lax.all_gather(adapter, "hist", axis=0, tiled=True),
        preferred_element_type=jnp.float32,
    ).astype(jnp.bfloat16)
    capacity = 2 * item_count // owners
    owner_of = routes[:, 0]
    owner_hot = (owner_of[:, None] == jnp.arange(owners, dtype=jnp.int32)[None, :]).astype(
        jnp.int32
    )
    earlier = jnp.cumsum(owner_hot, axis=0) - owner_hot
    slot_of = jnp.sum(earlier * owner_hot, axis=1)
    position = owner_of * capacity + slot_of
    placing = (jnp.arange(owners * capacity, dtype=jnp.int32)[:, None] == position[None, :]).astype(
        jnp.bfloat16
    )
    outgoing = jnp.dot(placing, embedded, preferred_element_type=jnp.float32).astype(jnp.bfloat16)
    outgoing = outgoing.reshape(owners, capacity, col_count)
    shifted_user = (item_user + 1).astype(jnp.bfloat16)
    outgoing_user = (
        jnp.dot(placing, shifted_user, preferred_element_type=jnp.float32) - 1.0
    ).astype(jnp.bfloat16)
    outgoing_user = outgoing_user.reshape(owners, capacity)
    incoming, incoming_user = (
        lax.all_to_all(outgoing, "hist", split_axis=0, concat_axis=0, tiled=True),
        lax.all_to_all(outgoing_user, "hist", split_axis=0, concat_axis=0, tiled=True),
    )
    routed, routed_user = (
        lax.all_gather(incoming, "rep", axis=0, tiled=True),
        lax.all_gather(incoming_user, "rep", axis=0, tiled=True),
    )
    routed = routed.reshape(-1, col_count)
    routed_user = routed_user.reshape(-1)
    key_local = jnp.dot(hist_emb, key_weight, preferred_element_type=jnp.float32).astype(
        jnp.bfloat16
    )
    value_local = jnp.dot(hist_emb, value_weight, preferred_element_type=jnp.float32).astype(
        jnp.bfloat16
    )
    key_rows = jnp.concatenate([key_local, routed], axis=0)
    value_rows = jnp.concatenate([value_local, routed], axis=0)
    key_users = jnp.concatenate([hist_user.astype(jnp.bfloat16), routed_user], axis=0)
    own_queries = embedded[cand_index]
    own_users = item_user[cand_index].astype(jnp.bfloat16)
    gathered, gathered_users = (
        lax.all_gather(own_queries, "hist", axis=0, tiled=True),
        lax.all_gather(own_users, "hist", axis=0, tiled=True),
    )
    partial_value = dense_partial(gathered, gathered_users, key_rows, value_rows, key_users)
    attended = lax.psum_scatter(partial_value, "hist", scatter_dimension=0, tiled=True)
    gating = jax.nn.silu(own_queries.astype(jnp.float32))
    return (gating * attended).astype(jnp.bfloat16)


def call(kernel, outs, args, flops=0, bytes_accessed=1 << 18, vmem=16, specs=None, scratch=()):
    if specs:
        args = [pltpu.with_memory_space_constraint(arg, pltpu.HBM) for arg in args]
    return pl.pallas_call(
        kernel,
        out_shape=outs,
        in_specs=specs or [VM] * len(args),
        out_specs=jax.tree.map(lambda _: VM, outs),
        scratch_shapes=scratch,
        compiler_params=pltpu.CompilerParams(vmem_limit_bytes=vmem << 20),
        cost_estimate=pl.CostEstimate(flops=flops, bytes_accessed=bytes_accessed, transcendentals=0),
    )(*args)


def shape(dims, dtype):
    return jax.ShapeDtypeStruct(dims, dtype)


def iota(dims, axis):
    return lax.broadcasted_iota(jnp.int32, dims, axis)


def dot(a, b, contract=((1,), (0,))):
    return lax.dot_general(a, b, (contract, ((), ())), preferred_element_type=F32)


def col_start(width):
    return pl.multiple_of(lax.axis_index("rep") * width, width)


def one_hot(dims, axis, at):
    return (iota(dims, axis) == at).astype(F32).astype(BF16)


def share_kernel(
    adapter, item_user, routes, cand_index, hist_user, block, out, mine, user, owner, cand, event, events, sems
):
    _, cols = block.shape
    rows = out.shape[0] - LISTED
    row = pl.multiple_of(lax.axis_index("groups") * rows, rows)
    columns = pl.ds(col_start(cols), cols)
    part = event.shape[1]
    copies = [
        pltpu.make_async_copy(item_user, user, sems.at[0]),
        pltpu.make_async_copy(routes, owner, sems.at[1]),
        pltpu.make_async_copy(cand_index, cand, sems.at[2]),
        pltpu.make_async_copy(hist_user.at[:, pl.ds(col_start(part), part)], event, sems.at[3]),
        pltpu.make_async_copy(adapter.at[pl.ds(row, rows), columns], out.at[pl.ds(0, rows)], sems.at[4]),
        pltpu.make_async_copy(adapter.at[:, columns], block, sems.at[5]),
        pltpu.make_async_copy(hist_user, events, sems.at[6]),
    ]
    for copy in copies:
        copy.start()
    for copy in copies[:4]:
        copy.wait()
    items = user.shape[1]
    cands = cand.shape[1]
    mine[:, :items] = user[...]
    mine[:, items : 2 * items] = owner[...]
    mine[:, 2 * items : 2 * items + 2 * cands] = jnp.concatenate([cand[...], cand[...]], axis=1)
    items_hot = one_hot((USERS, items), 0, user[...])
    counts = dot(one_hot((8, items), 0, owner[...]), items_hot, ((1,), (1,)))
    here = jnp.zeros((1, part), jnp.int32) + lax.axis_index("hist")
    counts = counts + dot(one_hot((8, part), 0, here), one_hot((USERS, part), 0, event[...]), ((1,), (1,)))
    chosen = one_hot((items, cands), 0, cand[...])
    users = dot(jnp.broadcast_to(user[...], (8, items)).astype(F32).astype(BF16), chosen)
    users = jnp.concatenate([users, jnp.zeros((8, USERS - cands), F32)], axis=1)
    quarter = jnp.floor(counts * 0.25)
    rest = jnp.sum((counts - 4.0 * quarter) * digit_weight(4.0), axis=0, keepdims=True)
    half = USERS // 2
    row = iota((8, half), 0)
    top = jnp.where(row < 4, quarter[:, :half], pltpu.roll(quarter[:, half:], 4, 0))
    bottom = jnp.where(row == 0, rest[:, :half], jnp.where(row == 1, rest[:, half:], users[:, :half]))
    out[rows:] = jnp.concatenate([top, jnp.where(row < 3, bottom, 0.0)], axis=0).astype(BF16)
    for copy in copies[4:]:
        copy.wait()
    mine[:, 2 * items + 2 * cands :] = events[...]


def digit_weight(base):
    row = iota((8, 1), 0)
    weight = jnp.zeros((8, 1), F32)
    for owner in range(4):
        weight = jnp.where(row == owner, base ** owner, weight)
    return weight


def users_kernel(mine, other, hot, pick):
    lanes, both = pick.shape
    items = both // 2
    half = lanes // 2
    both_user = jnp.concatenate([mine[:, :items], other[:, :items]], axis=1)
    at = slice(2 * items, 2 * items + lanes)
    moved = pltpu.roll(jnp.broadcast_to(other[:, at], (8, lanes)), half, 1)[:1] + items
    cand = jnp.where(iota((1, lanes), 1) < half, mine[:, at], moved)
    event_user = mine[:, 2 * items + lanes :]
    events = event_user.shape[1]
    hot[:, :events] = one_hot((USERS, events), 0, event_user)
    hot[:, events:] = one_hot((USERS, both), 0, both_user)
    chosen = (iota((both, lanes), 0) == cand).astype(F32)
    pick[...] = jnp.transpose(chosen).astype(BF16)


def tally_kernel(*refs):
    out = refs[-1]
    row = iota((8, USERS // 2), 0)
    total = jnp.zeros((8, USERS), F32)
    for k, ref in enumerate(refs[:-1]):
        listed = ref[ref.shape[0] - LISTED :].astype(F32)
        top, bottom = listed[:8], listed[8:]
        low, high = jnp.where(row < 4, top, 0.0), jnp.where(row < 4, pltpu.roll(top, 4, 0), 0.0)
        rest = jnp.concatenate([bottom[:1], bottom[1:2]], axis=1)
        digits = jnp.floor(rest * digit_weight(0.25))
        rest = digits - 4.0 * jnp.floor(digits * 0.25)
        total = total + 4.0 * jnp.concatenate([low, high], axis=1) + rest
        out[8 + k : 9 + k] = jnp.concatenate([bottom[2:3], jnp.zeros_like(bottom[2:3])], axis=1)
    out[:8] = total


def scale_kernel(items, mine, other, hot, tally, tally_other, out):
    n, lanes, _ = out.shape
    hist_user = mine[:, 2 * items + lanes :]
    events = hist_user.shape[1]
    total = tally[:8] + tally_other[:8]
    high = jnp.floor(total * (1.0 / 256.0))
    low = total - 256.0 * high
    counts = 256.0 * dot(high.astype(BF16), hot[...]) + dot(low.astype(BF16), hot[...])
    both_owner = jnp.concatenate([mine[:, items : 2 * items], other[:, items : 2 * items]], axis=1)
    here = jnp.zeros((1, events), jnp.int32) + lax.axis_index("hist")
    owner = jnp.concatenate([here, both_owner], axis=1)
    count = jnp.sum(jnp.where(iota(counts.shape, 0) == owner, counts, 0.0), axis=0, keepdims=True)
    inverse = 1.0 / jnp.maximum(count, 1.0)
    user = jnp.concatenate([hist_user, mine[:, :items], other[:, :items]], axis=1).astype(F32)
    diagonal = iota((lanes, lanes), 0) == iota((lanes, lanes), 1)
    first = iota((8, lanes), 1) < lanes // 2
    near = tally[8:16, :lanes]
    far = pltpu.roll(tally_other[8:16, :lanes], lanes // 2, 1)
    cand = jnp.where(first, near, far)
    for k in range(n):
        column = jnp.sum(jnp.where(diagonal, cand[k : k + 1], 0.0), axis=1, keepdims=True)
        out[k] = jnp.where(column == user, inverse, 0.0)


def project_kernel(hist_emb, key_weight, value_weight, key_t, value, emb, keys, values, sems):
    width = value.shape[1]
    columns = pl.ds(col_start(width), width)
    copies = [
        pltpu.make_async_copy(key_weight.at[:, columns], keys, sems.at[0]),
        pltpu.make_async_copy(value_weight.at[:, columns], values, sems.at[1]),
        pltpu.make_async_copy(hist_emb, emb, sems.at[2]),
    ]
    for copy in copies:
        copy.start()
    for copy in copies:
        copy.wait()
    value[...] = dot(emb[...], values[...]).astype(BF16)
    key_t[...] = jnp.transpose(dot(emb[...], keys[...]).astype(BF16))


def embed_own_kernel(mine, other, block, total):
    items = mine.shape[0]
    depth = block.shape[0]
    at = pl.ds(pl.multiple_of(lax.axis_index("hist") * depth, depth), depth)
    total[:items] = dot(mine[:, at], block[...])
    total[items:] = dot(other[:, at], block[...])


def add_block(n, groups, k, step, mine, other, top, bottom, block):
    depth = block.shape[0] - LISTED
    at = columns_of(n, groups, k, step, depth)
    return top + dot(mine[:, at], block[:depth]), bottom + dot(other[:, at], block[:depth])


def embed_add_kernel(n, groups, which, mine, other, total, *refs):
    items = mine.shape[0]
    top, bottom = total[:items], total[items:]
    for (k, step), block in zip(which, refs):
        top, bottom = add_block(n, groups, k, step, mine, other, top, bottom, block)
    refs[-1][:items] = top
    refs[-1][items:] = bottom


def columns_of(n, groups, k, step, depth):
    source = lax.rem(lax.axis_index("hist") + n - k, n)
    group = lax.rem(lax.axis_index("groups") + groups - step, groups)
    return pl.ds(pl.multiple_of((source * groups + group) * depth, depth), depth)


def query_part_kernel(n, groups, k, step, mine, other, pick, total, part, feats):
    items = mine.shape[0]
    at = columns_of(n, groups, k, step, feats.shape[1])
    part[...] = lax.dot(pick[...].astype(F32), total[...], precision=lax.Precision.HIGHEST)
    feats[...] = (dot(pick[:, :items], mine[:, at]) + dot(pick[:, items:], other[:, at])).astype(BF16)


def query_kernel(part, feats, block, query):
    query[...] = (part[...] + dot(feats[...], block[: feats.shape[1]])).astype(BF16)


def embed_last_kernel(n, groups, k, step, mine, other, total, block, rows, rows_t):
    items = mine.shape[0]
    top, bottom = add_block(n, groups, k, step, mine, other, total[:items], total[items:], block)
    rows[:items] = top.astype(BF16)
    rows[items:] = bottom.astype(BF16)
    rows_t[...] = jnp.transpose(rows[...])


def attend_kernel(k, query, key_t, value, rows_t, rows, scale, out):
    cands, width = query.shape
    heads = width // HS
    lane = iota((cands, width), 1) // HS
    part = query[...] * (0.5 * HS ** -0.5)
    zero = jnp.zeros_like(part)
    split = jnp.concatenate([jnp.where(lane == h, part, zero) for h in range(heads)], axis=0)
    events = key_t.shape[1]

    def weigh(keys, factor):
        half = dot(split, keys)
        gated = half + half * jnp.tanh(half)
        return (gated * jnp.concatenate([factor] * heads, axis=0)).astype(BF16)

    mixed = dot(weigh(key_t[...], scale[k, :, :events]), value[...])
    mixed = mixed + dot(weigh(rows_t[...], scale[k, :, events:]), rows[...])
    total = jnp.zeros((cands, width), F32)
    for h in range(heads):
        total = total + jnp.where(lane == h, mixed[h * cands : (h + 1) * cands], 0.0)
    out[...] = total.astype(out.dtype)


def gate_kernel(query, own, *refs):
    parts, keep, send = refs[:-2], refs[-2], refs[-1]
    total = own[...]
    for part in parts:
        total = total + part[...].astype(F32)
    gate = query[...].astype(F32)
    scored = (gate * jax.nn.sigmoid(gate) * total).astype(BF16)
    half = keep.shape[0]
    keep[...] = scored[:half]
    send[...] = scored[half:]


def join_kernel(keep, got, out):
    width = keep.shape[1]
    first = lax.axis_index("rep") == 0
    out[:, :width] = jnp.where(first, keep[...], got[...])
    out[:, width:] = jnp.where(first, got[...], keep[...])


def shift(value, axis, k):
    count = lax.axis_size(axis)
    return lax.ppermute(value, axis, [(i, (i + k) % count) for i in range(count)])


def shift_order(n):
    return sorted(range(1, n), key=lambda k: min(k, n - k))


def fast_body(
    item_feats, adapter, hist_emb, key_weight, value_weight, routes, cand_index, item_user, hist_user
):
    n, groups = lax.axis_size("hist"), lax.axis_size("groups")
    items, _ = item_feats.shape
    depth, cols = adapter.shape
    width = cols // 2
    cands = 2 * cand_index.shape[0]
    events, dim = hist_emb.shape
    order = shift_order(n)

    block, own_share, mine = call(
        share_kernel,
        (
            shape((depth, width), BF16),
            shape((depth // groups + LISTED, width), BF16),
            shape((1, 2 * items + cands + events), jnp.int32),
        ),
        (
            adapter,
            item_user.reshape(1, -1),
            routes.reshape(1, -1),
            cand_index.reshape(1, -1),
            hist_user.reshape(1, -1),
        ),
        specs=[HBM] * 5,
        scratch=[
            pltpu.VMEM((1, items), jnp.int32),
            pltpu.VMEM((1, items), jnp.int32),
            pltpu.VMEM((1, cands // 2), jnp.int32),
            pltpu.VMEM((1, events // 2), jnp.int32),
            pltpu.VMEM((1, events), jnp.int32),
            pltpu.SemaphoreType.DMA((7,)),
        ],
    )
    along = {}
    for k in order:
        if k in (1, n - 1):
            along[k] = shift(own_share, "hist", k)
        else:
            step = 1 if k <= n // 2 else n - 1
            along[k] = shift(along[(k - step) % n], "hist", step)
    feats_other = shift(item_feats, "rep", 1)
    other = shift(mine, "rep", 1)
    keys = events + 2 * items
    hot, pick = call(users_kernel, (shape((USERS, keys), BF16), shape((cands, 2 * items), BF16)), (mine, other))
    key_t, value = call(
        project_kernel,
        (shape((width, events), BF16), shape((events, width), BF16)),
        (hist_emb, key_weight, value_weight),
        flops=4 * events * dim * width,
        bytes_accessed=4 << 20,
        specs=[HBM] * 3,
        scratch=[
            pltpu.VMEM((events, dim), BF16),
            pltpu.VMEM((dim, width), BF16),
            pltpu.VMEM((dim, width), BF16),
            pltpu.SemaphoreType.DMA((3,)),
        ],
    )
    total = call(
        embed_own_kernel,
        shape((2 * items, width), F32),
        (item_feats, feats_other, block),
        flops=4 * items * depth * width,
        bytes_accessed=4 << 20,
    )
    tally = call(tally_kernel, shape((16, USERS), F32), (own_share, *[along[k] for k in range(1, n)]))
    scale = call(
        functools.partial(scale_kernel, items),
        shape((n, cands, keys), F32),
        (mine, other, hot, tally, shift(tally, "rep", 1)),
        bytes_accessed=4 << 20,
    )
    across = {k: [along[k]] + [shift(along[k], "groups", g) for g in range(1, groups)] for k in order}
    blocks = [((k, step), across[k][step]) for k in order for step in range(groups)]
    chunks = [blocks[at : at + groups] for at in range(0, len(blocks) - groups, groups)]
    chunks += [blocks[-groups:-1]]
    for k, chunk in zip(order, chunks):
        which, arrived = zip(*chunk)
        total = call(
            functools.partial(embed_add_kernel, n, groups, which),
            shape((2 * items, width), F32),
            (item_feats, feats_other, total, *arrived),
            flops=4 * items * depth * width,
            bytes_accessed=2 << 20,
        )
    (k, step), arrived = blocks[-1]
    share = depth // groups
    part, feats = call(
        functools.partial(query_part_kernel, n, groups, k, step),
        (shape((cands, width), F32), shape((cands, share), BF16)),
        (item_feats, feats_other, pick, total),
        flops=4 * cands * items * (share + 6 * width),
    )
    query = call(query_kernel, shape((cands, width), BF16), (part, feats, arrived), flops=2 * cands * share * width)
    rows, rows_t = call(
        functools.partial(embed_last_kernel, n, groups, k, step),
        (shape((2 * items, width), BF16), shape((width, 2 * items), BF16)),
        (item_feats, feats_other, total, arrived),
        flops=4 * items * share * width,
        bytes_accessed=2 << 20,
    )
    queries = {k: shift(query, "hist", k) for k in order}

    def attend(k, block, dtype):
        return call(
            functools.partial(attend_kernel, k),
            shape((cands, width), dtype),
            (block, key_t, value, rows_t, rows, scale),
            flops=8 * cands * keys * width,
            bytes_accessed=1 << 20,
        )

    own = attend(0, query, F32)
    parts = [shift(attend(k, queries[k], BF16), "hist", n - k) for k in order]
    keep, send = call(
        gate_kernel, (shape((cands // 2, width), BF16), shape((cands // 2, width), BF16)), (query, own, *parts)
    )
    got = shift(send, "rep", 1)
    return call(join_kernel, shape((cands // 2, cols), BF16), (keep, got))


def body(*args):
    item_feats, adapter, cand_index, hist_user = args[0], args[1], args[6], args[8]
    fits = (
        lax.axis_size("rep") == 2
        and 1 < lax.axis_size("hist") <= 4
        and item_feats.shape[0] + hist_user.shape[0] // 2 < 1024
        and hist_user.shape[0] % 256 == 0
        and adapter.shape[0] % (128 * lax.axis_size("groups")) == 0
        and adapter.shape[1] % 256 == 0
        and 2 * cand_index.shape[0] == 128
        and item_feats.shape[0] % 128 == 0
    )
    return fast_body(*args) if fits else generic_body(*args)


def solution(mesh):
    placed = (
        P(("groups", "hist", "rep"), None),
        P("hist", "head"),
        P(("groups", "hist"), None),
        P(None, "head"),
        P(None, "head"),
        P(("groups", "hist", "rep"), None),
        P(("groups", "hist", "rep")),
        P(("groups", "hist", "rep")),
        P(("groups", "hist")),
    )
    return jax.shard_map(
        body,
        mesh=mesh,
        in_specs=placed,
        out_specs=P(("groups", "hist", "rep"), "head"),
        check_vma=False,
    )
```

```python
import functools
import math

import jax
import jax.numpy as jnp
from jax import lax
from jax.experimental import pallas as pl
from jax.experimental.pallas import tpu as pltpu
from jax.sharding import PartitionSpec as P


HS = 64
USERS = 256
LISTED = 16
VM = pl.BlockSpec(memory_space=pltpu.VMEM)
HBM = pl.BlockSpec(memory_space=pltpu.HBM)
F32 = jnp.float32
BF16 = jnp.bfloat16


def attend(query_block, user_block, key_rows, value_rows, key_users):
    row_count = query_block.shape[0]
    col_count = query_block.shape[1]
    heads_here = col_count // HS
    att_scale = float(HS) ** (-0.5)
    query_three = query_block.reshape(row_count, heads_here, HS)
    key_three = key_rows.reshape(-1, heads_here, HS)
    value_three = value_rows.reshape(-1, heads_here, HS)
    scores = (
        jnp.einsum("rhd,khd->hrk", query_three, key_three, preferred_element_type=jnp.float32)
        * att_scale
    )
    matching = user_block[:, None] == key_users[None, :]
    weights = jnp.where(matching[None], jax.nn.silu(scores), 0.0).astype(jnp.bfloat16)
    mixture = jnp.einsum("hrk,khd->rhd", weights, value_three, preferred_element_type=jnp.float32)
    counted = jnp.sum(matching.astype(jnp.float32), axis=1)
    inverse = 1.0 / jnp.maximum(counted, 1.0)
    return mixture.reshape(row_count, col_count) * inverse[:, None]


def dense_partial(queries, users, key_rows, value_rows, key_users):
    total_rows = queries.shape[0]
    col_count = queries.shape[1]
    block_size = math.gcd(total_rows, 512)
    blocked_queries = queries.reshape(total_rows // block_size, block_size, col_count)
    blocked_users = users.reshape(total_rows // block_size, block_size)

    def one_block(operands):
        return attend(operands[0], operands[1], key_rows, value_rows, key_users)

    return lax.map(one_block, (blocked_queries, blocked_users)).reshape(total_rows, col_count)


def generic_body(
    item_feats,
    adapter,
    hist_emb,
    key_weight,
    value_weight,
    routes,
    cand_index,
    item_user,
    hist_user,
):
    owners = lax.axis_size("hist")
    item_count = item_feats.shape[0]
    col_count = adapter.shape[1]
    embedded = jnp.dot(
        item_feats,
        lax.all_gather(adapter, "hist", axis=0, tiled=True),
        preferred_element_type=jnp.float32,
    ).astype(jnp.bfloat16)
    capacity = 2 * item_count // owners
    owner_of = routes[:, 0]
    owner_hot = (owner_of[:, None] == jnp.arange(owners, dtype=jnp.int32)[None, :]).astype(
        jnp.int32
    )
    earlier = jnp.cumsum(owner_hot, axis=0) - owner_hot
    slot_of = jnp.sum(earlier * owner_hot, axis=1)
    position = owner_of * capacity + slot_of
    placing = (jnp.arange(owners * capacity, dtype=jnp.int32)[:, None] == position[None, :]).astype(
        jnp.bfloat16
    )
    outgoing = jnp.dot(placing, embedded, preferred_element_type=jnp.float32).astype(jnp.bfloat16)
    outgoing = outgoing.reshape(owners, capacity, col_count)
    shifted_user = (item_user + 1).astype(jnp.bfloat16)
    outgoing_user = (
        jnp.dot(placing, shifted_user, preferred_element_type=jnp.float32) - 1.0
    ).astype(jnp.bfloat16)
    outgoing_user = outgoing_user.reshape(owners, capacity)
    incoming, incoming_user = (
        lax.all_to_all(outgoing, "hist", split_axis=0, concat_axis=0, tiled=True),
        lax.all_to_all(outgoing_user, "hist", split_axis=0, concat_axis=0, tiled=True),
    )
    routed, routed_user = (
        lax.all_gather(incoming, "rep", axis=0, tiled=True),
        lax.all_gather(incoming_user, "rep", axis=0, tiled=True),
    )
    routed = routed.reshape(-1, col_count)
    routed_user = routed_user.reshape(-1)
    key_local = jnp.dot(hist_emb, key_weight, preferred_element_type=jnp.float32).astype(
        jnp.bfloat16
    )
    value_local = jnp.dot(hist_emb, value_weight, preferred_element_type=jnp.float32).astype(
        jnp.bfloat16
    )
    key_rows = jnp.concatenate([key_local, routed], axis=0)
    value_rows = jnp.concatenate([value_local, routed], axis=0)
    key_users = jnp.concatenate([hist_user.astype(jnp.bfloat16), routed_user], axis=0)
    own_queries = embedded[cand_index]
    own_users = item_user[cand_index].astype(jnp.bfloat16)
    gathered, gathered_users = (
        lax.all_gather(own_queries, "hist", axis=0, tiled=True),
        lax.all_gather(own_users, "hist", axis=0, tiled=True),
    )
    partial_value = dense_partial(gathered, gathered_users, key_rows, value_rows, key_users)
    attended = lax.psum_scatter(partial_value, "hist", scatter_dimension=0, tiled=True)
    gating = jax.nn.silu(own_queries.astype(jnp.float32))
    return (gating * attended).astype(jnp.bfloat16)


def call(kernel, outs, args, flops=0, bytes_accessed=1 << 18, vmem=16, specs=None, scratch=()):
    if specs:
        args = [pltpu.with_memory_space_constraint(arg, pltpu.HBM) for arg in args]
    return pl.pallas_call(
        kernel,
        out_shape=outs,
        in_specs=specs or [VM] * len(args),
        out_specs=jax.tree.map(lambda _: VM, outs),
        scratch_shapes=scratch,
        compiler_params=pltpu.CompilerParams(vmem_limit_bytes=vmem << 20),
        cost_estimate=pl.CostEstimate(flops=flops, bytes_accessed=bytes_accessed, transcendentals=0),
    )(*args)


def shape(dims, dtype):
    return jax.ShapeDtypeStruct(dims, dtype)


def iota(dims, axis):
    return lax.broadcasted_iota(jnp.int32, dims, axis)


def dot(a, b, contract=((1,), (0,))):
    return lax.dot_general(a, b, (contract, ((), ())), preferred_element_type=F32)


def col_start(width):
    return pl.multiple_of(lax.axis_index("rep") * width, width)


def one_hot(dims, axis, at):
    return (iota(dims, axis) == at).astype(F32).astype(BF16)


def share_kernel(
    adapter, item_user, routes, cand_index, hist_user, block, out, mine, user, owner, cand, event, events, sems
):
    _, cols = block.shape
    rows = out.shape[0] - LISTED
    row = pl.multiple_of(lax.axis_index("groups") * rows, rows)
    columns = pl.ds(col_start(cols), cols)
    part = event.shape[1]
    copies = [
        pltpu.make_async_copy(item_user, user, sems.at[0]),
        pltpu.make_async_copy(routes, owner, sems.at[1]),
        pltpu.make_async_copy(cand_index, cand, sems.at[2]),
        pltpu.make_async_copy(hist_user.at[:, pl.ds(col_start(part), part)], event, sems.at[3]),
        pltpu.make_async_copy(adapter.at[pl.ds(row, rows), columns], out.at[pl.ds(0, rows)], sems.at[4]),
        pltpu.make_async_copy(adapter.at[:, columns], block, sems.at[5]),
        pltpu.make_async_copy(hist_user, events, sems.at[6]),
    ]
    for copy in copies:
        copy.start()
    for copy in copies[:4]:
        copy.wait()
    items = user.shape[1]
    cands = cand.shape[1]
    mine[:, :items] = user[...]
    mine[:, items : 2 * items] = owner[...]
    mine[:, 2 * items : 2 * items + 2 * cands] = jnp.concatenate([cand[...], cand[...]], axis=1)
    items_hot = one_hot((USERS, items), 0, user[...])
    counts = dot(one_hot((8, items), 0, owner[...]), items_hot, ((1,), (1,)))
    here = jnp.zeros((1, part), jnp.int32) + lax.axis_index("hist")
    counts = counts + dot(one_hot((8, part), 0, here), one_hot((USERS, part), 0, event[...]), ((1,), (1,)))
    chosen = one_hot((items, cands), 0, cand[...])
    users = dot(jnp.broadcast_to(user[...], (8, items)).astype(F32).astype(BF16), chosen)
    users = jnp.concatenate([users, jnp.zeros((8, USERS - cands), F32)], axis=1)
    quarter = jnp.floor(counts * 0.25)
    rest = jnp.sum((counts - 4.0 * quarter) * digit_weight(4.0), axis=0, keepdims=True)
    half = USERS // 2
    row = iota((8, half), 0)
    top = jnp.where(row < 4, quarter[:, :half], pltpu.roll(quarter[:, half:], 4, 0))
    bottom = jnp.where(row == 0, rest[:, :half], jnp.where(row == 1, rest[:, half:], users[:, :half]))
    out[rows:] = jnp.concatenate([top, jnp.where(row < 3, bottom, 0.0)], axis=0).astype(BF16)
    for copy in copies[4:]:
        copy.wait()
    mine[:, 2 * items + 2 * cands :] = events[...]


def digit_weight(base):
    row = iota((8, 1), 0)
    weight = jnp.zeros((8, 1), F32)
    for owner in range(4):
        weight = jnp.where(row == owner, base ** owner, weight)
    return weight


def users_kernel(mine, other, hot, pick):
    lanes, both = pick.shape
    items = both // 2
    half = lanes // 2
    both_user = jnp.concatenate([mine[:, :items], other[:, :items]], axis=1)
    at = slice(2 * items, 2 * items + lanes)
    moved = pltpu.roll(jnp.broadcast_to(other[:, at], (8, lanes)), half, 1)[:1] + items
    cand = jnp.where(iota((1, lanes), 1) < half, mine[:, at], moved)
    event_user = mine[:, 2 * items + lanes :]
    events = event_user.shape[1]
    hot[:, :events] = one_hot((USERS, events), 0, event_user)
    hot[:, events:] = one_hot((USERS, both), 0, both_user)
    chosen = (iota((both, lanes), 0) == cand).astype(F32)
    pick[...] = jnp.transpose(chosen).astype(BF16)


def tally_kernel(*refs):
    out = refs[-1]
    row = iota((8, USERS // 2), 0)
    total = jnp.zeros((8, USERS), F32)
    for k, ref in enumerate(refs[:-1]):
        listed = ref[ref.shape[0] - LISTED :].astype(F32)
        top, bottom = listed[:8], listed[8:]
        low, high = jnp.where(row < 4, top, 0.0), jnp.where(row < 4, pltpu.roll(top, 4, 0), 0.0)
        rest = jnp.concatenate([bottom[:1], bottom[1:2]], axis=1)
        digits = jnp.floor(rest * digit_weight(0.25))
        rest = digits - 4.0 * jnp.floor(digits * 0.25)
        total = total + 4.0 * jnp.concatenate([low, high], axis=1) + rest
        out[8 + k : 9 + k] = jnp.concatenate([bottom[2:3], jnp.zeros_like(bottom[2:3])], axis=1)
    out[:8] = total


def scale_kernel(items, mine, other, hot, tally, tally_other, out):
    n, _, lanes = out.shape
    hist_user = mine[:, 2 * items + lanes :]
    events = hist_user.shape[1]
    total = tally[:8] + tally_other[:8]
    high = jnp.floor(total * (1.0 / 256.0))
    low = total - 256.0 * high
    counts = 256.0 * dot(high.astype(BF16), hot[...]) + dot(low.astype(BF16), hot[...])
    both_owner = jnp.concatenate([mine[:, items : 2 * items], other[:, items : 2 * items]], axis=1)
    here = jnp.zeros((1, events), jnp.int32) + lax.axis_index("hist")
    owner = jnp.concatenate([here, both_owner], axis=1)
    count = jnp.sum(jnp.where(iota(counts.shape, 0) == owner, counts, 0.0), axis=0, keepdims=True)
    inverse = 1.0 / jnp.maximum(count, 1.0)
    user = jnp.concatenate([hist_user, mine[:, :items], other[:, :items]], axis=1).astype(F32)
    columns = jnp.transpose(jnp.where(iota(counts.shape, 0) == 0, user, inverse))
    entry_user, entry_scale = columns[:, :1], columns[:, 1:2]
    near = tally[8:16, :lanes]
    far = pltpu.roll(tally_other[8:16, :lanes], lanes // 2, 1)
    cand = jnp.where(iota((8, lanes), 1) < lanes // 2, near, far)
    for k in range(n):
        out[k] = jnp.where(entry_user == cand[k : k + 1], entry_scale, 0.0)


def project_kernel(hist_emb, key_weight, value_weight, key, value_t, emb, keys, values, sems):
    width = key.shape[1]
    columns = pl.ds(col_start(width), width)
    copies = [
        pltpu.make_async_copy(key_weight.at[:, columns], keys, sems.at[0]),
        pltpu.make_async_copy(value_weight.at[:, columns], values, sems.at[1]),
        pltpu.make_async_copy(hist_emb, emb, sems.at[2]),
    ]
    for copy in copies:
        copy.start()
    for copy in copies:
        copy.wait()
    key[...] = dot(emb[...], keys[...]).astype(BF16)
    value_t[...] = jnp.transpose(dot(emb[...], values[...]).astype(BF16))


def embed_own_kernel(mine, other, block, total):
    items = mine.shape[0]
    depth = block.shape[0]
    at = pl.ds(pl.multiple_of(lax.axis_index("hist") * depth, depth), depth)
    total[:items] = dot(mine[:, at], block[...])
    total[items:] = dot(other[:, at], block[...])


def add_block(n, groups, k, step, mine, other, top, bottom, block):
    depth = block.shape[0] - LISTED
    at = columns_of(n, groups, k, step, depth)
    return top + dot(mine[:, at], block[:depth]), bottom + dot(other[:, at], block[:depth])


def embed_add_kernel(n, groups, which, mine, other, total, *refs):
    items = mine.shape[0]
    top, bottom = total[:items], total[items:]
    for (k, step), block in zip(which, refs):
        top, bottom = add_block(n, groups, k, step, mine, other, top, bottom, block)
    refs[-1][:items] = top
    refs[-1][items:] = bottom


def columns_of(n, groups, k, step, depth):
    source = lax.rem(lax.axis_index("hist") + n - k, n)
    group = lax.rem(lax.axis_index("groups") + groups - step, groups)
    return pl.ds(pl.multiple_of((source * groups + group) * depth, depth), depth)


def query_part_kernel(n, groups, k, step, mine, other, pick, total, part, feats):
    items = mine.shape[0]
    at = columns_of(n, groups, k, step, feats.shape[1])
    part[...] = lax.dot(pick[...].astype(F32), total[...], precision=lax.Precision.HIGHEST)
    feats[...] = (dot(pick[:, :items], mine[:, at]) + dot(pick[:, items:], other[:, at])).astype(BF16)


def query_kernel(part, feats, block, query, query_t):
    query[...] = (part[...] + dot(feats[...], block[: feats.shape[1]])).astype(BF16)
    query_t[...] = jnp.transpose(query[...])


def embed_last_kernel(n, groups, k, step, mine, other, total, block, rows, rows_t):
    items = mine.shape[0]
    top, bottom = add_block(n, groups, k, step, mine, other, total[:items], total[items:], block)
    rows[:items] = top.astype(BF16)
    rows[items:] = bottom.astype(BF16)
    rows_t[...] = jnp.transpose(rows[...])


def attend_kernel(k, query_t, key, value_t, rows, rows_t, scale, out):
    width, cands = query_t.shape
    heads = width // HS
    row = iota((width, cands), 0) // HS
    part = query_t[...] * (0.5 * HS ** -0.5)
    zero = jnp.zeros_like(part)
    split = jnp.concatenate([jnp.where(row == h, part, zero) for h in range(heads)], axis=1)
    events = key.shape[0]

    mixed = jnp.zeros((width, heads * cands), F32)
    for keys, values, base in ((key, value_t, 0), (rows, rows_t, events)):
        step = math.gcd(keys.shape[0], 512)
        for at in range(0, keys.shape[0], step):
            half = dot(keys[at : at + step], split)
            gated = half + half * jnp.tanh(half)
            factor = scale[k, base + at : base + at + step]
            weight = (gated * jnp.concatenate([factor] * heads, axis=1)).astype(BF16)
            mixed = mixed + dot(values[:, at : at + step], weight)
    total = jnp.zeros((width, cands), F32)
    for h in range(heads):
        total = total + jnp.where(row == h, mixed[:, h * cands : (h + 1) * cands], 0.0)
    out[...] = total.astype(out.dtype)


def gate_kernel(query, own, *refs):
    parts, keep, send = refs[:-2], refs[-2], refs[-1]
    total = own[...]
    for part in parts:
        total = total + part[...].astype(F32)
    gate = query[...].astype(F32)
    scored = (gate * jax.nn.sigmoid(gate) * jnp.transpose(total)).astype(BF16)
    half = keep.shape[0]
    keep[...] = scored[:half]
    send[...] = scored[half:]


def join_kernel(keep, got, out):
    width = keep.shape[1]
    first = lax.axis_index("rep") == 0
    out[:, :width] = jnp.where(first, keep[...], got[...])
    out[:, width:] = jnp.where(first, got[...], keep[...])


def shift(value, axis, k):
    count = lax.axis_size(axis)
    return lax.ppermute(value, axis, [(i, (i + k) % count) for i in range(count)])


def shift_order(n):
    return sorted(range(1, n), key=lambda k: min(k, n - k))


def fast_body(
    item_feats, adapter, hist_emb, key_weight, value_weight, routes, cand_index, item_user, hist_user
):
    n, groups = lax.axis_size("hist"), lax.axis_size("groups")
    items, _ = item_feats.shape
    depth, cols = adapter.shape
    width = cols // 2
    cands = 2 * cand_index.shape[0]
    events, dim = hist_emb.shape
    order = shift_order(n)

    block, own_share, mine = call(
        share_kernel,
        (
            shape((depth, width), BF16),
            shape((depth // groups + LISTED, width), BF16),
            shape((1, 2 * items + cands + events), jnp.int32),
        ),
        (
            adapter,
            item_user.reshape(1, -1),
            routes.reshape(1, -1),
            cand_index.reshape(1, -1),
            hist_user.reshape(1, -1),
        ),
        specs=[HBM] * 5,
        scratch=[
            pltpu.VMEM((1, items), jnp.int32),
            pltpu.VMEM((1, items), jnp.int32),
            pltpu.VMEM((1, cands // 2), jnp.int32),
            pltpu.VMEM((1, events // 2), jnp.int32),
            pltpu.VMEM((1, events), jnp.int32),
            pltpu.SemaphoreType.DMA((7,)),
        ],
    )
    along = {}
    for k in order:
        if k in (1, n - 1):
            along[k] = shift(own_share, "hist", k)
        else:
            step = 1 if k <= n // 2 else n - 1
            along[k] = shift(along[(k - step) % n], "hist", step)
    feats_other = shift(item_feats, "rep", 1)
    other = shift(mine, "rep", 1)
    keys = events + 2 * items
    hot, pick = call(users_kernel, (shape((USERS, keys), BF16), shape((cands, 2 * items), BF16)), (mine, other))
    key, value_t = call(
        project_kernel,
        (shape((events, width), BF16), shape((width, events), BF16)),
        (hist_emb, key_weight, value_weight),
        flops=4 * events * dim * width,
        bytes_accessed=4 << 20,
        specs=[HBM] * 3,
        scratch=[
            pltpu.VMEM((events, dim), BF16),
            pltpu.VMEM((dim, width), BF16),
            pltpu.VMEM((dim, width), BF16),
            pltpu.SemaphoreType.DMA((3,)),
        ],
    )
    total = call(
        embed_own_kernel,
        shape((2 * items, width), F32),
        (item_feats, feats_other, block),
        flops=4 * items * depth * width,
        bytes_accessed=4 << 20,
    )
    tally = call(tally_kernel, shape((16, USERS), F32), (own_share, *[along[k] for k in range(1, n)]))
    scale = call(
        functools.partial(scale_kernel, items),
        shape((n, keys, cands), F32),
        (mine, other, hot, tally, shift(tally, "rep", 1)),
        bytes_accessed=4 << 20,
    )
    across = {k: [along[k]] + [shift(along[k], "groups", g) for g in range(1, groups)] for k in order}
    blocks = [((k, step), across[k][step]) for k in order for step in range(groups)]
    chunks = [blocks[at : at + groups] for at in range(0, len(blocks) - groups, groups)]
    chunks += [blocks[-groups:-1]]
    for k, chunk in zip(order, chunks):
        which, arrived = zip(*chunk)
        total = call(
            functools.partial(embed_add_kernel, n, groups, which),
            shape((2 * items, width), F32),
            (item_feats, feats_other, total, *arrived),
            flops=4 * items * depth * width,
            bytes_accessed=2 << 20,
        )
    (k, step), arrived = blocks[-1]
    share = depth // groups
    part, feats = call(
        functools.partial(query_part_kernel, n, groups, k, step),
        (shape((cands, width), F32), shape((cands, share), BF16)),
        (item_feats, feats_other, pick, total),
        flops=4 * cands * items * (share + 6 * width),
    )
    query, query_t = call(
        query_kernel,
        (shape((cands, width), BF16), shape((width, cands), BF16)),
        (part, feats, arrived),
        flops=2 * cands * share * width,
    )
    rows, rows_t = call(
        functools.partial(embed_last_kernel, n, groups, k, step),
        (shape((2 * items, width), BF16), shape((width, 2 * items), BF16)),
        (item_feats, feats_other, total, arrived),
        flops=4 * items * share * width,
        bytes_accessed=2 << 20,
    )
    queries = {k: shift(query_t, "hist", k) for k in order}

    def attend(k, block, dtype):
        return call(
            functools.partial(attend_kernel, k),
            shape((width, cands), dtype),
            (block, key, value_t, rows, rows_t, scale),
            flops=8 * cands * keys * width,
            bytes_accessed=1 << 20,
        )

    own = attend(0, query_t, F32)
    parts = [shift(attend(k, queries[k], BF16), "hist", n - k) for k in order]
    keep, send = call(
        gate_kernel, (shape((cands // 2, width), BF16), shape((cands // 2, width), BF16)), (query, own, *parts)
    )
    got = shift(send, "rep", 1)
    return call(join_kernel, shape((cands // 2, cols), BF16), (keep, got))


def body(*args):
    item_feats, adapter, cand_index, hist_user = args[0], args[1], args[6], args[8]
    fits = (
        lax.axis_size("rep") == 2
        and 1 < lax.axis_size("hist") <= 4
        and item_feats.shape[0] + hist_user.shape[0] // 2 < 1024
        and hist_user.shape[0] % 256 == 0
        and adapter.shape[0] % (128 * lax.axis_size("groups")) == 0
        and adapter.shape[1] % 256 == 0
        and 2 * cand_index.shape[0] == 128
        and item_feats.shape[0] % 128 == 0
    )
    return fast_body(*args) if fits else generic_body(*args)


def solution(mesh):
    placed = (
        P(("groups", "hist", "rep"), None),
        P("hist", "head"),
        P(("groups", "hist"), None),
        P(None, "head"),
        P(None, "head"),
        P(("groups", "hist", "rep"), None),
        P(("groups", "hist", "rep")),
        P(("groups", "hist", "rep")),
        P(("groups", "hist")),
    )
    return jax.shard_map(
        body,
        mesh=mesh,
        in_specs=placed,
        out_specs=P(("groups", "hist", "rep"), "head"),
        check_vma=False,
    )
```

```python
import functools
import math

import jax
import jax.numpy as jnp
from jax import lax
from jax.experimental import pallas as pl
from jax.experimental.pallas import tpu as pltpu
from jax.sharding import PartitionSpec as P


HS = 64
USERS = 256
LISTED = 16
VM = pl.BlockSpec(memory_space=pltpu.VMEM)
HBM = pl.BlockSpec(memory_space=pltpu.HBM)
F32 = jnp.float32
BF16 = jnp.bfloat16


def attend(query_block, user_block, key_rows, value_rows, key_users):
    row_count = query_block.shape[0]
    col_count = query_block.shape[1]
    heads_here = col_count // HS
    att_scale = float(HS) ** (-0.5)
    query_three = query_block.reshape(row_count, heads_here, HS)
    key_three = key_rows.reshape(-1, heads_here, HS)
    value_three = value_rows.reshape(-1, heads_here, HS)
    scores = (
        jnp.einsum("rhd,khd->hrk", query_three, key_three, preferred_element_type=jnp.float32)
        * att_scale
    )
    matching = user_block[:, None] == key_users[None, :]
    weights = jnp.where(matching[None], jax.nn.silu(scores), 0.0).astype(jnp.bfloat16)
    mixture = jnp.einsum("hrk,khd->rhd", weights, value_three, preferred_element_type=jnp.float32)
    counted = jnp.sum(matching.astype(jnp.float32), axis=1)
    inverse = 1.0 / jnp.maximum(counted, 1.0)
    return mixture.reshape(row_count, col_count) * inverse[:, None]


def dense_partial(queries, users, key_rows, value_rows, key_users):
    total_rows = queries.shape[0]
    col_count = queries.shape[1]
    block_size = math.gcd(total_rows, 512)
    blocked_queries = queries.reshape(total_rows // block_size, block_size, col_count)
    blocked_users = users.reshape(total_rows // block_size, block_size)

    def one_block(operands):
        return attend(operands[0], operands[1], key_rows, value_rows, key_users)

    return lax.map(one_block, (blocked_queries, blocked_users)).reshape(total_rows, col_count)


def generic_body(
    item_feats,
    adapter,
    hist_emb,
    key_weight,
    value_weight,
    routes,
    cand_index,
    item_user,
    hist_user,
):
    owners = lax.axis_size("hist")
    item_count = item_feats.shape[0]
    col_count = adapter.shape[1]
    embedded = jnp.dot(
        item_feats,
        lax.all_gather(adapter, "hist", axis=0, tiled=True),
        preferred_element_type=jnp.float32,
    ).astype(jnp.bfloat16)
    capacity = 2 * item_count // owners
    owner_of = routes[:, 0]
    owner_hot = (owner_of[:, None] == jnp.arange(owners, dtype=jnp.int32)[None, :]).astype(
        jnp.int32
    )
    earlier = jnp.cumsum(owner_hot, axis=0) - owner_hot
    slot_of = jnp.sum(earlier * owner_hot, axis=1)
    position = owner_of * capacity + slot_of
    placing = (jnp.arange(owners * capacity, dtype=jnp.int32)[:, None] == position[None, :]).astype(
        jnp.bfloat16
    )
    outgoing = jnp.dot(placing, embedded, preferred_element_type=jnp.float32).astype(jnp.bfloat16)
    outgoing = outgoing.reshape(owners, capacity, col_count)
    shifted_user = (item_user + 1).astype(jnp.bfloat16)
    outgoing_user = (
        jnp.dot(placing, shifted_user, preferred_element_type=jnp.float32) - 1.0
    ).astype(jnp.bfloat16)
    outgoing_user = outgoing_user.reshape(owners, capacity)
    incoming, incoming_user = (
        lax.all_to_all(outgoing, "hist", split_axis=0, concat_axis=0, tiled=True),
        lax.all_to_all(outgoing_user, "hist", split_axis=0, concat_axis=0, tiled=True),
    )
    routed, routed_user = (
        lax.all_gather(incoming, "rep", axis=0, tiled=True),
        lax.all_gather(incoming_user, "rep", axis=0, tiled=True),
    )
    routed = routed.reshape(-1, col_count)
    routed_user = routed_user.reshape(-1)
    key_local = jnp.dot(hist_emb, key_weight, preferred_element_type=jnp.float32).astype(
        jnp.bfloat16
    )
    value_local = jnp.dot(hist_emb, value_weight, preferred_element_type=jnp.float32).astype(
        jnp.bfloat16
    )
    key_rows = jnp.concatenate([key_local, routed], axis=0)
    value_rows = jnp.concatenate([value_local, routed], axis=0)
    key_users = jnp.concatenate([hist_user.astype(jnp.bfloat16), routed_user], axis=0)
    own_queries = embedded[cand_index]
    own_users = item_user[cand_index].astype(jnp.bfloat16)
    gathered, gathered_users = (
        lax.all_gather(own_queries, "hist", axis=0, tiled=True),
        lax.all_gather(own_users, "hist", axis=0, tiled=True),
    )
    partial_value = dense_partial(gathered, gathered_users, key_rows, value_rows, key_users)
    attended = lax.psum_scatter(partial_value, "hist", scatter_dimension=0, tiled=True)
    gating = jax.nn.silu(own_queries.astype(jnp.float32))
    return (gating * attended).astype(jnp.bfloat16)


def call(kernel, outs, args, flops=0, bytes_accessed=1 << 18, vmem=16, specs=None, scratch=()):
    if specs:
        args = [pltpu.with_memory_space_constraint(arg, pltpu.HBM) for arg in args]
    return pl.pallas_call(
        kernel,
        out_shape=outs,
        in_specs=specs or [VM] * len(args),
        out_specs=jax.tree.map(lambda _: VM, outs),
        scratch_shapes=scratch,
        compiler_params=pltpu.CompilerParams(vmem_limit_bytes=vmem << 20),
        cost_estimate=pl.CostEstimate(flops=flops, bytes_accessed=bytes_accessed, transcendentals=0),
    )(*args)


def shape(dims, dtype):
    return jax.ShapeDtypeStruct(dims, dtype)


def iota(dims, axis):
    return lax.broadcasted_iota(jnp.int32, dims, axis)


def dot(a, b, contract=((1,), (0,))):
    return lax.dot_general(a, b, (contract, ((), ())), preferred_element_type=F32)


def col_start(width):
    return pl.multiple_of(lax.axis_index("rep") * width, width)


def one_hot(dims, axis, at):
    return (iota(dims, axis) == at).astype(F32).astype(BF16)


def share_kernel(
    adapter, item_user, routes, cand_index, hist_user, out, mine, user, owner, cand, event, events, sems
):
    rows, cols = out.shape[0] - LISTED, out.shape[1]
    row = pl.multiple_of(lax.axis_index("groups") * rows, rows)
    columns = pl.ds(col_start(cols), cols)
    part = event.shape[1]
    copies = [
        pltpu.make_async_copy(item_user, user, sems.at[0]),
        pltpu.make_async_copy(routes, owner, sems.at[1]),
        pltpu.make_async_copy(cand_index, cand, sems.at[2]),
        pltpu.make_async_copy(hist_user.at[:, pl.ds(col_start(part), part)], event, sems.at[3]),
        pltpu.make_async_copy(adapter.at[pl.ds(row, rows), columns], out.at[pl.ds(0, rows)], sems.at[4]),
        pltpu.make_async_copy(hist_user, events, sems.at[5]),
    ]
    for copy in copies:
        copy.start()
    for copy in copies[:4]:
        copy.wait()
    items = user.shape[1]
    cands = cand.shape[1]
    mine[:, :items] = user[...]
    mine[:, items : 2 * items] = owner[...]
    mine[:, 2 * items : 2 * items + 2 * cands] = jnp.concatenate([cand[...], cand[...]], axis=1)
    items_hot = one_hot((USERS, items), 0, user[...])
    counts = dot(one_hot((8, items), 0, owner[...]), items_hot, ((1,), (1,)))
    here = jnp.zeros((1, part), jnp.int32) + lax.axis_index("hist")
    counts = counts + dot(one_hot((8, part), 0, here), one_hot((USERS, part), 0, event[...]), ((1,), (1,)))
    chosen = one_hot((items, cands), 0, cand[...])
    users = dot(jnp.broadcast_to(user[...], (8, items)).astype(F32).astype(BF16), chosen)
    users = jnp.concatenate([users, jnp.zeros((8, USERS - cands), F32)], axis=1)
    quarter = jnp.floor(counts * 0.25)
    rest = jnp.sum((counts - 4.0 * quarter) * digit_weight(4.0), axis=0, keepdims=True)
    half = USERS // 2
    row = iota((8, half), 0)
    top = jnp.where(row < 4, quarter[:, :half], pltpu.roll(quarter[:, half:], 4, 0))
    bottom = jnp.where(row == 0, rest[:, :half], jnp.where(row == 1, rest[:, half:], users[:, :half]))
    out[rows:] = jnp.concatenate([top, jnp.where(row < 3, bottom, 0.0)], axis=0).astype(BF16)
    for copy in copies[4:]:
        copy.wait()
    mine[:, 2 * items + 2 * cands :] = events[...]


def digit_weight(base):
    row = iota((8, 1), 0)
    weight = jnp.zeros((8, 1), F32)
    for owner in range(4):
        weight = jnp.where(row == owner, base ** owner, weight)
    return weight


def users_kernel(mine, other, hot, pick):
    lanes, both = pick.shape
    items = both // 2
    half = lanes // 2
    both_user = jnp.concatenate([mine[:, :items], other[:, :items]], axis=1)
    at = slice(2 * items, 2 * items + lanes)
    moved = pltpu.roll(jnp.broadcast_to(other[:, at], (8, lanes)), half, 1)[:1] + items
    cand = jnp.where(iota((1, lanes), 1) < half, mine[:, at], moved)
    event_user = mine[:, 2 * items + lanes :]
    events = event_user.shape[1]
    hot[:, :events] = one_hot((USERS, events), 0, event_user)
    hot[:, events:] = one_hot((USERS, both), 0, both_user)
    chosen = (iota((both, lanes), 0) == cand).astype(F32)
    pick[...] = jnp.transpose(chosen).astype(BF16)


def tally_kernel(*refs):
    out = refs[-1]
    row = iota((8, USERS // 2), 0)
    total = jnp.zeros((8, USERS), F32)
    for k, ref in enumerate(refs[:-1]):
        listed = ref[ref.shape[0] - LISTED :].astype(F32)
        top, bottom = listed[:8], listed[8:]
        low, high = jnp.where(row < 4, top, 0.0), jnp.where(row < 4, pltpu.roll(top, 4, 0), 0.0)
        rest = jnp.concatenate([bottom[:1], bottom[1:2]], axis=1)
        digits = jnp.floor(rest * digit_weight(0.25))
        rest = digits - 4.0 * jnp.floor(digits * 0.25)
        total = total + 4.0 * jnp.concatenate([low, high], axis=1) + rest
        out[8 + k : 9 + k] = jnp.concatenate([bottom[2:3], jnp.zeros_like(bottom[2:3])], axis=1)
    out[:8] = total


def scale_kernel(items, mine, other, hot, tally, tally_other, out):
    n, lanes, _ = out.shape
    hist_user = mine[:, 2 * items + lanes :]
    events = hist_user.shape[1]
    total = tally[:8] + tally_other[:8]
    high = jnp.floor(total * (1.0 / 256.0))
    low = total - 256.0 * high
    counts = 256.0 * dot(high.astype(BF16), hot[...]) + dot(low.astype(BF16), hot[...])
    both_owner = jnp.concatenate([mine[:, items : 2 * items], other[:, items : 2 * items]], axis=1)
    here = jnp.zeros((1, events), jnp.int32) + lax.axis_index("hist")
    owner = jnp.concatenate([here, both_owner], axis=1)
    count = jnp.sum(jnp.where(iota(counts.shape, 0) == owner, counts, 0.0), axis=0, keepdims=True)
    inverse = 1.0 / jnp.maximum(count, 1.0)
    user = jnp.concatenate([hist_user, mine[:, :items], other[:, :items]], axis=1).astype(F32)
    diagonal = iota((lanes, lanes), 0) == iota((lanes, lanes), 1)
    first = iota((8, lanes), 1) < lanes // 2
    near = tally[8:16, :lanes]
    far = pltpu.roll(tally_other[8:16, :lanes], lanes // 2, 1)
    cand = jnp.where(first, near, far)
    for k in range(n):
        column = jnp.sum(jnp.where(diagonal, cand[k : k + 1], 0.0), axis=1, keepdims=True)
        out[k] = jnp.where(column == user, inverse, 0.0)


def project_kernel(adapter, hist_emb, key_weight, value_weight, key_t, value, block, emb, keys, values, sems):
    width = value.shape[1]
    columns = pl.ds(col_start(width), width)
    copies = [
        pltpu.make_async_copy(key_weight.at[:, columns], keys, sems.at[0]),
        pltpu.make_async_copy(value_weight.at[:, columns], values, sems.at[1]),
        pltpu.make_async_copy(hist_emb, emb, sems.at[2]),
        pltpu.make_async_copy(adapter.at[:, columns], block, sems.at[3]),
    ]
    for copy in copies:
        copy.start()
    for copy in copies:
        copy.wait()
    value[...] = dot(emb[...], values[...]).astype(BF16)
    key_t[...] = jnp.transpose(dot(emb[...], keys[...]).astype(BF16))


def embed_own_kernel(mine, other, block, total):
    items = mine.shape[0]
    depth = block.shape[0]
    at = pl.ds(pl.multiple_of(lax.axis_index("hist") * depth, depth), depth)
    total[:items] = dot(mine[:, at], block[...])
    total[items:] = dot(other[:, at], block[...])


def add_block(n, groups, k, step, mine, other, top, bottom, block):
    depth = block.shape[0] - LISTED
    at = columns_of(n, groups, k, step, depth)
    return top + dot(mine[:, at], block[:depth]), bottom + dot(other[:, at], block[:depth])


def embed_add_kernel(n, groups, which, mine, other, total, *refs):
    items = mine.shape[0]
    top, bottom = total[:items], total[items:]
    for (k, step), block in zip(which, refs):
        top, bottom = add_block(n, groups, k, step, mine, other, top, bottom, block)
    refs[-1][:items] = top
    refs[-1][items:] = bottom


def columns_of(n, groups, k, step, depth):
    source = lax.rem(lax.axis_index("hist") + n - k, n)
    group = lax.rem(lax.axis_index("groups") + groups - step, groups)
    return pl.ds(pl.multiple_of((source * groups + group) * depth, depth), depth)


def query_part_kernel(n, groups, k, step, mine, other, pick, total, part, feats):
    items = mine.shape[0]
    at = columns_of(n, groups, k, step, feats.shape[1])
    part[...] = lax.dot(pick[...].astype(F32), total[...], precision=lax.Precision.HIGHEST)
    feats[...] = (dot(pick[:, :items], mine[:, at]) + dot(pick[:, items:], other[:, at])).astype(BF16)


def query_kernel(part, feats, block, query):
    query[...] = (part[...] + dot(feats[...], block[: feats.shape[1]])).astype(BF16)


def embed_last_kernel(n, groups, k, step, mine, other, total, block, rows, rows_t):
    items = mine.shape[0]
    top, bottom = add_block(n, groups, k, step, mine, other, total[:items], total[items:], block)
    rows[:items] = top.astype(BF16)
    rows[items:] = bottom.astype(BF16)
    rows_t[...] = jnp.transpose(rows[...])


def attend_kernel(k, query, key_t, value, rows_t, rows, scale, out):
    cands, width = query.shape
    heads = width // HS
    lane = iota((cands, width), 1) // HS
    part = query[...] * (0.5 * HS ** -0.5)
    zero = jnp.zeros_like(part)
    split = jnp.concatenate([jnp.where(lane == h, part, zero) for h in range(heads)], axis=0)
    events = key_t.shape[1]

    def weigh(keys, factor):
        half = dot(split, keys)
        gated = half + half * jnp.tanh(half)
        return (gated * jnp.concatenate([factor] * heads, axis=0)).astype(BF16)

    mixed = dot(weigh(key_t[...], scale[k, :, :events]), value[...])
    mixed = mixed + dot(weigh(rows_t[...], scale[k, :, events:]), rows[...])
    total = jnp.zeros((cands, width), F32)
    for h in range(heads):
        total = total + jnp.where(lane == h, mixed[h * cands : (h + 1) * cands], 0.0)
    out[...] = total.astype(out.dtype)


def gate_kernel(query, own, *refs):
    parts, keep, send = refs[:-2], refs[-2], refs[-1]
    total = own[...]
    for part in parts:
        total = total + part[...].astype(F32)
    gate = query[...].astype(F32)
    scored = (gate * jax.nn.sigmoid(gate) * total).astype(BF16)
    half = keep.shape[0]
    keep[...] = scored[:half]
    send[...] = scored[half:]


def join_kernel(keep, got, out):
    width = keep.shape[1]
    first = lax.axis_index("rep") == 0
    out[:, :width] = jnp.where(first, keep[...], got[...])
    out[:, width:] = jnp.where(first, got[...], keep[...])


def shift(value, axis, k):
    count = lax.axis_size(axis)
    return lax.ppermute(value, axis, [(i, (i + k) % count) for i in range(count)])


def shift_order(n):
    return sorted(range(1, n), key=lambda k: min(k, n - k))


def fast_body(
    item_feats, adapter, hist_emb, key_weight, value_weight, routes, cand_index, item_user, hist_user
):
    n, groups = lax.axis_size("hist"), lax.axis_size("groups")
    items, _ = item_feats.shape
    depth, cols = adapter.shape
    width = cols // 2
    cands = 2 * cand_index.shape[0]
    events, dim = hist_emb.shape
    order = shift_order(n)

    own_share, mine = call(
        share_kernel,
        (
            shape((depth // groups + LISTED, width), BF16),
            shape((1, 2 * items + cands + events), jnp.int32),
        ),
        (
            adapter,
            item_user.reshape(1, -1),
            routes.reshape(1, -1),
            cand_index.reshape(1, -1),
            hist_user.reshape(1, -1),
        ),
        specs=[HBM] * 5,
        scratch=[
            pltpu.VMEM((1, items), jnp.int32),
            pltpu.VMEM((1, items), jnp.int32),
            pltpu.VMEM((1, cands // 2), jnp.int32),
            pltpu.VMEM((1, events // 2), jnp.int32),
            pltpu.VMEM((1, events), jnp.int32),
            pltpu.SemaphoreType.DMA((6,)),
        ],
    )
    along = {}
    for k in order:
        if k in (1, n - 1):
            along[k] = shift(own_share, "hist", k)
        else:
            step = 1 if k <= n // 2 else n - 1
            along[k] = shift(along[(k - step) % n], "hist", step)
    feats_other = shift(item_feats, "rep", 1)
    other = shift(mine, "rep", 1)
    keys = events + 2 * items
    hot, pick = call(users_kernel, (shape((USERS, keys), BF16), shape((cands, 2 * items), BF16)), (mine, other))
    key_t, value, block = call(
        project_kernel,
        (shape((width, events), BF16), shape((events, width), BF16), shape((depth, width), BF16)),
        (adapter, hist_emb, key_weight, value_weight),
        flops=4 * events * dim * width,
        bytes_accessed=4 << 20,
        specs=[HBM] * 4,
        scratch=[
            pltpu.VMEM((events, dim), BF16),
            pltpu.VMEM((dim, width), BF16),
            pltpu.VMEM((dim, width), BF16),
            pltpu.SemaphoreType.DMA((4,)),
        ],
    )
    total = call(
        embed_own_kernel,
        shape((2 * items, width), F32),
        (item_feats, feats_other, block),
        flops=4 * items * depth * width,
        bytes_accessed=4 << 20,
    )
    tally = call(tally_kernel, shape((16, USERS), F32), (own_share, *[along[k] for k in range(1, n)]))
    scale = call(
        functools.partial(scale_kernel, items),
        shape((n, cands, keys), F32),
        (mine, other, hot, tally, shift(tally, "rep", 1)),
        bytes_accessed=4 << 20,
    )
    across = {k: [along[k]] + [shift(along[k], "groups", g) for g in range(1, groups)] for k in order}
    blocks = [((k, step), across[k][step]) for k in order for step in range(groups)]
    chunks = [blocks[at : at + groups] for at in range(0, len(blocks) - groups, groups)]
    chunks += [blocks[-groups:-1]]
    for k, chunk in zip(order, chunks):
        which, arrived = zip(*chunk)
        total = call(
            functools.partial(embed_add_kernel, n, groups, which),
            shape((2 * items, width), F32),
            (item_feats, feats_other, total, *arrived),
            flops=4 * items * depth * width,
            bytes_accessed=2 << 20,
        )
    (k, step), arrived = blocks[-1]
    share = depth // groups
    part, feats = call(
        functools.partial(query_part_kernel, n, groups, k, step),
        (shape((cands, width), F32), shape((cands, share), BF16)),
        (item_feats, feats_other, pick, total),
        flops=4 * cands * items * (share + 6 * width),
    )
    query = call(query_kernel, shape((cands, width), BF16), (part, feats, arrived), flops=2 * cands * share * width)
    rows, rows_t = call(
        functools.partial(embed_last_kernel, n, groups, k, step),
        (shape((2 * items, width), BF16), shape((width, 2 * items), BF16)),
        (item_feats, feats_other, total, arrived),
        flops=4 * items * share * width,
        bytes_accessed=2 << 20,
    )
    queries = {k: shift(query, "hist", k) for k in order}

    def attend(k, block, dtype):
        return call(
            functools.partial(attend_kernel, k),
            shape((cands, width), dtype),
            (block, key_t, value, rows_t, rows, scale),
            flops=8 * cands * keys * width,
            bytes_accessed=1 << 20,
        )

    own = attend(0, query, F32)
    parts = [shift(attend(k, queries[k], BF16), "hist", n - k) for k in order]
    keep, send = call(
        gate_kernel, (shape((cands // 2, width), BF16), shape((cands // 2, width), BF16)), (query, own, *parts)
    )
    got = shift(send, "rep", 1)
    return call(join_kernel, shape((cands // 2, cols), BF16), (keep, got))


def body(*args):
    item_feats, adapter, cand_index, hist_user = args[0], args[1], args[6], args[8]
    fits = (
        lax.axis_size("rep") == 2
        and 1 < lax.axis_size("hist") <= 4
        and item_feats.shape[0] + hist_user.shape[0] // 2 < 1024
        and hist_user.shape[0] % 256 == 0
        and adapter.shape[0] % (128 * lax.axis_size("groups")) == 0
        and adapter.shape[1] % 256 == 0
        and 2 * cand_index.shape[0] == 128
        and item_feats.shape[0] % 128 == 0
    )
    return fast_body(*args) if fits else generic_body(*args)


def solution(mesh):
    placed = (
        P(("groups", "hist", "rep"), None),
        P("hist", "head"),
        P(("groups", "hist"), None),
        P(None, "head"),
        P(None, "head"),
        P(("groups", "hist", "rep"), None),
        P(("groups", "hist", "rep")),
        P(("groups", "hist", "rep")),
        P(("groups", "hist")),
    )
    return jax.shard_map(
        body,
        mesh=mesh,
        in_specs=placed,
        out_specs=P(("groups", "hist", "rep"), "head"),
        check_vma=False,
    )
```

```python
import functools
import math

import jax
import jax.numpy as jnp
from jax import lax
from jax.experimental import pallas as pl
from jax.experimental.pallas import tpu as pltpu
from jax.sharding import PartitionSpec as P


HS = 64
USERS = 256
LISTED = 16
VM = pl.BlockSpec(memory_space=pltpu.VMEM)
HBM = pl.BlockSpec(memory_space=pltpu.HBM)
F32 = jnp.float32
BF16 = jnp.bfloat16


def attend(query_block, user_block, key_rows, value_rows, key_users):
    row_count = query_block.shape[0]
    col_count = query_block.shape[1]
    heads_here = col_count // HS
    att_scale = float(HS) ** (-0.5)
    query_three = query_block.reshape(row_count, heads_here, HS)
    key_three = key_rows.reshape(-1, heads_here, HS)
    value_three = value_rows.reshape(-1, heads_here, HS)
    scores = (
        jnp.einsum("rhd,khd->hrk", query_three, key_three, preferred_element_type=jnp.float32)
        * att_scale
    )
    matching = user_block[:, None] == key_users[None, :]
    weights = jnp.where(matching[None], jax.nn.silu(scores), 0.0).astype(jnp.bfloat16)
    mixture = jnp.einsum("hrk,khd->rhd", weights, value_three, preferred_element_type=jnp.float32)
    counted = jnp.sum(matching.astype(jnp.float32), axis=1)
    inverse = 1.0 / jnp.maximum(counted, 1.0)
    return mixture.reshape(row_count, col_count) * inverse[:, None]


def dense_partial(queries, users, key_rows, value_rows, key_users):
    total_rows = queries.shape[0]
    col_count = queries.shape[1]
    block_size = math.gcd(total_rows, 512)
    blocked_queries = queries.reshape(total_rows // block_size, block_size, col_count)
    blocked_users = users.reshape(total_rows // block_size, block_size)

    def one_block(operands):
        return attend(operands[0], operands[1], key_rows, value_rows, key_users)

    return lax.map(one_block, (blocked_queries, blocked_users)).reshape(total_rows, col_count)


def generic_body(
    item_feats,
    adapter,
    hist_emb,
    key_weight,
    value_weight,
    routes,
    cand_index,
    item_user,
    hist_user,
):
    owners = lax.axis_size("hist")
    item_count = item_feats.shape[0]
    col_count = adapter.shape[1]
    embedded = jnp.dot(
        item_feats,
        lax.all_gather(adapter, "hist", axis=0, tiled=True),
        preferred_element_type=jnp.float32,
    ).astype(jnp.bfloat16)
    capacity = 2 * item_count // owners
    owner_of = routes[:, 0]
    owner_hot = (owner_of[:, None] == jnp.arange(owners, dtype=jnp.int32)[None, :]).astype(
        jnp.int32
    )
    earlier = jnp.cumsum(owner_hot, axis=0) - owner_hot
    slot_of = jnp.sum(earlier * owner_hot, axis=1)
    position = owner_of * capacity + slot_of
    placing = (jnp.arange(owners * capacity, dtype=jnp.int32)[:, None] == position[None, :]).astype(
        jnp.bfloat16
    )
    outgoing = jnp.dot(placing, embedded, preferred_element_type=jnp.float32).astype(jnp.bfloat16)
    outgoing = outgoing.reshape(owners, capacity, col_count)
    shifted_user = (item_user + 1).astype(jnp.bfloat16)
    outgoing_user = (
        jnp.dot(placing, shifted_user, preferred_element_type=jnp.float32) - 1.0
    ).astype(jnp.bfloat16)
    outgoing_user = outgoing_user.reshape(owners, capacity)
    incoming, incoming_user = (
        lax.all_to_all(outgoing, "hist", split_axis=0, concat_axis=0, tiled=True),
        lax.all_to_all(outgoing_user, "hist", split_axis=0, concat_axis=0, tiled=True),
    )
    routed, routed_user = (
        lax.all_gather(incoming, "rep", axis=0, tiled=True),
        lax.all_gather(incoming_user, "rep", axis=0, tiled=True),
    )
    routed = routed.reshape(-1, col_count)
    routed_user = routed_user.reshape(-1)
    key_local = jnp.dot(hist_emb, key_weight, preferred_element_type=jnp.float32).astype(
        jnp.bfloat16
    )
    value_local = jnp.dot(hist_emb, value_weight, preferred_element_type=jnp.float32).astype(
        jnp.bfloat16
    )
    key_rows = jnp.concatenate([key_local, routed], axis=0)
    value_rows = jnp.concatenate([value_local, routed], axis=0)
    key_users = jnp.concatenate([hist_user.astype(jnp.bfloat16), routed_user], axis=0)
    own_queries = embedded[cand_index]
    own_users = item_user[cand_index].astype(jnp.bfloat16)
    gathered, gathered_users = (
        lax.all_gather(own_queries, "hist", axis=0, tiled=True),
        lax.all_gather(own_users, "hist", axis=0, tiled=True),
    )
    partial_value = dense_partial(gathered, gathered_users, key_rows, value_rows, key_users)
    attended = lax.psum_scatter(partial_value, "hist", scatter_dimension=0, tiled=True)
    gating = jax.nn.silu(own_queries.astype(jnp.float32))
    return (gating * attended).astype(jnp.bfloat16)


def call(kernel, outs, args, flops=0, bytes_accessed=1 << 18, vmem=16, specs=None, scratch=()):
    if specs:
        args = [pltpu.with_memory_space_constraint(arg, pltpu.HBM) for arg in args]
    return pl.pallas_call(
        kernel,
        out_shape=outs,
        in_specs=specs or [VM] * len(args),
        out_specs=jax.tree.map(lambda _: VM, outs),
        scratch_shapes=scratch,
        compiler_params=pltpu.CompilerParams(vmem_limit_bytes=vmem << 20),
        cost_estimate=pl.CostEstimate(flops=flops, bytes_accessed=bytes_accessed, transcendentals=0),
    )(*args)


def shape(dims, dtype):
    return jax.ShapeDtypeStruct(dims, dtype)


def iota(dims, axis):
    return lax.broadcasted_iota(jnp.int32, dims, axis)


def dot(a, b, contract=((1,), (0,))):
    return lax.dot_general(a, b, (contract, ((), ())), preferred_element_type=F32)


def col_start(width):
    return pl.multiple_of(lax.axis_index("rep") * width, width)


def one_hot(dims, axis, at):
    return (iota(dims, axis) == at).astype(F32).astype(BF16)


def share_kernel(
    adapter, item_user, routes, cand_index, hist_user, block, out, mine, user, owner, cand, event, events, sems
):
    _, cols = block.shape
    rows = out.shape[0] - LISTED
    row = pl.multiple_of(lax.axis_index("groups") * rows, rows)
    columns = pl.ds(col_start(cols), cols)
    part = event.shape[1]
    copies = [
        pltpu.make_async_copy(item_user, user, sems.at[0]),
        pltpu.make_async_copy(routes, owner, sems.at[1]),
        pltpu.make_async_copy(cand_index, cand, sems.at[2]),
        pltpu.make_async_copy(hist_user.at[:, pl.ds(col_start(part), part)], event, sems.at[3]),
        pltpu.make_async_copy(adapter.at[pl.ds(row, rows), columns], out.at[pl.ds(0, rows)], sems.at[4]),
        pltpu.make_async_copy(adapter.at[:, columns], block, sems.at[5]),
        pltpu.make_async_copy(hist_user, events, sems.at[6]),
    ]
    for copy in copies:
        copy.start()
    for copy in copies[:4]:
        copy.wait()
    items = user.shape[1]
    cands = cand.shape[1]
    mine[:, :items] = user[...]
    mine[:, items : 2 * items] = owner[...]
    mine[:, 2 * items : 2 * items + 2 * cands] = jnp.concatenate([cand[...], cand[...]], axis=1)
    items_hot = one_hot((USERS, items), 0, user[...])
    counts = dot(one_hot((8, items), 0, owner[...]), items_hot, ((1,), (1,)))
    here = jnp.zeros((1, part), jnp.int32) + lax.axis_index("hist")
    counts = counts + dot(one_hot((8, part), 0, here), one_hot((USERS, part), 0, event[...]), ((1,), (1,)))
    chosen = one_hot((items, cands), 0, cand[...])
    users = dot(jnp.broadcast_to(user[...], (8, items)).astype(F32).astype(BF16), chosen)
    users = jnp.concatenate([users, jnp.zeros((8, USERS - cands), F32)], axis=1)
    quarter = jnp.floor(counts * 0.25)
    rest = jnp.sum((counts - 4.0 * quarter) * digit_weight(4.0), axis=0, keepdims=True)
    half = USERS // 2
    row = iota((8, half), 0)
    top = jnp.where(row < 4, quarter[:, :half], pltpu.roll(quarter[:, half:], 4, 0))
    bottom = jnp.where(row == 0, rest[:, :half], jnp.where(row == 1, rest[:, half:], users[:, :half]))
    out[rows:] = jnp.concatenate([top, jnp.where(row < 3, bottom, 0.0)], axis=0).astype(BF16)
    for copy in copies[4:]:
        copy.wait()
    mine[:, 2 * items + 2 * cands :] = events[...]


def digit_weight(base):
    row = iota((8, 1), 0)
    weight = jnp.zeros((8, 1), F32)
    for owner in range(4):
        weight = jnp.where(row == owner, base ** owner, weight)
    return weight


def users_kernel(mine, other, hot, pick):
    lanes, both = pick.shape
    items = both // 2
    half = lanes // 2
    both_user = jnp.concatenate([mine[:, :items], other[:, :items]], axis=1)
    at = slice(2 * items, 2 * items + lanes)
    moved = pltpu.roll(jnp.broadcast_to(other[:, at], (8, lanes)), half, 1)[:1] + items
    cand = jnp.where(iota((1, lanes), 1) < half, mine[:, at], moved)
    event_user = mine[:, 2 * items + lanes :]
    events = event_user.shape[1]
    hot[:, :events] = one_hot((USERS, events), 0, event_user)
    hot[:, events:] = one_hot((USERS, both), 0, both_user)
    chosen = (iota((both, lanes), 0) == cand).astype(F32)
    pick[...] = jnp.transpose(chosen).astype(BF16)


def tally_kernel(*refs):
    out = refs[-1]
    row = iota((8, USERS // 2), 0)
    total = jnp.zeros((8, USERS), F32)
    for k, ref in enumerate(refs[:-1]):
        listed = ref[ref.shape[0] - LISTED :].astype(F32)
        top, bottom = listed[:8], listed[8:]
        low, high = jnp.where(row < 4, top, 0.0), jnp.where(row < 4, pltpu.roll(top, 4, 0), 0.0)
        rest = jnp.concatenate([bottom[:1], bottom[1:2]], axis=1)
        digits = jnp.floor(rest * digit_weight(0.25))
        rest = digits - 4.0 * jnp.floor(digits * 0.25)
        total = total + 4.0 * jnp.concatenate([low, high], axis=1) + rest
        out[8 + k : 9 + k] = jnp.concatenate([bottom[2:3], jnp.zeros_like(bottom[2:3])], axis=1)
    out[:8] = total


def scale_kernel(items, mine, other, hot, tally, tally_other, out):
    n, lanes, _ = out.shape
    hist_user = mine[:, 2 * items + lanes :]
    events = hist_user.shape[1]
    total = tally[:8] + tally_other[:8]
    high = jnp.floor(total * (1.0 / 256.0))
    low = total - 256.0 * high
    counts = 256.0 * dot(high.astype(BF16), hot[...]) + dot(low.astype(BF16), hot[...])
    both_owner = jnp.concatenate([mine[:, items : 2 * items], other[:, items : 2 * items]], axis=1)
    here = jnp.zeros((1, events), jnp.int32) + lax.axis_index("hist")
    owner = jnp.concatenate([here, both_owner], axis=1)
    count = jnp.sum(jnp.where(iota(counts.shape, 0) == owner, counts, 0.0), axis=0, keepdims=True)
    inverse = 1.0 / jnp.maximum(count, 1.0)
    user = jnp.concatenate([hist_user, mine[:, :items], other[:, :items]], axis=1).astype(F32)
    diagonal = iota((lanes, lanes), 0) == iota((lanes, lanes), 1)
    first = iota((8, lanes), 1) < lanes // 2
    near = tally[8:16, :lanes]
    far = pltpu.roll(tally_other[8:16, :lanes], lanes // 2, 1)
    cand = jnp.where(first, near, far)
    for k in range(n):
        column = jnp.sum(jnp.where(diagonal, cand[k : k + 1], 0.0), axis=1, keepdims=True)
        out[k] = jnp.where(column == user, inverse, 0.0)


def project_kernel(hist_emb, key_weight, value_weight, key_t, value, emb, keys, values, sems):
    width = value.shape[1]
    columns = pl.ds(col_start(width), width)
    copies = [
        pltpu.make_async_copy(key_weight.at[:, columns], keys, sems.at[0]),
        pltpu.make_async_copy(value_weight.at[:, columns], values, sems.at[1]),
        pltpu.make_async_copy(hist_emb, emb, sems.at[2]),
    ]
    for copy in copies:
        copy.start()
    for copy in copies:
        copy.wait()
    value[...] = dot(emb[...], values[...]).astype(BF16)
    key_t[...] = jnp.transpose(dot(emb[...], keys[...]).astype(BF16))


def embed_own_kernel(mine, other, block, total):
    items = mine.shape[0]
    depth = block.shape[0]
    at = pl.ds(pl.multiple_of(lax.axis_index("hist") * depth, depth), depth)
    total[:items] = dot(mine[:, at], block[...])
    total[items:] = dot(other[:, at], block[...])


def add_block(n, groups, k, step, mine, other, top, bottom, block):
    depth = block.shape[0] - LISTED
    at = columns_of(n, groups, k, step, depth)
    return top + dot(mine[:, at], block[:depth]), bottom + dot(other[:, at], block[:depth])


def embed_add_kernel(n, groups, which, mine, other, total, *refs):
    items = mine.shape[0]
    top, bottom = total[:items], total[items:]
    for (k, step), block in zip(which, refs):
        top, bottom = add_block(n, groups, k, step, mine, other, top, bottom, block)
    refs[-1][:items] = top
    refs[-1][items:] = bottom


def columns_of(n, groups, k, step, depth):
    source = lax.rem(lax.axis_index("hist") + n - k, n)
    group = lax.rem(lax.axis_index("groups") + groups - step, groups)
    return pl.ds(pl.multiple_of((source * groups + group) * depth, depth), depth)


def query_part_kernel(n, groups, which, mine, other, pick, total, part, feats):
    items = mine.shape[0]
    depth = feats.shape[1] // len(which)
    part[...] = lax.dot(pick[...].astype(F32), total[...], precision=lax.Precision.HIGHEST)
    for slot, (k, step) in enumerate(which):
        at = columns_of(n, groups, k, step, depth)
        picked = dot(pick[:, :items], mine[:, at]) + dot(pick[:, items:], other[:, at])
        feats[:, slot * depth : (slot + 1) * depth] = picked.astype(BF16)


def query_kernel(part, feats, *refs):
    blocks, query = refs[:-1], refs[-1]
    depth = feats.shape[1] // len(blocks)
    total = part[...]
    for slot, block in enumerate(blocks):
        total = total + dot(feats[:, slot * depth : (slot + 1) * depth], block[:depth])
    query[...] = total.astype(BF16)


def embed_last_kernel(n, groups, which, mine, other, total, *refs):
    items = mine.shape[0]
    blocks, (rows, rows_t) = refs[:-2], refs[-2:]
    top, bottom = total[:items], total[items:]
    for (k, step), block in zip(which, blocks):
        top, bottom = add_block(n, groups, k, step, mine, other, top, bottom, block)
    rows[:items] = top.astype(BF16)
    rows[items:] = bottom.astype(BF16)
    rows_t[...] = jnp.transpose(rows[...])


def attend_kernel(k, query, key_t, value, rows_t, rows, scale, out):
    cands, width = query.shape
    heads = width // HS
    lane = iota((cands, width), 1) // HS
    part = query[...] * (0.5 * HS ** -0.5)
    zero = jnp.zeros_like(part)
    split = jnp.concatenate([jnp.where(lane == h, part, zero) for h in range(heads)], axis=0)
    events = key_t.shape[1]

    def weigh(keys, factor):
        half = dot(split, keys)
        gated = half + half * jnp.tanh(half)
        return (gated * jnp.concatenate([factor] * heads, axis=0)).astype(BF16)

    mixed = dot(weigh(key_t[...], scale[k, :, :events]), value[...])
    mixed = mixed + dot(weigh(rows_t[...], scale[k, :, events:]), rows[...])
    total = jnp.zeros((cands, width), F32)
    for h in range(heads):
        total = total + jnp.where(lane == h, mixed[h * cands : (h + 1) * cands], 0.0)
    out[...] = total.astype(out.dtype)


def gate_kernel(query, own, *refs):
    parts, keep, send = refs[:-2], refs[-2], refs[-1]
    total = own[...]
    for part in parts:
        total = total + part[...].astype(F32)
    gate = query[...].astype(F32)
    scored = (gate * jax.nn.sigmoid(gate) * total).astype(BF16)
    half = keep.shape[0]
    keep[...] = scored[:half]
    send[...] = scored[half:]


def join_kernel(keep, got, out):
    width = keep.shape[1]
    first = lax.axis_index("rep") == 0
    out[:, :width] = jnp.where(first, keep[...], got[...])
    out[:, width:] = jnp.where(first, got[...], keep[...])


def shift(value, axis, k):
    count = lax.axis_size(axis)
    return lax.ppermute(value, axis, [(i, (i + k) % count) for i in range(count)])


def shift_order(n):
    return sorted(range(1, n), key=lambda k: min(k, n - k))


def fast_body(
    item_feats, adapter, hist_emb, key_weight, value_weight, routes, cand_index, item_user, hist_user
):
    n, groups = lax.axis_size("hist"), lax.axis_size("groups")
    items, _ = item_feats.shape
    depth, cols = adapter.shape
    width = cols // 2
    cands = 2 * cand_index.shape[0]
    events, dim = hist_emb.shape
    order = shift_order(n)

    block, own_share, mine = call(
        share_kernel,
        (
            shape((depth, width), BF16),
            shape((depth // groups + LISTED, width), BF16),
            shape((1, 2 * items + cands + events), jnp.int32),
        ),
        (
            adapter,
            item_user.reshape(1, -1),
            routes.reshape(1, -1),
            cand_index.reshape(1, -1),
            hist_user.reshape(1, -1),
        ),
        specs=[HBM] * 5,
        scratch=[
            pltpu.VMEM((1, items), jnp.int32),
            pltpu.VMEM((1, items), jnp.int32),
            pltpu.VMEM((1, cands // 2), jnp.int32),
            pltpu.VMEM((1, events // 2), jnp.int32),
            pltpu.VMEM((1, events), jnp.int32),
            pltpu.SemaphoreType.DMA((7,)),
        ],
    )
    along = {}
    for k in order:
        if k in (1, n - 1):
            along[k] = shift(own_share, "hist", k)
        else:
            step = 1 if k <= n // 2 else n - 1
            along[k] = shift(along[(k - step) % n], "hist", step)
    feats_other = shift(item_feats, "rep", 1)
    other = shift(mine, "rep", 1)
    keys = events + 2 * items
    hot, pick = call(users_kernel, (shape((USERS, keys), BF16), shape((cands, 2 * items), BF16)), (mine, other))
    key_t, value = call(
        project_kernel,
        (shape((width, events), BF16), shape((events, width), BF16)),
        (hist_emb, key_weight, value_weight),
        flops=4 * events * dim * width,
        bytes_accessed=4 << 20,
        specs=[HBM] * 3,
        scratch=[
            pltpu.VMEM((events, dim), BF16),
            pltpu.VMEM((dim, width), BF16),
            pltpu.VMEM((dim, width), BF16),
            pltpu.SemaphoreType.DMA((3,)),
        ],
    )
    total = call(
        embed_own_kernel,
        shape((2 * items, width), F32),
        (item_feats, feats_other, block),
        flops=4 * items * depth * width,
        bytes_accessed=4 << 20,
    )
    tally = call(tally_kernel, shape((16, USERS), F32), (own_share, *[along[k] for k in range(1, n)]))
    scale = call(
        functools.partial(scale_kernel, items),
        shape((n, cands, keys), F32),
        (mine, other, hot, tally, shift(tally, "rep", 1)),
        bytes_accessed=4 << 20,
    )
    across = {k: [along[k]] + [shift(along[k], "groups", g) for g in range(1, groups)] for k in order}
    near = [((k, 0), across[k][0]) for k in order]
    far = [((k, step), across[k][step]) for k in order for step in range(1, groups)]
    for chunk in (near, far[:1]):
        which, arrived = zip(*chunk)
        total = call(
            functools.partial(embed_add_kernel, n, groups, which),
            shape((2 * items, width), F32),
            (item_feats, feats_other, total, *arrived),
            flops=4 * items * depth * width,
            bytes_accessed=2 << 20,
        )
    which, arrived = zip(*far[1:])
    share = depth // groups
    part, feats = call(
        functools.partial(query_part_kernel, n, groups, which),
        (shape((cands, width), F32), shape((cands, share * len(which)), BF16)),
        (item_feats, feats_other, pick, total),
        flops=4 * cands * items * (share + 6 * width),
    )
    query = call(query_kernel, shape((cands, width), BF16), (part, feats, *arrived), flops=4 * cands * share * width)
    rows, rows_t = call(
        functools.partial(embed_last_kernel, n, groups, which),
        (shape((2 * items, width), BF16), shape((width, 2 * items), BF16)),
        (item_feats, feats_other, total, *arrived),
        flops=8 * items * share * width,
        bytes_accessed=2 << 20,
    )
    queries = {k: shift(query, "hist", k) for k in order}

    def attend(k, block, dtype):
        return call(
            functools.partial(attend_kernel, k),
            shape((cands, width), dtype),
            (block, key_t, value, rows_t, rows, scale),
            flops=8 * cands * keys * width,
            bytes_accessed=1 << 20,
        )

    own = attend(0, query, F32)
    parts = [shift(attend(k, queries[k], BF16), "hist", n - k) for k in order]
    keep, send = call(
        gate_kernel, (shape((cands // 2, width), BF16), shape((cands // 2, width), BF16)), (query, own, *parts)
    )
    got = shift(send, "rep", 1)
    return call(join_kernel, shape((cands // 2, cols), BF16), (keep, got))


def body(*args):
    item_feats, adapter, cand_index, hist_user = args[0], args[1], args[6], args[8]
    fits = (
        lax.axis_size("rep") == 2
        and 1 < lax.axis_size("hist") <= 4
        and item_feats.shape[0] + hist_user.shape[0] // 2 < 1024
        and hist_user.shape[0] % 256 == 0
        and adapter.shape[0] % (128 * lax.axis_size("groups")) == 0
        and adapter.shape[1] % 256 == 0
        and 2 * cand_index.shape[0] == 128
        and item_feats.shape[0] % 128 == 0
    )
    return fast_body(*args) if fits else generic_body(*args)


def solution(mesh):
    placed = (
        P(("groups", "hist", "rep"), None),
        P("hist", "head"),
        P(("groups", "hist"), None),
        P(None, "head"),
        P(None, "head"),
        P(("groups", "hist", "rep"), None),
        P(("groups", "hist", "rep")),
        P(("groups", "hist", "rep")),
        P(("groups", "hist")),
    )
    return jax.shard_map(
        body,
        mesh=mesh,
        in_specs=placed,
        out_specs=P(("groups", "hist", "rep"), "head"),
        check_vma=False,
    )
```

```python
import functools
import math

import jax
import jax.numpy as jnp
from jax import lax
from jax.experimental import pallas as pl
from jax.experimental.pallas import tpu as pltpu
from jax.sharding import PartitionSpec as P


HS = 64
USERS = 256
LISTED = 16
VM = pl.BlockSpec(memory_space=pltpu.VMEM)
HBM = pl.BlockSpec(memory_space=pltpu.HBM)
F32 = jnp.float32
BF16 = jnp.bfloat16


def attend(query_block, user_block, key_rows, value_rows, key_users):
    row_count = query_block.shape[0]
    col_count = query_block.shape[1]
    heads_here = col_count // HS
    att_scale = float(HS) ** (-0.5)
    query_three = query_block.reshape(row_count, heads_here, HS)
    key_three = key_rows.reshape(-1, heads_here, HS)
    value_three = value_rows.reshape(-1, heads_here, HS)
    scores = (
        jnp.einsum("rhd,khd->hrk", query_three, key_three, preferred_element_type=jnp.float32)
        * att_scale
    )
    matching = user_block[:, None] == key_users[None, :]
    weights = jnp.where(matching[None], jax.nn.silu(scores), 0.0).astype(jnp.bfloat16)
    mixture = jnp.einsum("hrk,khd->rhd", weights, value_three, preferred_element_type=jnp.float32)
    counted = jnp.sum(matching.astype(jnp.float32), axis=1)
    inverse = 1.0 / jnp.maximum(counted, 1.0)
    return mixture.reshape(row_count, col_count) * inverse[:, None]


def dense_partial(queries, users, key_rows, value_rows, key_users):
    total_rows = queries.shape[0]
    col_count = queries.shape[1]
    block_size = math.gcd(total_rows, 512)
    blocked_queries = queries.reshape(total_rows // block_size, block_size, col_count)
    blocked_users = users.reshape(total_rows // block_size, block_size)

    def one_block(operands):
        return attend(operands[0], operands[1], key_rows, value_rows, key_users)

    return lax.map(one_block, (blocked_queries, blocked_users)).reshape(total_rows, col_count)


def generic_body(
    item_feats,
    adapter,
    hist_emb,
    key_weight,
    value_weight,
    routes,
    cand_index,
    item_user,
    hist_user,
):
    owners = lax.axis_size("hist")
    item_count = item_feats.shape[0]
    col_count = adapter.shape[1]
    embedded = jnp.dot(
        item_feats,
        lax.all_gather(adapter, "hist", axis=0, tiled=True),
        preferred_element_type=jnp.float32,
    ).astype(jnp.bfloat16)
    capacity = 2 * item_count // owners
    owner_of = routes[:, 0]
    owner_hot = (owner_of[:, None] == jnp.arange(owners, dtype=jnp.int32)[None, :]).astype(
        jnp.int32
    )
    earlier = jnp.cumsum(owner_hot, axis=0) - owner_hot
    slot_of = jnp.sum(earlier * owner_hot, axis=1)
    position = owner_of * capacity + slot_of
    placing = (jnp.arange(owners * capacity, dtype=jnp.int32)[:, None] == position[None, :]).astype(
        jnp.bfloat16
    )
    outgoing = jnp.dot(placing, embedded, preferred_element_type=jnp.float32).astype(jnp.bfloat16)
    outgoing = outgoing.reshape(owners, capacity, col_count)
    shifted_user = (item_user + 1).astype(jnp.bfloat16)
    outgoing_user = (
        jnp.dot(placing, shifted_user, preferred_element_type=jnp.float32) - 1.0
    ).astype(jnp.bfloat16)
    outgoing_user = outgoing_user.reshape(owners, capacity)
    incoming, incoming_user = (
        lax.all_to_all(outgoing, "hist", split_axis=0, concat_axis=0, tiled=True),
        lax.all_to_all(outgoing_user, "hist", split_axis=0, concat_axis=0, tiled=True),
    )
    routed, routed_user = (
        lax.all_gather(incoming, "rep", axis=0, tiled=True),
        lax.all_gather(incoming_user, "rep", axis=0, tiled=True),
    )
    routed = routed.reshape(-1, col_count)
    routed_user = routed_user.reshape(-1)
    key_local = jnp.dot(hist_emb, key_weight, preferred_element_type=jnp.float32).astype(
        jnp.bfloat16
    )
    value_local = jnp.dot(hist_emb, value_weight, preferred_element_type=jnp.float32).astype(
        jnp.bfloat16
    )
    key_rows = jnp.concatenate([key_local, routed], axis=0)
    value_rows = jnp.concatenate([value_local, routed], axis=0)
    key_users = jnp.concatenate([hist_user.astype(jnp.bfloat16), routed_user], axis=0)
    own_queries = embedded[cand_index]
    own_users = item_user[cand_index].astype(jnp.bfloat16)
    gathered, gathered_users = (
        lax.all_gather(own_queries, "hist", axis=0, tiled=True),
        lax.all_gather(own_users, "hist", axis=0, tiled=True),
    )
    partial_value = dense_partial(gathered, gathered_users, key_rows, value_rows, key_users)
    attended = lax.psum_scatter(partial_value, "hist", scatter_dimension=0, tiled=True)
    gating = jax.nn.silu(own_queries.astype(jnp.float32))
    return (gating * attended).astype(jnp.bfloat16)


def call(kernel, outs, args, flops=0, bytes_accessed=1 << 18, vmem=16, specs=None, scratch=()):
    if specs:
        args = [pltpu.with_memory_space_constraint(arg, pltpu.HBM) for arg in args]
    return pl.pallas_call(
        kernel,
        out_shape=outs,
        in_specs=specs or [VM] * len(args),
        out_specs=jax.tree.map(lambda _: VM, outs),
        scratch_shapes=scratch,
        compiler_params=pltpu.CompilerParams(vmem_limit_bytes=vmem << 20),
        cost_estimate=pl.CostEstimate(flops=flops, bytes_accessed=bytes_accessed, transcendentals=0),
    )(*args)


def shape(dims, dtype):
    return jax.ShapeDtypeStruct(dims, dtype)


def iota(dims, axis):
    return lax.broadcasted_iota(jnp.int32, dims, axis)


def dot(a, b, contract=((1,), (0,))):
    return lax.dot_general(a, b, (contract, ((), ())), preferred_element_type=F32)


def col_start(width):
    return pl.multiple_of(lax.axis_index("rep") * width, width)


def one_hot(dims, axis, at):
    return (iota(dims, axis) == at).astype(F32).astype(BF16)


def share_kernel(
    adapter, item_user, routes, cand_index, hist_user, out, mine, user, owner, cand, event, events, sems
):
    rows, cols = out.shape[0] - LISTED, out.shape[1]
    row = pl.multiple_of(lax.axis_index("groups") * rows, rows)
    columns = pl.ds(col_start(cols), cols)
    part = event.shape[1]
    copies = [
        pltpu.make_async_copy(item_user, user, sems.at[0]),
        pltpu.make_async_copy(routes, owner, sems.at[1]),
        pltpu.make_async_copy(cand_index, cand, sems.at[2]),
        pltpu.make_async_copy(hist_user.at[:, pl.ds(col_start(part), part)], event, sems.at[3]),
        pltpu.make_async_copy(adapter.at[pl.ds(row, rows), columns], out.at[pl.ds(0, rows)], sems.at[4]),
        pltpu.make_async_copy(hist_user, events, sems.at[5]),
    ]
    for copy in copies:
        copy.start()
    for copy in copies[:4]:
        copy.wait()
    items = user.shape[1]
    cands = cand.shape[1]
    mine[:, :items] = user[...]
    mine[:, items : 2 * items] = owner[...]
    mine[:, 2 * items : 2 * items + 2 * cands] = jnp.concatenate([cand[...], cand[...]], axis=1)
    items_hot = one_hot((USERS, items), 0, user[...])
    counts = dot(one_hot((8, items), 0, owner[...]), items_hot, ((1,), (1,)))
    here = jnp.zeros((1, part), jnp.int32) + lax.axis_index("hist")
    counts = counts + dot(one_hot((8, part), 0, here), one_hot((USERS, part), 0, event[...]), ((1,), (1,)))
    chosen = one_hot((items, cands), 0, cand[...])
    users = dot(jnp.broadcast_to(user[...], (8, items)).astype(F32).astype(BF16), chosen)
    users = jnp.concatenate([users, jnp.zeros((8, USERS - cands), F32)], axis=1)
    quarter = jnp.floor(counts * 0.25)
    rest = jnp.sum((counts - 4.0 * quarter) * digit_weight(4.0), axis=0, keepdims=True)
    half = USERS // 2
    row = iota((8, half), 0)
    top = jnp.where(row < 4, quarter[:, :half], pltpu.roll(quarter[:, half:], 4, 0))
    bottom = jnp.where(row == 0, rest[:, :half], jnp.where(row == 1, rest[:, half:], users[:, :half]))
    out[rows:] = jnp.concatenate([top, jnp.where(row < 3, bottom, 0.0)], axis=0).astype(BF16)
    for copy in copies[4:]:
        copy.wait()
    mine[:, 2 * items + 2 * cands :] = events[...]


def digit_weight(base):
    row = iota((8, 1), 0)
    weight = jnp.zeros((8, 1), F32)
    for owner in range(4):
        weight = jnp.where(row == owner, base ** owner, weight)
    return weight


def users_kernel(mine, other, hot, pick):
    lanes, both = pick.shape
    items = both // 2
    half = lanes // 2
    both_user = jnp.concatenate([mine[:, :items], other[:, :items]], axis=1)
    at = slice(2 * items, 2 * items + lanes)
    moved = pltpu.roll(jnp.broadcast_to(other[:, at], (8, lanes)), half, 1)[:1] + items
    cand = jnp.where(iota((1, lanes), 1) < half, mine[:, at], moved)
    event_user = mine[:, 2 * items + lanes :]
    events = event_user.shape[1]
    hot[:, :events] = one_hot((USERS, events), 0, event_user)
    hot[:, events:] = one_hot((USERS, both), 0, both_user)
    chosen = (iota((both, lanes), 0) == cand).astype(F32)
    pick[...] = jnp.transpose(chosen).astype(BF16)


def tally_kernel(*refs):
    out = refs[-1]
    row = iota((8, USERS // 2), 0)
    total = jnp.zeros((8, USERS), F32)
    for k, ref in enumerate(refs[:-1]):
        listed = ref[ref.shape[0] - LISTED :].astype(F32)
        top, bottom = listed[:8], listed[8:]
        low, high = jnp.where(row < 4, top, 0.0), jnp.where(row < 4, pltpu.roll(top, 4, 0), 0.0)
        rest = jnp.concatenate([bottom[:1], bottom[1:2]], axis=1)
        digits = jnp.floor(rest * digit_weight(0.25))
        rest = digits - 4.0 * jnp.floor(digits * 0.25)
        total = total + 4.0 * jnp.concatenate([low, high], axis=1) + rest
        out[8 + k : 9 + k] = jnp.concatenate([bottom[2:3], jnp.zeros_like(bottom[2:3])], axis=1)
    out[:8] = total


def scale_kernel(items, mine, other, hot, tally, tally_other, out):
    n, lanes, _ = out.shape
    hist_user = mine[:, 2 * items + lanes :]
    events = hist_user.shape[1]
    total = tally[:8] + tally_other[:8]
    high = jnp.floor(total * (1.0 / 256.0))
    low = total - 256.0 * high
    counts = 256.0 * dot(high.astype(BF16), hot[...]) + dot(low.astype(BF16), hot[...])
    both_owner = jnp.concatenate([mine[:, items : 2 * items], other[:, items : 2 * items]], axis=1)
    here = jnp.zeros((1, events), jnp.int32) + lax.axis_index("hist")
    owner = jnp.concatenate([here, both_owner], axis=1)
    count = jnp.sum(jnp.where(iota(counts.shape, 0) == owner, counts, 0.0), axis=0, keepdims=True)
    inverse = 1.0 / jnp.maximum(count, 1.0)
    user = jnp.concatenate([hist_user, mine[:, :items], other[:, :items]], axis=1).astype(F32)
    diagonal = iota((lanes, lanes), 0) == iota((lanes, lanes), 1)
    first = iota((8, lanes), 1) < lanes // 2
    near = tally[8:16, :lanes]
    far = pltpu.roll(tally_other[8:16, :lanes], lanes // 2, 1)
    cand = jnp.where(first, near, far)
    for k in range(n):
        column = jnp.sum(jnp.where(diagonal, cand[k : k + 1], 0.0), axis=1, keepdims=True)
        out[k] = jnp.where(column == user, inverse, 0.0)


def project_kernel(adapter, hist_emb, key_weight, value_weight, key_t, value, block, emb, keys, values, sems):
    width = value.shape[1]
    columns = pl.ds(col_start(width), width)
    copies = [
        pltpu.make_async_copy(key_weight.at[:, columns], keys, sems.at[0]),
        pltpu.make_async_copy(value_weight.at[:, columns], values, sems.at[1]),
        pltpu.make_async_copy(hist_emb, emb, sems.at[2]),
        pltpu.make_async_copy(adapter.at[:, columns], block, sems.at[3]),
    ]
    for copy in copies:
        copy.start()
    for copy in copies:
        copy.wait()
    value[...] = dot(emb[...], values[...]).astype(BF16)
    key_t[...] = jnp.transpose(dot(emb[...], keys[...]).astype(BF16))


def embed_own_kernel(mine, other, block, total):
    items = mine.shape[0]
    depth = block.shape[0]
    at = pl.ds(pl.multiple_of(lax.axis_index("hist") * depth, depth), depth)
    total[:items] = dot(mine[:, at], block[...])
    total[items:] = dot(other[:, at], block[...])


def add_block(n, groups, k, step, mine, other, top, bottom, block):
    depth = block.shape[0] - LISTED
    at = columns_of(n, groups, k, step, depth)
    return top + dot(mine[:, at], block[:depth]), bottom + dot(other[:, at], block[:depth])


def embed_add_kernel(n, groups, which, mine, other, total, *refs):
    items = mine.shape[0]
    top, bottom = total[:items], total[items:]
    for (k, step), block in zip(which, refs):
        top, bottom = add_block(n, groups, k, step, mine, other, top, bottom, block)
    refs[-1][:items] = top
    refs[-1][items:] = bottom


def columns_of(n, groups, k, step, depth):
    source = lax.rem(lax.axis_index("hist") + n - k, n)
    group = lax.rem(lax.axis_index("groups") + groups - step, groups)
    return pl.ds(pl.multiple_of((source * groups + group) * depth, depth), depth)


def query_part_kernel(n, groups, which, mine, other, pick, total, part, feats):
    items = mine.shape[0]
    depth = feats.shape[1] // len(which)
    part[...] = lax.dot(pick[...].astype(F32), total[...], precision=lax.Precision.HIGHEST)
    for slot, (k, step) in enumerate(which):
        at = columns_of(n, groups, k, step, depth)
        picked = dot(pick[:, :items], mine[:, at]) + dot(pick[:, items:], other[:, at])
        feats[:, slot * depth : (slot + 1) * depth] = picked.astype(BF16)


def query_kernel(part, feats, *refs):
    blocks, query = refs[:-1], refs[-1]
    depth = feats.shape[1] // len(blocks)
    total = part[...]
    for slot, block in enumerate(blocks):
        total = total + dot(feats[:, slot * depth : (slot + 1) * depth], block[:depth])
    query[...] = total.astype(BF16)


def embed_last_kernel(n, groups, which, mine, other, total, *refs):
    items = mine.shape[0]
    blocks, (rows, rows_t) = refs[:-2], refs[-2:]
    top, bottom = total[:items], total[items:]
    for (k, step), block in zip(which, blocks):
        top, bottom = add_block(n, groups, k, step, mine, other, top, bottom, block)
    rows[:items] = top.astype(BF16)
    rows[items:] = bottom.astype(BF16)
    rows_t[...] = jnp.transpose(rows[...])


def attend_kernel(k, query, key_t, value, rows_t, rows, scale, out):
    cands, width = query.shape
    heads = width // HS
    lane = iota((cands, width), 1) // HS
    part = query[...] * (0.5 * HS ** -0.5)
    zero = jnp.zeros_like(part)
    split = jnp.concatenate([jnp.where(lane == h, part, zero) for h in range(heads)], axis=0)
    events = key_t.shape[1]

    def weigh(keys, factor):
        half = dot(split, keys)
        gated = half + half * jnp.tanh(half)
        return (gated * jnp.concatenate([factor] * heads, axis=0)).astype(BF16)

    mixed = dot(weigh(key_t[...], scale[k, :, :events]), value[...])
    mixed = mixed + dot(weigh(rows_t[...], scale[k, :, events:]), rows[...])
    total = jnp.zeros((cands, width), F32)
    for h in range(heads):
        total = total + jnp.where(lane == h, mixed[h * cands : (h + 1) * cands], 0.0)
    out[...] = total.astype(out.dtype)


def gate_kernel(query, own, *refs):
    parts, keep, send = refs[:-2], refs[-2], refs[-1]
    total = own[...]
    for part in parts:
        total = total + part[...].astype(F32)
    gate = query[...].astype(F32)
    scored = (gate * jax.nn.sigmoid(gate) * total).astype(BF16)
    half = keep.shape[0]
    keep[...] = scored[:half]
    send[...] = scored[half:]


def join_kernel(keep, got, out):
    width = keep.shape[1]
    first = lax.axis_index("rep") == 0
    out[:, :width] = jnp.where(first, keep[...], got[...])
    out[:, width:] = jnp.where(first, got[...], keep[...])


def shift(value, axis, k):
    count = lax.axis_size(axis)
    return lax.ppermute(value, axis, [(i, (i + k) % count) for i in range(count)])


def shift_order(n):
    return sorted(range(1, n), key=lambda k: min(k, n - k))


def fast_body(
    item_feats, adapter, hist_emb, key_weight, value_weight, routes, cand_index, item_user, hist_user
):
    n, groups = lax.axis_size("hist"), lax.axis_size("groups")
    items, _ = item_feats.shape
    depth, cols = adapter.shape
    width = cols // 2
    cands = 2 * cand_index.shape[0]
    events, dim = hist_emb.shape
    order = shift_order(n)

    own_share, mine = call(
        share_kernel,
        (
            shape((depth // groups + LISTED, width), BF16),
            shape((1, 2 * items + cands + events), jnp.int32),
        ),
        (
            adapter,
            item_user.reshape(1, -1),
            routes.reshape(1, -1),
            cand_index.reshape(1, -1),
            hist_user.reshape(1, -1),
        ),
        specs=[HBM] * 5,
        scratch=[
            pltpu.VMEM((1, items), jnp.int32),
            pltpu.VMEM((1, items), jnp.int32),
            pltpu.VMEM((1, cands // 2), jnp.int32),
            pltpu.VMEM((1, events // 2), jnp.int32),
            pltpu.VMEM((1, events), jnp.int32),
            pltpu.SemaphoreType.DMA((6,)),
        ],
    )
    along = {}
    for k in order:
        if k in (1, n - 1):
            along[k] = shift(own_share, "hist", k)
        else:
            step = 1 if k <= n // 2 else n - 1
            along[k] = shift(along[(k - step) % n], "hist", step)
    feats_other = shift(item_feats, "rep", 1)
    other = shift(mine, "rep", 1)
    keys = events + 2 * items
    hot, pick = call(users_kernel, (shape((USERS, keys), BF16), shape((cands, 2 * items), BF16)), (mine, other))
    key_t, value, block = call(
        project_kernel,
        (shape((width, events), BF16), shape((events, width), BF16), shape((depth, width), BF16)),
        (adapter, hist_emb, key_weight, value_weight),
        flops=4 * events * dim * width,
        bytes_accessed=4 << 20,
        specs=[HBM] * 4,
        scratch=[
            pltpu.VMEM((events, dim), BF16),
            pltpu.VMEM((dim, width), BF16),
            pltpu.VMEM((dim, width), BF16),
            pltpu.SemaphoreType.DMA((4,)),
        ],
    )
    total = call(
        embed_own_kernel,
        shape((2 * items, width), F32),
        (item_feats, feats_other, block),
        flops=4 * items * depth * width,
        bytes_accessed=4 << 20,
    )
    tally = call(tally_kernel, shape((16, USERS), F32), (own_share, *[along[k] for k in range(1, n)]))
    scale = call(
        functools.partial(scale_kernel, items),
        shape((n, cands, keys), F32),
        (mine, other, hot, tally, shift(tally, "rep", 1)),
        bytes_accessed=4 << 20,
    )
    across = {k: [along[k]] + [shift(along[k], "groups", g) for g in range(1, groups)] for k in order}
    near = [((k, 0), across[k][0]) for k in order]
    far = [((k, step), across[k][step]) for k in order for step in range(1, groups)]
    for chunk in (near, far[:1]):
        which, arrived = zip(*chunk)
        total = call(
            functools.partial(embed_add_kernel, n, groups, which),
            shape((2 * items, width), F32),
            (item_feats, feats_other, total, *arrived),
            flops=4 * items * depth * width,
            bytes_accessed=2 << 20,
        )
    which, arrived = zip(*far[1:])
    share = depth // groups
    part, feats = call(
        functools.partial(query_part_kernel, n, groups, which),
        (shape((cands, width), F32), shape((cands, share * len(which)), BF16)),
        (item_feats, feats_other, pick, total),
        flops=4 * cands * items * (share + 6 * width),
    )
    query = call(query_kernel, shape((cands, width), BF16), (part, feats, *arrived), flops=4 * cands * share * width)
    rows, rows_t = call(
        functools.partial(embed_last_kernel, n, groups, which),
        (shape((2 * items, width), BF16), shape((width, 2 * items), BF16)),
        (item_feats, feats_other, total, *arrived),
        flops=8 * items * share * width,
        bytes_accessed=2 << 20,
    )
    queries = {k: shift(query, "hist", k) for k in order}

    def attend(k, block, dtype):
        return call(
            functools.partial(attend_kernel, k),
            shape((cands, width), dtype),
            (block, key_t, value, rows_t, rows, scale),
            flops=8 * cands * keys * width,
            bytes_accessed=1 << 20,
        )

    own = attend(0, query, F32)
    parts = [shift(attend(k, queries[k], BF16), "hist", n - k) for k in order]
    keep, send = call(
        gate_kernel, (shape((cands // 2, width), BF16), shape((cands // 2, width), BF16)), (query, own, *parts)
    )
    got = shift(send, "rep", 1)
    return call(join_kernel, shape((cands // 2, cols), BF16), (keep, got))


def body(*args):
    item_feats, adapter, cand_index, hist_user = args[0], args[1], args[6], args[8]
    fits = (
        lax.axis_size("rep") == 2
        and 1 < lax.axis_size("hist") <= 4
        and item_feats.shape[0] + hist_user.shape[0] // 2 < 1024
        and hist_user.shape[0] % 256 == 0
        and adapter.shape[0] % (128 * lax.axis_size("groups")) == 0
        and adapter.shape[1] % 256 == 0
        and 2 * cand_index.shape[0] == 128
        and item_feats.shape[0] % 128 == 0
    )
    return fast_body(*args) if fits else generic_body(*args)


def solution(mesh):
    placed = (
        P(("groups", "hist", "rep"), None),
        P("hist", "head"),
        P(("groups", "hist"), None),
        P(None, "head"),
        P(None, "head"),
        P(("groups", "hist", "rep"), None),
        P(("groups", "hist", "rep")),
        P(("groups", "hist", "rep")),
        P(("groups", "hist")),
    )
    return jax.shard_map(
        body,
        mesh=mesh,
        in_specs=placed,
        out_specs=P(("groups", "hist", "rep"), "head"),
        check_vma=False,
    )
```
